32 devices in a mesh: dirs: 2 (over y), taps: 4 (over z), tm: 2 (over x), floors: 2 (over core).
Axes of the slice: x: 2, y: 2, z: 4, core: 2. Of those that a mesh axis runs over, the one named last changes fastest.
Arguments:
- pressures: bfloat16 [4096, 16384], P(('dirs', 'tm'), ('taps', 'floors')), parts along dimension 0, may hold values from -6 to 6
- tap_area: bfloat16 [16384], P(('taps', 'floors')), may hold values from 0.29882812 to 3
- tap_panel: int32 [16384], P(('taps', 'floors')), may hold values from 0 to 255
- tap_floor: int32 [16384], P(('taps', 'floors')), may hold values from 0 to 15
- panel_shape: bfloat16 [256, 512], replicated, may hold values from -0.046875 to 0.046875
- floor_shape: bfloat16 [16, 512], replicated, may hold values from -0.25 to 0.25
- mode_order: int32 [512], replicated, may hold values from 0 to 511, each once
- mode_decay: float32 [512], replicated, may hold values from 4.8828125e-05 to 0.08
- mode_freq: float32 [512], replicated, may hold values from 0.02 to 1.2
Outputs:
- modal_response: float32 [512, 4096], P(('taps', 'floors'), ('dirs', 'tm')), parts along dimension 1
- floor_motion: float32 [16, 4096], P(('taps', 'floors'), ('dirs', 'tm')), parts along dimension 1
- floor_load: float32 [16, 4096], P(('taps', 'floors'), ('dirs', 'tm')), parts along dimension 1
The draws below stay inside these ranges and needn't reach their ends.
There are 2 independent parts, one for each index of `dirs`. The reference program is written for one: setup_inputs(seed, part) draws one part's arguments, and reference() takes and returns one part's arrays. A program takes and returns all parts, laid end to end along the dimension named above; an argument that names none is the same for every part. Nothing has to cross between parts.
All inputs are finite; a program needn't handle non-finite values.
Results may differ from the reference program's by a relative error of at most 0.0029.
Values sent between devices are 32-bit elements; how exact they have to be, the bound alone decides.
A program may use at most 64 MiB of HBM per device.

```python
import math
import jax
import jax.numpy as jnp
from jax import lax

M = 512
PANELS = 256
TAP_DEV = 2048
TIME = 2048
TAPS = 16384
FLOORS = 16


def draw_mode_decay(key, part):
    key_pick = jax.random.fold_in(key, 11)
    key_slow = jax.random.fold_in(key, 12)
    key_fast = jax.random.fold_in(key, 13)
    slow_share = 0.5
    slow_pick = jax.random.uniform(key_pick, (M,), jnp.float32) < slow_share
    slow_rates = 0.1 / TIME * jnp.exp(jax.random.uniform(key_slow, (M,), jnp.float32, 0.0, math.log(10.0)))
    fast_rates = jnp.exp(jax.random.uniform(key_fast, (M,), jnp.float32, math.log(0.02), math.log(0.08)))
    return jnp.where(slow_pick, slow_rates, fast_rates).astype(jnp.float32)


def touch_ends(values, own_key, least, largest):
    extent = values.shape
    index_at = [jax.random.randint(jax.random.fold_in(own_key, axis), (), 0, extent[axis]) for axis in range(len(extent))]
    values = values.at[tuple(index_at)].set(least)
    longest = extent.index(max(extent))
    index_at[longest] = (index_at[longest] + 1) % extent[longest]
    return values.at[tuple(index_at)].set(largest)


def block_levels(stream_key, shape, cuts, least, largest):
    level, own = 1.0, jax.random.fold_in(stream_key, 6)
    for position, blocks in cuts:
        heights = jnp.exp(jax.random.uniform(jax.random.fold_in(own, position), (blocks,), jnp.float32, least / len(cuts), largest / len(cuts)))
        level = level * jnp.repeat(heights, shape[position] // blocks).reshape([-1 if axis == position else 1 for axis in range(len(shape))])
    return level


def noise(own_key, extent, spread, limit, shards=(), held_as=jnp.bfloat16):
    result = spread * jax.random.normal(own_key, extent, jnp.float32)
    if shards:
        result = result * block_levels(own_key, extent, shards, -0.22, 0.18)
    return jnp.clip(result, -limit, limit).astype(held_as)


def setup_inputs(seed: int = 0, part: int = 0) -> dict:
    streams_of = jax.random.split(jax.random.key(seed), 10)
    own_keys = jax.random.split(jax.random.fold_in(streams_of[9], part), 10)
    pressures = noise(own_keys[0], (TIME, TAPS), 1.0, 6.0, ((0, 2), (1, 8)))
    tap_area = jnp.clip(jnp.exp(math.log(3.0) - 2.306499 * jax.random.uniform(streams_of[1], (TAPS,), jnp.float32) ** block_levels(streams_of[1], (TAPS,), ((0, 8),), -0.2, 0.2)), 0.29882812, 3.0).astype(jnp.bfloat16)
    tap_panel = touch_ends(jax.random.randint(streams_of[2], (TAPS,), 0, PANELS), jax.random.fold_in(streams_of[2], 1), 0, PANELS - 1).astype(jnp.int32)
    tap_floor = touch_ends(jax.random.randint(streams_of[3], (TAPS,), 0, FLOORS), jax.random.fold_in(streams_of[3], 1), 0, FLOORS - 1).astype(jnp.int32)
    panel_shape = noise(streams_of[4], (PANELS, M), TAPS ** -0.5, 0.046875)
    floor_shape = noise(streams_of[5], (FLOORS, M), M ** -0.5, 0.25)
    mode_order = jax.random.permutation(streams_of[6], M).astype(jnp.int32)
    mode_decay = draw_mode_decay(jax.random.fold_in(streams_of[9], 71), part)
    mode_freq = jnp.clip(jnp.exp(jax.random.uniform(streams_of[8], (M,), jnp.float32, math.log(0.02), math.log(1.2))), 0.02, 1.2)
    return {"pressures": pressures, "tap_area": tap_area, "tap_panel": tap_panel, "tap_floor": tap_floor, "panel_shape": panel_shape, "floor_shape": floor_shape, "mode_order": mode_order, "mode_decay": mode_decay, "mode_freq": mode_freq}


def reference(pressures, tap_area, tap_panel, tap_floor, panel_shape, floor_shape, mode_order, mode_decay, mode_freq):
    ordered = jnp.take(panel_shape, mode_order, axis=1)
    floor_ids = jnp.arange(FLOORS, dtype=jnp.int32)
    block_count = TAPS // TAP_DEV

    def accumulate(carried, block_idx):
        start = (block_idx * TAP_DEV).astype(jnp.int32)
        window = lax.dynamic_slice_in_dim(pressures, start, TAP_DEV, 1)
        area_block = lax.dynamic_slice_in_dim(tap_area, start, TAP_DEV, 0)
        panel_block = lax.dynamic_slice_in_dim(tap_panel, start, TAP_DEV, 0)
        floor_block = lax.dynamic_slice_in_dim(tap_floor, start, TAP_DEV, 0)
        tributary = (jnp.take(ordered, panel_block, axis=0).astype(jnp.float32) * area_block.astype(jnp.float32)[:, None]).astype(jnp.bfloat16)
        forces = carried[0] + lax.dot_general(tributary, window, (((0,), (1,)), ((), ())), preferred_element_type=jnp.float32)
        weights = jnp.where(floor_block[None, :] == floor_ids[:, None], area_block[None, :], jnp.zeros((), jnp.bfloat16))
        loads = carried[1] + lax.dot_general(weights, window, (((1,), (1,)), ((), ())), preferred_element_type=jnp.float32)
        return ((forces, loads), None)
    start_sums = (jnp.zeros((M, TIME), jnp.float32), jnp.zeros((FLOORS, TIME), jnp.float32))
    (forces, loads), _ = lax.scan(accumulate, start_sums, jnp.arange(block_count, dtype=jnp.int32))
    decays = jnp.take(mode_decay, mode_order)
    angles = jnp.take(mode_freq, mode_order)
    input_gain = jnp.sqrt(-jnp.expm1(-2.0 * decays))
    turn_re = jnp.exp(-decays) * jnp.cos(angles)
    turn_im = jnp.exp(-decays) * jnp.sin(angles)

    def advance(carried, force_now):
        real_part, imag_part = carried
        next_real = turn_re * real_part - turn_im * imag_part + input_gain * force_now
        next_imag = turn_im * real_part + turn_re * imag_part
        return ((next_real, next_imag), next_real)
    zeros_state = jnp.zeros((M,), jnp.float32)
    _, history = lax.scan(advance, (zeros_state, zeros_state), forces.T)
    motion = history.T
    local_shape = jnp.take(floor_shape, mode_order, axis=1).astype(jnp.float32)
    floor_motion = jnp.dot(local_shape, motion, precision=lax.Precision.HIGHEST, preferred_element_type=jnp.float32)
    floor_load = loads * (FLOORS / TAPS) ** 0.5
    return (motion, floor_motion, floor_load)
```

```python
import functools

import jax
import jax.numpy as jnp
from jax import lax
from jax.experimental import pallas as pl
from jax.experimental.pallas import tpu as pltpu
from jax.sharding import PartitionSpec as P

MESH = pl.DeviceIdType.MESH
LANES = 128
LAG = 2
VMEM_LIMIT = 32 * 1024 * 1024
NT = (((1,), (1,)), ((), ()))


def dot_nt(a, b):
    return lax.dot_general(a, b, NT, preferred_element_type=jnp.float32)


def dot_split(a, b):
    hi = b.astype(jnp.bfloat16)
    lo = (b - hi.astype(jnp.float32)).astype(jnp.bfloat16)
    return jnp.dot(a, hi, preferred_element_type=jnp.float32) + jnp.dot(
        a, lo, preferred_element_type=jnp.float32
    )


def kernel(
    cfg,
    p_hbm, area_h, panel_h, floor_h, shape_h, fshape_h, order_h, decay_h, freq_h,
    y_ref, fm_ref, fl_ref,
    area_ref, panel_ref, floor_ref, shape_ref, fshape_ref, order_ref, decay_ref, freq_ref, order_col,
    pv, w_ref, mine, send_p, recv_p, rin, lin, rout, lout, xs, fb, tabs, loc, loc_im, st_send, st_recv,
    fs, fr,
    in_sem, p_sem, pp_s, pp_r, r_s, r_r, l_s, l_r, x_s, x_r, t_s, t_r, f_s, f_r,
):
    nz, nc, ntm, splits = cfg
    owners = nz * nc
    z = lax.axis_index("taps")
    c = lax.axis_index("floors")
    x = lax.axis_index("tm")
    me = z * nc + c
    other = nc - 1 - c
    time_dev, taps = pv.shape
    panels, modes = shape_ref.shape
    floors = fshape_ref.shape[0]
    rows = panels + floors
    th = time_dev // nc
    tblocks = th // LANES
    crows = rows // splits
    nch = tblocks * splits
    md = modes // owners
    fd = floors // owners
    f32 = jnp.float32
    bf16 = jnp.bfloat16

    small = [
        pltpu.make_async_copy(src, dst, in_sem.at[i])
        for i, (src, dst) in enumerate(
            (
                (area_h, area_ref), (panel_h, panel_ref), (floor_h, floor_ref), (shape_h, shape_ref),
                (fshape_h, fshape_ref), (order_h, order_ref), (decay_h, decay_ref), (freq_h, freq_ref),
            )
        )
    ]
    for cp in small:
        cp.start()

    barrier = pltpu.get_barrier_semaphore()

    def greet(k, carry):
        j = lax.rem(me + k, owners)
        pl.semaphore_signal(
            barrier, inc=1, device_id={"taps": j // nc, "floors": lax.rem(j, nc)}, device_id_type=MESH
        )
        return carry

    lax.fori_loop(1, owners, greet, 0)
    for k in range(1, ntm):
        pl.semaphore_signal(
            barrier, inc=1, device_id={"tm": lax.rem(x + k, ntm)}, device_id_type=MESH
        )

    step_t = min(256, th)
    per_half = th // step_t
    loads = []
    for h in range(2):
        half = other if h == 0 else c
        for b in range(per_half):
            off = pl.multiple_of(half * th + b * step_t, step_t)
            cp = pltpu.make_async_copy(
                p_hbm.at[pl.ds(off, step_t)], pv.at[pl.ds(off, step_t)], p_sem.at[h * per_half + b]
            )
            cp.start()
            loads.append((cp, off))

    for cp in small[:3]:
        cp.wait()
    ids = lax.broadcasted_iota(jnp.int32, (panels, LANES), 0)
    fids = lax.broadcasted_iota(jnp.int32, (floors, LANES), 0)
    area = area_ref[...].astype(f32)
    for r in range(taps // LANES):
        cols = slice(r * LANES, (r + 1) * LANES)
        row = area[r : r + 1, :]
        w_ref[0:panels, cols] = jnp.where(panel_ref[:, cols] == ids, row, 0.0).astype(bf16)
        w_ref[panels:rows, cols] = jnp.where(floor_ref[:, cols] == fids, row, 0.0).astype(bf16)

    def sums(b, h, dst):
        cp, off = loads[h * per_half + b]
        cp.wait()
        q = dot_nt(w_ref[...], pv[pl.ds(off, step_t), :])
        for i in range(step_t // LANES):
            for s in range(splits):
                dst[(b * step_t // LANES + i) * splits + s] = q[
                    s * crows : (s + 1) * crows, i * LANES : (i + 1) * LANES
                ]

    def pair_copy(k):
        return pltpu.make_async_remote_copy(
            src_ref=send_p.at[k], dst_ref=recv_p.at[k], send_sem=pp_s.at[k], recv_sem=pp_r.at[k],
            device_id={"floors": other}, device_id_type=MESH,
        )

    per_step = step_t // LANES * splits

    @pl.when(z == 0)
    def _():
        rin[...] = jnp.zeros_like(rin)

    @pl.when(z == nz - 1)
    def _():
        lin[...] = jnp.zeros_like(lin)

    def line_copy(k, right):
        src, dst, ss, rs = (rout, rin, r_s, r_r) if right else (lout, lin, l_s, l_r)
        to = jnp.minimum(z + 1, nz - 1) if right else jnp.maximum(z - 1, 0)
        return pltpu.make_async_remote_copy(
            src_ref=src.at[k], dst_ref=dst.at[k], send_sem=ss.at[k], recv_sem=rs.at[k],
            device_id={"taps": to}, device_id_type=MESH,
        )

    def line_step(s, carry):
        for right in (True, False):
            hop = z if right else nz - 1 - z
            k = s - LAG * hop
            came, out = (rin, rout) if right else (lin, lout)

            @pl.when(jnp.logical_and(k >= 0, k < nch))
            def _():
                @pl.when(hop > 0)
                def _():
                    line_copy(k, right).wait_recv()

                @pl.when(hop < nz - 1)
                def _():
                    out[k] = mine[k] + came[k]
                    line_copy(k, right).start()

        return carry

    def merge(b):
        for k in range(b * per_step, (b + 1) * per_step):
            pair_copy(k).wait_recv()
            mine[k] = mine[k] + recv_p[k]

    for b in range(per_half):
        sums(b, 0, send_p)
        if b == 0:
            pl.semaphore_wait(barrier, owners - 1 + ntm - 1)
        for k in range(b * per_step, (b + 1) * per_step):
            pair_copy(k).start()
        if b > 0:
            merge(b - 1)
        if b == 1:
            lax.fori_loop(0, min(LAG, per_step), line_step, 0)
        sums(b, 1, mine)
    merge(per_half - 1)
    first = min(LAG, per_step) if per_half > 1 else 0
    early = min(LAG, nch)
    lax.fori_loop(first, early, line_step, 0)

    for cp in small[3:]:
        cp.wait()
    order_col[...] = jnp.transpose(jnp.broadcast_to(order_ref[...].astype(f32), (LANES, modes)))
    mode_ids = lax.broadcasted_iota(jnp.int32, (md, modes), 1).astype(f32)

    def pick(owner):
        return order_col[pl.ds(pl.multiple_of(owner * md, md), md), 0:1] == mode_ids

    def shapes(hot):
        return dot_nt(hot.astype(f32).astype(bf16), shape_ref[...]).astype(bf16)

    hot_me = pick(me)
    hot_other = pick(z * nc + other)
    g_both = jnp.concatenate([shapes(hot_other), shapes(hot_me)], axis=0)
    d = jnp.sum(jnp.where(hot_me, decay_ref[...], 0.0), axis=1, keepdims=True)
    w = jnp.sum(jnp.where(hot_me, freq_ref[...], 0.0), axis=1, keepdims=True)
    ls = dot_nt(fshape_ref[...], hot_me.astype(f32).astype(bf16)).astype(bf16)
    e2 = 2.0 * d
    poly = jnp.full_like(e2, 1.0 / 40320.0)
    for coef in (1.0 / 5040, 1.0 / 720, 1.0 / 120, 1.0 / 24, 1.0 / 6, 0.5, 1.0):
        poly = coef - e2 * poly
    gain = jnp.sqrt(e2 * poly)
    lane = lax.broadcasted_iota(jnp.int32, (md, LANES), 1)
    ahead = (lane + 1).astype(f32)
    mag = jnp.exp(-d * ahead)
    t_re = mag * jnp.cos(w * ahead)
    t_im = mag * jnp.sin(w * ahead)
    tabs[0] = t_re
    tabs[1] = t_im
    hops = []
    step = 1
    while step < LANES:
        i = 2 + 2 * len(hops)
        tabs[i] = jnp.where(lane >= step, t_re[:, step - 1 : step], 0.0)
        tabs[i + 1] = jnp.where(lane >= step, t_im[:, step - 1 : step], 0.0)
        hops.append(step)
        step *= 2

    floor_row = lax.broadcasted_iota(jnp.int32, (floors, LANES), 0)

    def load_row(q, row):
        return jnp.sum(jnp.where(floor_row == row, q, 0.0), axis=0, keepdims=True)

    def exchange(tb):
        return pltpu.make_async_remote_copy(
            src_ref=xs.at[tb], dst_ref=fb.at[c * tblocks + tb],
            send_sem=x_s.at[tb], recv_sem=x_r.at[tb],
            device_id={"floors": other}, device_id_type=MESH,
        )

    def forces(tb):
        q = jnp.concatenate(
            [mine[k] + rin[k] + lin[k] for k in range(tb * splits, (tb + 1) * splits)], axis=0
        )
        both = dot_split(g_both, q[:panels])
        blk = c * tblocks + tb
        pad = [jnp.zeros((xs.shape[1] - md - fd, LANES), f32)] if xs.shape[1] > md + fd else []
        theirs = [load_row(q[panels:], (z * nc + other) * fd + r) for r in range(fd)]
        ours = [load_row(q[panels:], me * fd + r) for r in range(fd)]
        xs[tb] = jnp.concatenate([both[:md]] + theirs + pad, axis=0)
        exchange(tb).start()
        fb[blk] = jnp.concatenate([both[md:]] + ours + pad, axis=0)

    def at_rest(blk):
        re = gain * fb[blk, 0:md, :]
        im = None
        for i, step in enumerate(hops):
            a, b = tabs[2 + 2 * i], tabs[3 + 2 * i]
            rr = pltpu.roll(re, step, 1)
            if im is None:
                re, im = re + a * rr, b * rr
            else:
                ri = pltpu.roll(im, step, 1)
                re, im = re + a * rr - b * ri, im + a * ri + b * rr
        loc[blk] = re
        loc_im[blk] = im

    done = early
    for tb in range(tblocks):
        upto = (tb + 1) * splits + LAG * (nz - 1)
        lax.fori_loop(done, upto, line_step, 0)
        done = upto
        forces(tb)
        at_rest(c * tblocks + tb)
        if tb > 0:
            exchange(tb - 1).wait_recv()
            at_rest(other * tblocks + tb - 1)
    exchange(tblocks - 1).wait_recv()
    at_rest(other * tblocks + tblocks - 1)
    nb = time_dev // LANES
    end_re = [loc[blk][:, LANES - 1 :] for blk in range(nb)]
    end_im = [loc_im[blk][:, LANES - 1 :] for blk in range(nb)]

    zb_re, zb_im = t_re[:, LANES - 1 :], t_im[:, LANES - 1 :]
    s_re, s_im = end_re[0], end_im[0]
    for blk in range(1, nb):
        s_re, s_im = (
            zb_re * s_re - zb_im * s_im + end_re[blk],
            zb_im * s_re + zb_re * s_im + end_im[blk],
        )

    def state_copy(to, src):
        return pltpu.make_async_remote_copy(
            src_ref=st_send, dst_ref=st_recv.at[src], send_sem=t_s.at[to], recv_sem=t_r.at[src],
            device_id={"tm": to}, device_id_type=MESH,
        )

    st_send[...] = jnp.where(lane == 0, s_re, s_im)
    in_re = jnp.zeros((md, 1), f32)
    in_im = jnp.zeros((md, 1), f32)
    if ntm > 1:
        for to in range(1, ntm):

            @pl.when(x < to)
            def _():
                state_copy(to, jnp.minimum(x, ntm - 2)).start()

        for src in range(ntm - 1):

            @pl.when(x > src)
            def _():
                state_copy(lax.rem(x + 1, ntm), src).wait_recv()

            @pl.when(x <= src)
            def _():
                st_recv[src] = jnp.zeros_like(st_send)

            got_re, got_im = st_recv[src][:, 0:1], st_recv[src][:, 1:2]
            if ntm == 2:
                in_re, in_im = got_re, got_im
                continue
            length = (jnp.maximum(x - 1 - src, 0) * time_dev).astype(f32)
            pm = jnp.exp(-d * length)
            pr, pi = pm * jnp.cos(w * length), pm * jnp.sin(w * length)
            in_re = in_re + pr * got_re - pi * got_im
            in_im = in_im + pi * got_re + pr * got_im

    t_re, t_im = tabs[0], tabs[1]
    for blk in range(nb):
        y = loc[blk] + t_re * in_re - t_im * in_im
        cols = slice(blk * LANES, (blk + 1) * LANES)
        y_ref[:, cols] = y
        in_re, in_im = (
            zb_re * in_re - zb_im * in_im + end_re[blk],
            zb_im * in_re + zb_re * in_im + end_im[blk],
        )
    part = dot_split(ls, y_ref[...])
    for j in range(owners):
        fs[j] = part[j * fd : (j + 1) * fd]

    def motion_copy(k):
        j = lax.rem(me + k, owners)
        return pltpu.make_async_remote_copy(
            src_ref=fs.at[j], dst_ref=fr.at[me], send_sem=f_s.at[k], recv_sem=f_r.at[k],
            device_id={"taps": j // nc, "floors": lax.rem(j, nc)}, device_id_type=MESH,
        )

    def motion_start(k, carry):
        motion_copy(k).start()
        return carry

    def motion_recv(k, total):
        motion_copy(k).wait_recv()
        return total + fr[lax.rem(me + owners - k, owners)]

    def motion_sent(k, carry):
        motion_copy(k).wait_send()
        return carry

    lax.fori_loop(1, owners, motion_start, 0)
    load_scale = (floors / (taps * owners)) ** 0.5
    for blk in range(nb):
        fl_ref[:, blk * LANES : (blk + 1) * LANES] = fb[blk, md : md + fd, :] * load_scale

    for k in range(nch):
        pair_copy(k).wait_send()

    def line_sent(k, carry):
        @pl.when(z < nz - 1)
        def _():
            line_copy(k, True).wait_send()

        @pl.when(z > 0)
        def _():
            line_copy(k, False).wait_send()

        return carry

    lax.fori_loop(0, nch, line_sent, 0)
    for tb in range(tblocks):
        exchange(tb).wait_send()
    for to in range(1, ntm):

        @pl.when(x < to)
        def _():
            state_copy(to, jnp.minimum(x, ntm - 2)).wait_send()

    fm_ref[...] = lax.fori_loop(1, owners, motion_recv, fs[me])
    lax.fori_loop(1, owners, motion_sent, 0)


def write_out(y, fm, fl, y_out, fm_out, fl_out, sem):
    copies = [
        pltpu.make_async_copy(src, dst, sem.at[i])
        for i, (src, dst) in enumerate(((y, y_out), (fm, fm_out), (fl, fl_out)))
    ]
    for cp in copies:
        cp.start()
    for cp in copies:
        cp.wait()


def on_device(
    pressures, tap_area, tap_panel, tap_floor, panel_shape, floor_shape, mode_order, mode_decay, mode_freq
):
    nz, nc, ntm = lax.axis_size("taps"), lax.axis_size("floors"), lax.axis_size("tm")
    owners = nz * nc
    time_dev, taps = pressures.shape
    panels, modes = panel_shape.shape
    floors = floor_shape.shape[0]
    rows = panels + floors
    splits = 2
    th = time_dev // nc
    md, fd = modes // owners, floors // owners
    nch = th // LANES * splits
    xrows = md + -(-fd // 8) * 8
    chunk = pltpu.VMEM((nch, rows // splits, LANES), jnp.float32)
    vmem = pl.BlockSpec(memory_space=pltpu.VMEM)
    dma = pltpu.SemaphoreType.DMA
    f32 = jnp.float32
    out = pl.pallas_call(
        functools.partial(kernel, (nz, nc, ntm, splits)),
        out_shape=(
            pltpu.VMEM((md, time_dev), f32),
            pltpu.VMEM((fd, time_dev), f32),
            pltpu.VMEM((fd, time_dev), f32),
        ),
        in_specs=[pl.BlockSpec(memory_space=pltpu.HBM)] * 9,
        out_specs=(vmem,) * 3,
        scratch_shapes=[
            pltpu.VMEM((taps // LANES, LANES), jnp.bfloat16),
            pltpu.VMEM((1, taps), jnp.int32),
            pltpu.VMEM((1, taps), jnp.int32),
            pltpu.VMEM(panel_shape.shape, jnp.bfloat16),
            pltpu.VMEM(floor_shape.shape, jnp.bfloat16),
            pltpu.VMEM((1, modes), jnp.int32),
            pltpu.VMEM((1, modes), f32),
            pltpu.VMEM((1, modes), f32),
            pltpu.VMEM((modes, LANES), f32),
            pltpu.VMEM((time_dev, taps), jnp.bfloat16),
            pltpu.VMEM((rows, taps), jnp.bfloat16),
            chunk, chunk, chunk, chunk, chunk, chunk, chunk,
            pltpu.VMEM((th // LANES, xrows, LANES), f32),
            pltpu.VMEM((time_dev // LANES, xrows, LANES), f32),
            pltpu.VMEM((16, md, LANES), f32),
            pltpu.VMEM((time_dev // LANES, md, LANES), f32),
            pltpu.VMEM((time_dev // LANES, md, LANES), f32),
            pltpu.VMEM((md, LANES), f32),
            pltpu.VMEM((max(ntm - 1, 1), md, LANES), f32),
            pltpu.VMEM((owners, fd, time_dev), f32),
            pltpu.VMEM((owners, fd, time_dev), f32),
            dma((8,)),
            dma((2 * (th // min(256, th)),)),
            dma((nch,)), dma((nch,)), dma((nch,)), dma((nch,)), dma((nch,)), dma((nch,)),
            dma((th // LANES,)), dma((th // LANES,)),
            dma((ntm,)), dma((ntm,)),
            dma((owners,)), dma((owners,)),
        ],
        compiler_params=pltpu.CompilerParams(
            collective_id=0, has_side_effects=True, vmem_limit_bytes=VMEM_LIMIT
        ),
    )(
        *(
            pltpu.with_memory_space_constraint(a, pltpu.HBM)
            for a in (
                pressures,
                tap_area.reshape(taps // LANES, LANES),
                tap_panel.reshape(1, taps),
                tap_floor.reshape(1, taps),
                panel_shape,
                floor_shape,
                mode_order.reshape(1, modes),
                mode_decay.reshape(1, modes),
                mode_freq.reshape(1, modes),
            )
        )
    )
    return pl.pallas_call(
        write_out,
        out_shape=tuple(jax.ShapeDtypeStruct(o.shape, o.dtype) for o in out),
        in_specs=[vmem] * 3,
        out_specs=(pl.BlockSpec(memory_space=pltpu.HBM),) * 3,
        scratch_shapes=[dma((3,))],
        compiler_params=pltpu.CompilerParams(vmem_limit_bytes=VMEM_LIMIT),
    )(*out)


def solution(mesh):
    own = P(("taps", "floors"))
    out_spec = P(("taps", "floors"), ("dirs", "tm"))
    return jax.shard_map(
        on_device,
        mesh=mesh,
        in_specs=(P(("dirs", "tm"), ("taps", "floors")), own, own, own, P(), P(), P(), P(), P()),
        out_specs=(out_spec, out_spec, out_spec),
        check_vma=False,
    )
```

```python
import functools

import jax
import jax.numpy as jnp
from jax import lax
from jax.experimental import pallas as pl
from jax.experimental.pallas import tpu as pltpu
from jax.sharding import PartitionSpec as P

MESH = pl.DeviceIdType.MESH
LANES = 128
LAG = 2
VMEM_LIMIT = 32 * 1024 * 1024
NT = (((1,), (1,)), ((), ()))


def dot_nt(a, b):
    return lax.dot_general(a, b, NT, preferred_element_type=jnp.float32)


def dot_split(a, b):
    hi = b.astype(jnp.bfloat16)
    lo = (b - hi.astype(jnp.float32)).astype(jnp.bfloat16)
    return jnp.dot(a, hi, preferred_element_type=jnp.float32) + jnp.dot(
        a, lo, preferred_element_type=jnp.float32
    )


def kernel(
    cfg,
    p_hbm, area_h, panel_h, floor_h, shape_h, fshape_h, order_h, decay_h, freq_h,
    y_ref, fm_ref, fl_ref,
    area_ref, panel_ref, floor_ref, shape_ref, fshape_ref, order_ref, decay_ref, freq_ref, order_col,
    pv, w_ref, mine, send_p, recv_p, rin, lin, rout, lout, xs, fb, tabs, loc, loc_im, st_send, st_recv,
    fs, fr,
    in_sem, p_sem, pp_s, pp_r, r_s, r_r, l_s, l_r, x_s, x_r, t_s, t_r, f_s, f_r,
):
    nz, nc, ntm, splits = cfg
    owners = nz * nc
    z = lax.axis_index("taps")
    c = lax.axis_index("floors")
    x = lax.axis_index("tm")
    me = z * nc + c
    other = nc - 1 - c
    time_dev, taps = pv.shape
    panels, modes = shape_ref.shape
    floors = fshape_ref.shape[0]
    rows = panels + floors
    th = time_dev // nc
    tblocks = th // LANES
    crows = rows // splits
    nch = tblocks * splits
    md = modes // owners
    fd = floors // owners
    f32 = jnp.float32
    bf16 = jnp.bfloat16

    small = [
        pltpu.make_async_copy(src, dst, in_sem.at[i])
        for i, (src, dst) in enumerate(
            (
                (area_h, area_ref), (panel_h, panel_ref), (floor_h, floor_ref), (shape_h, shape_ref),
                (fshape_h, fshape_ref), (order_h, order_ref), (decay_h, decay_ref), (freq_h, freq_ref),
            )
        )
    ]
    for cp in small:
        cp.start()

    barrier = pltpu.get_barrier_semaphore()

    def greet(k, carry):
        j = lax.rem(me + k, owners)
        pl.semaphore_signal(
            barrier, inc=1, device_id={"taps": j // nc, "floors": lax.rem(j, nc)}, device_id_type=MESH
        )
        return carry

    lax.fori_loop(1, owners, greet, 0)
    for k in range(1, ntm):
        pl.semaphore_signal(
            barrier, inc=1, device_id={"tm": lax.rem(x + k, ntm)}, device_id_type=MESH
        )

    step_t = min(256, th)
    per_half = th // step_t
    loads = []
    for h in range(2):
        half = other if h == 0 else c
        for b in range(per_half):
            off = pl.multiple_of(half * th + b * step_t, step_t)
            cp = pltpu.make_async_copy(
                p_hbm.at[pl.ds(off, step_t)], pv.at[pl.ds(off, step_t)], p_sem.at[h * per_half + b]
            )
            cp.start()
            loads.append((cp, off))

    for cp in small[:3]:
        cp.wait()
    ids = lax.broadcasted_iota(jnp.int32, (panels, LANES), 0)
    fids = lax.broadcasted_iota(jnp.int32, (floors, LANES), 0)
    area = area_ref[...].astype(f32)
    for r in range(taps // LANES):
        cols = slice(r * LANES, (r + 1) * LANES)
        row = area[r : r + 1, :]
        w_ref[0:panels, cols] = jnp.where(panel_ref[:, cols] == ids, row, 0.0).astype(bf16)
        w_ref[panels:rows, cols] = jnp.where(floor_ref[:, cols] == fids, row, 0.0).astype(bf16)

    def sums(b, h, dst):
        cp, off = loads[h * per_half + b]
        cp.wait()
        q = dot_nt(w_ref[...], pv[pl.ds(off, step_t), :])
        for i in range(step_t // LANES):
            for s in range(splits):
                dst[(b * step_t // LANES + i) * splits + s] = q[
                    s * crows : (s + 1) * crows, i * LANES : (i + 1) * LANES
                ]

    def pair_copy(k):
        return pltpu.make_async_remote_copy(
            src_ref=send_p.at[k], dst_ref=recv_p.at[k], send_sem=pp_s.at[k], recv_sem=pp_r.at[k],
            device_id={"floors": other}, device_id_type=MESH,
        )

    per_step = step_t // LANES * splits

    @pl.when(z == 0)
    def _():
        rin[...] = jnp.zeros_like(rin)

    @pl.when(z == nz - 1)
    def _():
        lin[...] = jnp.zeros_like(lin)

    def line_copy(k, right):
        src, dst, ss, rs = (rout, rin, r_s, r_r) if right else (lout, lin, l_s, l_r)
        to = jnp.minimum(z + 1, nz - 1) if right else jnp.maximum(z - 1, 0)
        return pltpu.make_async_remote_copy(
            src_ref=src.at[k], dst_ref=dst.at[k], send_sem=ss.at[k], recv_sem=rs.at[k],
            device_id={"taps": to}, device_id_type=MESH,
        )

    def line_step(s, carry):
        for right in (True, False):
            hop = z if right else nz - 1 - z
            k = s - LAG * hop
            came, out = (rin, rout) if right else (lin, lout)

            @pl.when(jnp.logical_and(k >= 0, k < nch))
            def _():
                @pl.when(hop > 0)
                def _():
                    line_copy(k, right).wait_recv()

                @pl.when(hop < nz - 1)
                def _():
                    out[k] = mine[k] + came[k]
                    line_copy(k, right).start()

        return carry

    def merge(b):
        for k in range(b * per_step, (b + 1) * per_step):
            pair_copy(k).wait_recv()
            mine[k] = mine[k] + recv_p[k]

    for b in range(per_half):
        sums(b, 0, send_p)
        if b == 0:
            pl.semaphore_wait(barrier, owners - 1 + ntm - 1)
        for k in range(b * per_step, (b + 1) * per_step):
            pair_copy(k).start()
        if b > 0:
            merge(b - 1)
        if b == 1:
            lax.fori_loop(0, min(LAG, per_step), line_step, 0)
        sums(b, 1, mine)
    merge(per_half - 1)
    first = min(LAG, per_step) if per_half > 1 else 0
    early = min(LAG, nch)
    lax.fori_loop(first, early, line_step, 0)

    for cp in small[3:]:
        cp.wait()
    order_col[...] = jnp.transpose(jnp.broadcast_to(order_ref[...].astype(f32), (LANES, modes)))
    mode_ids = lax.broadcasted_iota(jnp.int32, (md, modes), 1).astype(f32)

    def pick(owner):
        return order_col[pl.ds(pl.multiple_of(owner * md, md), md), 0:1] == mode_ids

    def shapes(hot):
        return dot_nt(hot.astype(f32).astype(bf16), shape_ref[...]).astype(bf16)

    hot_me = pick(me)
    hot_other = pick(z * nc + other)
    g_both = jnp.concatenate([shapes(hot_other), shapes(hot_me)], axis=0)
    d = jnp.sum(jnp.where(hot_me, decay_ref[...], 0.0), axis=1, keepdims=True)
    w = jnp.sum(jnp.where(hot_me, freq_ref[...], 0.0), axis=1, keepdims=True)
    ls = dot_nt(fshape_ref[...], hot_me.astype(f32).astype(bf16)).astype(bf16)
    e2 = 2.0 * d
    poly = jnp.full_like(e2, 1.0 / 40320.0)
    for coef in (1.0 / 5040, 1.0 / 720, 1.0 / 120, 1.0 / 24, 1.0 / 6, 0.5, 1.0):
        poly = coef - e2 * poly
    gain = jnp.sqrt(e2 * poly)
    lane = lax.broadcasted_iota(jnp.int32, (md, LANES), 1)
    ahead = (lane + 1).astype(f32)
    mag = jnp.exp(-d * ahead)
    t_re = mag * jnp.cos(w * ahead)
    t_im = mag * jnp.sin(w * ahead)
    tabs[0] = t_re
    tabs[1] = t_im
    hops = []
    step = 1
    while step < LANES:
        i = 2 + 2 * len(hops)
        tabs[i] = jnp.where(lane >= step, t_re[:, step - 1 : step], 0.0)
        tabs[i + 1] = jnp.where(lane >= step, t_im[:, step - 1 : step], 0.0)
        hops.append(step)
        step *= 2

    floor_row = lax.broadcasted_iota(jnp.int32, (floors, LANES), 0)

    def load_row(q, row):
        return jnp.sum(jnp.where(floor_row == row, q, 0.0), axis=0, keepdims=True)

    def exchange(tb):
        return pltpu.make_async_remote_copy(
            src_ref=xs.at[tb], dst_ref=fb.at[c * tblocks + tb],
            send_sem=x_s.at[tb], recv_sem=x_r.at[tb],
            device_id={"floors": other}, device_id_type=MESH,
        )

    def forces(tb):
        q = jnp.concatenate(
            [mine[k] + rin[k] + lin[k] for k in range(tb * splits, (tb + 1) * splits)], axis=0
        )
        both = dot_split(g_both, q[:panels])
        blk = c * tblocks + tb
        pad = [jnp.zeros((xs.shape[1] - md - fd, LANES), f32)] if xs.shape[1] > md + fd else []
        theirs = [load_row(q[panels:], (z * nc + other) * fd + r) for r in range(fd)]
        ours = [load_row(q[panels:], me * fd + r) for r in range(fd)]
        xs[tb] = jnp.concatenate([both[:md]] + theirs + pad, axis=0)
        exchange(tb).start()
        fb[blk] = jnp.concatenate([both[md:]] + ours + pad, axis=0)

    def at_rest(blk):
        re = gain * fb[blk, 0:md, :]
        im = None
        for i, step in enumerate(hops):
            a, b = tabs[2 + 2 * i], tabs[3 + 2 * i]
            rr = pltpu.roll(re, step, 1)
            if im is None:
                re, im = re + a * rr, b * rr
            else:
                ri = pltpu.roll(im, step, 1)
                re, im = re + a * rr - b * ri, im + a * ri + b * rr
        loc[blk] = re
        loc_im[blk] = im

    done = early
    for tb in range(tblocks):
        upto = (tb + 1) * splits + LAG * (nz - 1)
        lax.fori_loop(done, upto, line_step, 0)
        done = upto
        forces(tb)
        at_rest(c * tblocks + tb)
        if tb > 0:
            exchange(tb - 1).wait_recv()
            at_rest(other * tblocks + tb - 1)
    exchange(tblocks - 1).wait_recv()
    at_rest(other * tblocks + tblocks - 1)
    nb = time_dev // LANES
    end_re = [loc[blk][:, LANES - 1 :] for blk in range(nb)]
    end_im = [loc_im[blk][:, LANES - 1 :] for blk in range(nb)]

    zb_re, zb_im = t_re[:, LANES - 1 :], t_im[:, LANES - 1 :]
    s_re, s_im = end_re[0], end_im[0]
    for blk in range(1, nb):
        s_re, s_im = (
            zb_re * s_re - zb_im * s_im + end_re[blk],
            zb_im * s_re + zb_re * s_im + end_im[blk],
        )

    def state_copy(to, src):
        return pltpu.make_async_remote_copy(
            src_ref=st_send, dst_ref=st_recv.at[src], send_sem=t_s.at[to], recv_sem=t_r.at[src],
            device_id={"tm": to}, device_id_type=MESH,
        )

    st_send[...] = jnp.where(lane == 0, s_re, s_im)
    in_re = jnp.zeros((md, 1), f32)
    in_im = jnp.zeros((md, 1), f32)
    if ntm > 1:
        for to in range(1, ntm):

            @pl.when(x < to)
            def _():
                state_copy(to, jnp.minimum(x, ntm - 2)).start()

        for src in range(ntm - 1):

            @pl.when(x > src)
            def _():
                state_copy(lax.rem(x + 1, ntm), src).wait_recv()

            @pl.when(x <= src)
            def _():
                st_recv[src] = jnp.zeros_like(st_send)

            got_re, got_im = st_recv[src][:, 0:1], st_recv[src][:, 1:2]
            if ntm == 2:
                in_re, in_im = got_re, got_im
                continue
            length = (jnp.maximum(x - 1 - src, 0) * time_dev).astype(f32)
            pm = jnp.exp(-d * length)
            pr, pi = pm * jnp.cos(w * length), pm * jnp.sin(w * length)
            in_re = in_re + pr * got_re - pi * got_im
            in_im = in_im + pi * got_re + pr * got_im

    t_re, t_im = tabs[0], tabs[1]
    for blk in range(nb):
        y = loc[blk] + t_re * in_re - t_im * in_im
        cols = slice(blk * LANES, (blk + 1) * LANES)
        y_ref[:, cols] = y
        in_re, in_im = (
            zb_re * in_re - zb_im * in_im + end_re[blk],
            zb_im * in_re + zb_re * in_im + end_im[blk],
        )
    part = dot_split(ls, y_ref[...])
    for j in range(owners):
        fs[j] = part[j * fd : (j + 1) * fd]

    def motion_copy(k):
        j = lax.rem(me + k, owners)
        return pltpu.make_async_remote_copy(
            src_ref=fs.at[j], dst_ref=fr.at[me], send_sem=f_s.at[k], recv_sem=f_r.at[k],
            device_id={"taps": j // nc, "floors": lax.rem(j, nc)}, device_id_type=MESH,
        )

    def motion_start(k, carry):
        motion_copy(k).start()
        return carry

    def motion_recv(k, total):
        motion_copy(k).wait_recv()
        return total + fr[lax.rem(me + owners - k, owners)]

    def motion_sent(k, carry):
        motion_copy(k).wait_send()
        return carry

    lax.fori_loop(1, owners, motion_start, 0)
    load_scale = (floors / (taps * owners)) ** 0.5
    for blk in range(nb):
        fl_ref[:, blk * LANES : (blk + 1) * LANES] = fb[blk, md : md + fd, :] * load_scale

    for k in range(nch):
        pair_copy(k).wait_send()

    def line_sent(k, carry):
        @pl.when(z < nz - 1)
        def _():
            line_copy(k, True).wait_send()

        @pl.when(z > 0)
        def _():
            line_copy(k, False).wait_send()

        return carry

    lax.fori_loop(0, nch, line_sent, 0)
    for tb in range(tblocks):
        exchange(tb).wait_send()
    for to in range(1, ntm):

        @pl.when(x < to)
        def _():
            state_copy(to, jnp.minimum(x, ntm - 2)).wait_send()

    fm_ref[...] = lax.fori_loop(1, owners, motion_recv, fs[me])
    lax.fori_loop(1, owners, motion_sent, 0)


def two_stage(
    cfg,
    p_hbm, area_h, panel_h, floor_h, shape_h, fshape_h, order_h, decay_h, freq_h,
    y_ref, fm_ref, fl_ref,
    area_ref, panel_ref, floor_ref, shape_ref, fshape_ref, order_ref, decay_ref, freq_ref, order_col,
    pv, w_ref, g_ref, send_p, recv_p, mine, up, sx, fx, si, fi, sp, fb, tabs, loc, loc_im, st_send, st_recv,
    fls, flr, fs, fr,
    in_sem, p_sem, pp_s, pp_r, u_s, u_r, x_s, x_r, i_s, i_r, e_s, e_r, fl_s, fl_r, t_s, t_r, f_s, f_r, known,
):
    nz, nc, ntm, pieces = cfg
    owners = nz * nc
    z = lax.axis_index("taps")
    c = lax.axis_index("floors")
    x = lax.axis_index("tm")
    me = z * nc + c
    other = nc - 1 - c
    side = z // 2
    mate = z + 1 - 2 * lax.rem(z, 2)
    far = nz - 1 - z
    inner = jnp.logical_or(z == 1, z == 2)
    time_dev, taps = pv.shape
    panels, modes = shape_ref.shape
    floors = fshape_ref.shape[0]
    rows = panels + floors
    th = time_dev // nc
    tblocks = th // LANES
    md = modes // owners
    fd = floors // owners
    f32 = jnp.float32
    bf16 = jnp.bfloat16

    small = [
        pltpu.make_async_copy(src, dst, in_sem.at[i])
        for i, (src, dst) in enumerate(
            (
                (area_h, area_ref), (panel_h, panel_ref), (floor_h, floor_ref), (shape_h, shape_ref),
                (fshape_h, fshape_ref), (order_h, order_ref), (decay_h, decay_ref), (freq_h, freq_ref),
            )
        )
    ]
    for cp in small[:3]:
        cp.start()
    loads = []
    for i, (b, n) in enumerate(pieces):
        for h, half in enumerate((other, c)):
            off = pl.multiple_of(half * th + b * LANES, LANES)
            cp = pltpu.make_async_copy(
                p_hbm.at[pl.ds(off, n * LANES)], pv.at[pl.ds(off, n * LANES)], p_sem.at[2 * i + h]
            )
            cp.start()
            loads.append((cp, off))
    for cp in small[3:]:
        cp.start()

    barrier = pltpu.get_barrier_semaphore()

    def greet(**to):
        pl.semaphore_signal(barrier, inc=1, device_id=to, device_id_type=MESH)

    greet(floors=other)
    greet(taps=mate)
    for k in range(1, ntm):
        greet(tm=lax.rem(x + k, ntm))

    @pl.when(inner)
    def _():
        greet(taps=far)

    for cp in small[:3]:
        cp.wait()
    ids = lax.broadcasted_iota(jnp.int32, (panels, LANES), 0)
    fids = lax.broadcasted_iota(jnp.int32, (floors, LANES), 0)
    area = area_ref[...].astype(f32)
    for r in range(taps // LANES):
        cols = slice(r * LANES, (r + 1) * LANES)
        row = area[r : r + 1, :]
        w_ref[0:panels, cols] = jnp.where(panel_ref[:, cols] == ids, row, 0.0).astype(bf16)
        w_ref[panels:rows, cols] = jnp.where(floor_ref[:, cols] == fids, row, 0.0).astype(bf16)

    def sums(i, h, dst):
        b, n = pieces[i]
        cp, off = loads[2 * i + h]
        cp.wait()
        q = dot_nt(w_ref[...], pv[pl.ds(off, n * LANES), :])
        for k in range(n):
            dst[b + k] = q[:, k * LANES : (k + 1) * LANES]

    def pair_copy(k):
        return pltpu.make_async_remote_copy(
            src_ref=send_p.at[k], dst_ref=recv_p.at[k], send_sem=pp_s, recv_sem=pp_r.at[k],
            device_id={"floors": other}, device_id_type=MESH,
        )

    def up_copy(k):
        return pltpu.make_async_remote_copy(
            src_ref=mine.at[k, pl.ds(0, panels)], dst_ref=up.at[k], send_sem=u_s, recv_sem=u_r.at[k],
            device_id={"taps": mate}, device_id_type=MESH,
        )

    def merge(i):
        b, n = pieces[i]
        for k in range(b, b + n):
            pair_copy(k).wait_recv()
            mine[k] = mine[k] + recv_p[k]

            @pl.when(jnp.logical_not(inner))
            def _():
                up_copy(k).start()

    for i, (b, n) in enumerate(pieces):
        sums(i, 0, send_p)
        if i == 0:

            @pl.when(inner)
            def _():
                pl.semaphore_wait(barrier, 3 + ntm - 1)

            @pl.when(jnp.logical_not(inner))
            def _():
                pl.semaphore_wait(barrier, 2 + ntm - 1)

        for k in range(b, b + n):
            pair_copy(k).start()
        sums(i, 1, mine)
        merge(i)

    @pl.when(inner)
    def _():
        pl.semaphore_signal(known, inc=1, device_id={"taps": far}, device_id_type=MESH)

    for cp in small[3:]:
        cp.wait()
    order_col[...] = jnp.transpose(jnp.broadcast_to(order_ref[...].astype(f32), (LANES, modes)))

    def pick(off, n):
        mode_ids = lax.broadcasted_iota(jnp.int32, (n, modes), 1).astype(f32)
        return order_col[pl.ds(pl.multiple_of(off, n), n), 0:1] == mode_ids

    for r in range(owners):
        hot = pick(r * md, md).astype(f32).astype(bf16)
        g_ref[r * md : (r + 1) * md] = dot_nt(hot, shape_ref[...]).astype(bf16)

    def project(chip, n, q):
        size = n * nc * md
        return dot_split(g_ref[pl.ds(pl.multiple_of(chip * nc * md, size), size), :], q)

    def cross_copy(k, i):
        return pltpu.make_async_remote_copy(
            src_ref=sx.at[k, i], dst_ref=fx.at[k, c], send_sem=x_s, recv_sem=x_r.at[k],
            device_id={"taps": 2 * (1 - side) + i // nc, "floors": i % nc}, device_id_type=MESH,
        )

    def mate_copy(k, i):
        return pltpu.make_async_remote_copy(
            src_ref=si.at[k, i], dst_ref=fi.at[k, c], send_sem=i_s, recv_sem=i_r.at[k],
            device_id={"taps": mate, "floors": i}, device_id_type=MESH,
        )

    def exchange(k):
        return pltpu.make_async_remote_copy(
            src_ref=sp.at[k], dst_ref=fb.at[c * tblocks + k], send_sem=e_s, recv_sem=e_r.at[k],
            device_id={"floors": other}, device_id_type=MESH,
        )

    def keep(k, both):
        both = both.reshape(nc, md, LANES)
        sp[k] = jnp.where(c == 0, both[1], both[0])
        exchange(k).start()
        fb[c * tblocks + k] = jnp.where(c == 0, both[0], both[1])

    @pl.when(inner)
    def _():
        for k in range(tblocks):
            si[k] = project(mate, 1, mine[k, 0:panels]).reshape(nc, md, LANES)
            for i in range(nc):
                mate_copy(k, i).start()

    @pl.when(jnp.logical_not(inner))
    def _():
        for k in range(tblocks):
            keep(k, project(z, 1, mine[k, 0:panels]))

    for k in range(tblocks):
        part = mine[k, panels:rows]
        for j in range(owners):
            fls[j, :, k * LANES : (k + 1) * LANES] = part[j * fd : (j + 1) * fd]

    hot_me = pick(me * md, md)
    d = jnp.sum(jnp.where(hot_me, decay_ref[...], 0.0), axis=1, keepdims=True)
    w = jnp.sum(jnp.where(hot_me, freq_ref[...], 0.0), axis=1, keepdims=True)
    ls = dot_nt(fshape_ref[...], hot_me.astype(f32).astype(bf16)).astype(bf16)
    e2 = 2.0 * d
    poly = jnp.full_like(e2, 1.0 / 40320.0)
    for coef in (1.0 / 5040, 1.0 / 720, 1.0 / 120, 1.0 / 24, 1.0 / 6, 0.5, 1.0):
        poly = coef - e2 * poly
    gain = jnp.sqrt(e2 * poly)
    lane = lax.broadcasted_iota(jnp.int32, (md, LANES), 1)
    ahead = (lane + 1).astype(f32)
    mag = jnp.exp(-d * ahead)
    t_re = mag * jnp.cos(w * ahead)
    t_im = mag * jnp.sin(w * ahead)
    tabs[0] = t_re
    tabs[1] = t_im
    hops = []
    step = 1
    while step < LANES:
        i = 2 + 2 * len(hops)
        tabs[i] = jnp.where(lane >= step, t_re[:, step - 1 : step], 0.0)
        tabs[i + 1] = jnp.where(lane >= step, t_im[:, step - 1 : step], 0.0)
        hops.append(step)
        step *= 2

    @pl.when(inner)
    def _():
        pl.semaphore_wait(known, 1)
        pl.semaphore_signal(known, inc=1, device_id={"taps": mate}, device_id_type=MESH)
        for k in range(tblocks):
            up_copy(k).wait_recv()
            total = mine[k, 0:panels] + up[k]
            sx[k] = project(2 * (1 - side), 2, total).reshape(2 * nc, md, LANES)
            for i in range(2 * nc):
                cross_copy(k, i).start()
            keep(k, project(z, 1, total))

    @pl.when(jnp.logical_not(inner))
    def _():
        pl.semaphore_wait(known, 1)

    def load_copy(k):
        j = lax.rem(me + k, owners)
        return pltpu.make_async_remote_copy(
            src_ref=fls.at[j], dst_ref=flr.at[k - 1], send_sem=fl_s, recv_sem=fl_r,
            device_id={"taps": j // nc, "floors": lax.rem(j, nc)}, device_id_type=MESH,
        )

    def load_start(k, carry):
        load_copy(k).start()
        return carry

    lax.fori_loop(1, owners, load_start, 0)

    def at_rest(blk, force):
        re = gain * force
        im = None
        for i, step in enumerate(hops):
            a, b = tabs[2 + 2 * i], tabs[3 + 2 * i]
            rr = pltpu.roll(re, step, 1)
            if im is None:
                re, im = re + a * rr, b * rr
            else:
                ri = pltpu.roll(im, step, 1)
                re, im = re + a * rr - b * ri, im + a * ri + b * rr
        loc[blk] = re
        loc_im[blk] = im

    for k in range(tblocks):
        exchange(k).wait_recv()

        @pl.when(jnp.logical_not(inner))
        def _():
            pltpu.make_async_copy(fi.at[k], fi.at[k], i_r.at[k]).wait()
            for h in range(nc):
                fb[h * tblocks + k] = fb[h * tblocks + k] + fi[k, h]

        pltpu.make_async_copy(fx.at[k], fx.at[k], x_r.at[k]).wait()
        for h in range(nc):
            at_rest(h * tblocks + k, fb[h * tblocks + k] + fx[k, h])

    nb = time_dev // LANES
    end_re = [loc[blk][:, LANES - 1 :] for blk in range(nb)]
    end_im = [loc_im[blk][:, LANES - 1 :] for blk in range(nb)]
    zb_re, zb_im = t_re[:, LANES - 1 :], t_im[:, LANES - 1 :]
    s_re, s_im = end_re[0], end_im[0]
    for blk in range(1, nb):
        s_re, s_im = (
            zb_re * s_re - zb_im * s_im + end_re[blk],
            zb_im * s_re + zb_re * s_im + end_im[blk],
        )

    def state_copy(to, src):
        return pltpu.make_async_remote_copy(
            src_ref=st_send, dst_ref=st_recv.at[src], send_sem=t_s.at[to], recv_sem=t_r.at[src],
            device_id={"tm": to}, device_id_type=MESH,
        )

    st_send[...] = jnp.where(lane == 0, s_re, s_im)
    in_re = jnp.zeros((md, 1), f32)
    in_im = jnp.zeros((md, 1), f32)
    if ntm > 1:
        for to in range(1, ntm):

            @pl.when(x < to)
            def _():
                state_copy(to, jnp.minimum(x, ntm - 2)).start()

        for src in range(ntm - 1):

            @pl.when(x > src)
            def _():
                state_copy(lax.rem(x + 1, ntm), src).wait_recv()

            @pl.when(x <= src)
            def _():
                st_recv[src] = jnp.zeros_like(st_send)

            got_re, got_im = st_recv[src][:, 0:1], st_recv[src][:, 1:2]
            if ntm == 2:
                in_re, in_im = got_re, got_im
                continue
            length = (jnp.maximum(x - 1 - src, 0) * time_dev).astype(f32)
            pm = jnp.exp(-d * length)
            pr, pi = pm * jnp.cos(w * length), pm * jnp.sin(w * length)
            in_re = in_re + pr * got_re - pi * got_im
            in_im = in_im + pi * got_re + pr * got_im

    t_re, t_im = tabs[0], tabs[1]
    for blk in range(nb):
        y = loc[blk] + t_re * in_re - t_im * in_im
        cols = slice(blk * LANES, (blk + 1) * LANES)
        y_ref[:, cols] = y
        in_re, in_im = (
            zb_re * in_re - zb_im * in_im + end_re[blk],
            zb_im * in_re + zb_re * in_im + end_im[blk],
        )
    part = dot_split(ls, y_ref[...])
    for j in range(owners):
        fs[j] = part[j * fd : (j + 1) * fd]

    def motion_copy(k):
        j = lax.rem(me + k, owners)
        return pltpu.make_async_remote_copy(
            src_ref=fs.at[j], dst_ref=fr.at[k - 1], send_sem=f_s, recv_sem=f_r,
            device_id={"taps": j // nc, "floors": lax.rem(j, nc)}, device_id_type=MESH,
        )

    def motion_start(k, carry):
        motion_copy(k).start()
        return carry

    lax.fori_loop(1, owners, motion_start, 0)

    def drain(ref, sem):
        pltpu.make_async_copy(ref, ref, sem).wait()

    drain(flr, fl_r)
    load_scale = (floors / (taps * owners)) ** 0.5
    halves = []
    for h in range(nc):
        total = jnp.where(c == h, fls[me], 0.0)
        for k in range(1, owners):
            src = lax.rem(me + owners - k, owners)
            total = total + jnp.where(lax.rem(src, nc) == h, flr[k - 1], 0.0)
        halves.append(total * load_scale)
    for h in range(nc):
        fl_ref[:, h * th : (h + 1) * th] = halves[h]

    drain(send_p, pp_s)

    @pl.when(inner)
    def _():
        drain(si, i_s)
        drain(sx, x_s)

    @pl.when(jnp.logical_not(inner))
    def _():
        drain(up, u_s)

    drain(sp, e_s)
    drain(flr, fl_s)
    for to in range(1, ntm):

        @pl.when(x < to)
        def _():
            state_copy(to, jnp.minimum(x, ntm - 2)).wait_send()

    drain(fr, f_r)
    total = fs[me]
    for k in range(1, owners):
        total = total + fr[k - 1]
    fm_ref[...] = total
    drain(fr, f_s)


def write_out(y, fm, fl, y_out, fm_out, fl_out, sem):
    copies = [
        pltpu.make_async_copy(src, dst, sem.at[i])
        for i, (src, dst) in enumerate(((y, y_out), (fm, fm_out), (fl, fl_out)))
    ]
    for cp in copies:
        cp.start()
    for cp in copies:
        cp.wait()


def on_device(
    pressures, tap_area, tap_panel, tap_floor, panel_shape, floor_shape, mode_order, mode_decay, mode_freq
):
    nz, nc, ntm = lax.axis_size("taps"), lax.axis_size("floors"), lax.axis_size("tm")
    owners = nz * nc
    time_dev, taps = pressures.shape
    panels, modes = panel_shape.shape
    floors = floor_shape.shape[0]
    rows = panels + floors
    splits = 2
    th = time_dev // nc
    md, fd = modes // owners, floors // owners
    nch = th // LANES * splits
    xrows = md + -(-fd // 8) * 8
    vmem = pl.BlockSpec(memory_space=pltpu.VMEM)
    dma = pltpu.SemaphoreType.DMA
    f32 = jnp.float32
    tb, nb = th // LANES, time_dev // LANES
    inputs = [
        pltpu.VMEM((taps // LANES, LANES), jnp.bfloat16),
        pltpu.VMEM((1, taps), jnp.int32),
        pltpu.VMEM((1, taps), jnp.int32),
        pltpu.VMEM(panel_shape.shape, jnp.bfloat16),
        pltpu.VMEM(floor_shape.shape, jnp.bfloat16),
        pltpu.VMEM((1, modes), jnp.int32),
        pltpu.VMEM((1, modes), f32),
        pltpu.VMEM((1, modes), f32),
        pltpu.VMEM((modes, LANES), f32),
        pltpu.VMEM((time_dev, taps), jnp.bfloat16),
        pltpu.VMEM((rows, taps), jnp.bfloat16),
    ]
    response = [
        pltpu.VMEM((16, md, LANES), f32),
        pltpu.VMEM((nb, md, LANES), f32),
        pltpu.VMEM((nb, md, LANES), f32),
        pltpu.VMEM((md, LANES), f32),
        pltpu.VMEM((max(ntm - 1, 1), md, LANES), f32),
    ]
    if nz == 4 and nc == 2 and tb % 2 == 0:
        block = pltpu.VMEM((tb, rows, LANES), f32)
        pieces = ((0, 1), (1, 1)) + tuple((b, 2) for b in range(2, tb, 2))
        body = functools.partial(two_stage, (nz, nc, ntm, pieces))
        scratch = (
            inputs
            + [pltpu.VMEM((modes, panels), jnp.bfloat16), block, block, block]
            + [
                pltpu.VMEM((tb, panels, LANES), f32),
                pltpu.VMEM((tb, 2 * nc, md, LANES), f32),
                pltpu.VMEM((tb, nc, md, LANES), f32),
                pltpu.VMEM((tb, nc, md, LANES), f32),
                pltpu.VMEM((tb, nc, md, LANES), f32),
                pltpu.VMEM((tb, md, LANES), f32),
                pltpu.VMEM((nb, md, LANES), f32),
            ]
            + response
            + [
                pltpu.VMEM((owners, fd, th), f32),
                pltpu.VMEM((owners - 1, fd, th), f32),
                pltpu.VMEM((owners, fd, time_dev), f32),
                pltpu.VMEM((owners - 1, fd, time_dev), f32),
                dma((8,)), dma((2 * len(pieces),)),
                dma(()), dma((tb,)), dma(()), dma((tb,)), dma(()), dma((tb,)), dma(()), dma((tb,)),
                dma(()), dma((tb,)), dma(()), dma(()), dma((ntm,)), dma((ntm,)), dma(()), dma(()),
                pltpu.SemaphoreType.REGULAR,
            ]
        )
    else:
        chunk = pltpu.VMEM((nch, rows // splits, LANES), f32)
        body = functools.partial(kernel, (nz, nc, ntm, splits))
        scratch = (
            inputs
            + [chunk] * 7
            + [pltpu.VMEM((tb, xrows, LANES), f32), pltpu.VMEM((nb, xrows, LANES), f32)]
            + response
            + [
                pltpu.VMEM((owners, fd, time_dev), f32),
                pltpu.VMEM((owners, fd, time_dev), f32),
                dma((8,)),
                dma((2 * (th // min(256, th)),)),
                dma((nch,)), dma((nch,)), dma((nch,)), dma((nch,)), dma((nch,)), dma((nch,)),
                dma((tb,)), dma((tb,)),
                dma((ntm,)), dma((ntm,)),
                dma((owners,)), dma((owners,)),
            ]
        )
    out = pl.pallas_call(
        body,
        out_shape=(
            pltpu.VMEM((md, time_dev), f32),
            pltpu.VMEM((fd, time_dev), f32),
            pltpu.VMEM((fd, time_dev), f32),
        ),
        in_specs=[pl.BlockSpec(memory_space=pltpu.HBM)] * 9,
        out_specs=(vmem,) * 3,
        scratch_shapes=scratch,
        compiler_params=pltpu.CompilerParams(
            collective_id=0, has_side_effects=True, vmem_limit_bytes=VMEM_LIMIT
        ),
    )(
        *(
            pltpu.with_memory_space_constraint(a, pltpu.HBM)
            for a in (
                pressures,
                tap_area.reshape(taps // LANES, LANES),
                tap_panel.reshape(1, taps),
                tap_floor.reshape(1, taps),
                panel_shape,
                floor_shape,
                mode_order.reshape(1, modes),
                mode_decay.reshape(1, modes),
                mode_freq.reshape(1, modes),
            )
        )
    )
    return pl.pallas_call(
        write_out,
        out_shape=tuple(jax.ShapeDtypeStruct(o.shape, o.dtype) for o in out),
        in_specs=[vmem] * 3,
        out_specs=(pl.BlockSpec(memory_space=pltpu.HBM),) * 3,
        scratch_shapes=[dma((3,))],
        compiler_params=pltpu.CompilerParams(vmem_limit_bytes=VMEM_LIMIT),
    )(*out)


def solution(mesh):
    own = P(("taps", "floors"))
    out_spec = P(("taps", "floors"), ("dirs", "tm"))
    return jax.shard_map(
        on_device,
        mesh=mesh,
        in_specs=(P(("dirs", "tm"), ("taps", "floors")), own, own, own, P(), P(), P(), P(), P()),
        out_specs=(out_spec, out_spec, out_spec),
        check_vma=False,
    )
```

```python
import functools

import jax
import jax.numpy as jnp
from jax import lax
from jax.experimental import pallas as pl
from jax.experimental.pallas import tpu as pltpu
from jax.sharding import PartitionSpec as P

MESH = pl.DeviceIdType.MESH
LANES = 128
LAG = 2
VMEM_LIMIT = 32 * 1024 * 1024
NT = (((1,), (1,)), ((), ()))


def dot_nt(a, b):
    return lax.dot_general(a, b, NT, preferred_element_type=jnp.float32)


def dot_split(a, b):
    hi = b.astype(jnp.bfloat16)
    lo = (b - hi.astype(jnp.float32)).astype(jnp.bfloat16)
    return jnp.dot(a, hi, preferred_element_type=jnp.float32) + jnp.dot(
        a, lo, preferred_element_type=jnp.float32
    )


def kernel(
    cfg,
    p_hbm, area_h, panel_h, floor_h, shape_h, fshape_h, order_h, decay_h, freq_h,
    y_ref, fm_ref, fl_ref,
    area_ref, panel_ref, floor_ref, shape_ref, fshape_ref, order_ref, decay_ref, freq_ref, order_col,
    pv, w_ref, mine, send_p, recv_p, rin, lin, rout, lout, xs, fb, tabs, loc, loc_im, st_send, st_recv,
    fs, fr,
    in_sem, p_sem, pp_s, pp_r, r_s, r_r, l_s, l_r, x_s, x_r, t_s, t_r, f_s, f_r,
):
    nz, nc, ntm, splits = cfg
    owners = nz * nc
    z = lax.axis_index("taps")
    c = lax.axis_index("floors")
    x = lax.axis_index("tm")
    me = z * nc + c
    other = nc - 1 - c
    time_dev, taps = pv.shape
    panels, modes = shape_ref.shape
    floors = fshape_ref.shape[0]
    rows = panels + floors
    th = time_dev // nc
    tblocks = th // LANES
    crows = rows // splits
    nch = tblocks * splits
    md = modes // owners
    fd = floors // owners
    f32 = jnp.float32
    bf16 = jnp.bfloat16

    small = [
        pltpu.make_async_copy(src, dst, in_sem.at[i])
        for i, (src, dst) in enumerate(
            (
                (area_h, area_ref), (panel_h, panel_ref), (floor_h, floor_ref), (shape_h, shape_ref),
                (fshape_h, fshape_ref), (order_h, order_ref), (decay_h, decay_ref), (freq_h, freq_ref),
            )
        )
    ]
    for cp in small:
        cp.start()

    barrier = pltpu.get_barrier_semaphore()

    def greet(k, carry):
        j = lax.rem(me + k, owners)
        pl.semaphore_signal(
            barrier, inc=1, device_id={"taps": j // nc, "floors": lax.rem(j, nc)}, device_id_type=MESH
        )
        return carry

    lax.fori_loop(1, owners, greet, 0)
    for k in range(1, ntm):
        pl.semaphore_signal(
            barrier, inc=1, device_id={"tm": lax.rem(x + k, ntm)}, device_id_type=MESH
        )

    step_t = min(256, th)
    per_half = th // step_t
    loads = []
    for h in range(2):
        half = other if h == 0 else c
        for b in range(per_half):
            off = pl.multiple_of(half * th + b * step_t, step_t)
            cp = pltpu.make_async_copy(
                p_hbm.at[pl.ds(off, step_t)], pv.at[pl.ds(off, step_t)], p_sem.at[h * per_half + b]
            )
            cp.start()
            loads.append((cp, off))

    for cp in small[:3]:
        cp.wait()
    ids = lax.broadcasted_iota(jnp.int32, (panels, LANES), 0)
    fids = lax.broadcasted_iota(jnp.int32, (floors, LANES), 0)
    area = area_ref[...].astype(f32)
    for r in range(taps // LANES):
        cols = slice(r * LANES, (r + 1) * LANES)
        row = area[r : r + 1, :]
        w_ref[0:panels, cols] = jnp.where(panel_ref[:, cols] == ids, row, 0.0).astype(bf16)
        w_ref[panels:rows, cols] = jnp.where(floor_ref[:, cols] == fids, row, 0.0).astype(bf16)

    def sums(b, h, dst):
        cp, off = loads[h * per_half + b]
        cp.wait()
        q = dot_nt(w_ref[...], pv[pl.ds(off, step_t), :])
        for i in range(step_t // LANES):
            for s in range(splits):
                dst[(b * step_t // LANES + i) * splits + s] = q[
                    s * crows : (s + 1) * crows, i * LANES : (i + 1) * LANES
                ]

    def pair_copy(k):
        return pltpu.make_async_remote_copy(
            src_ref=send_p.at[k], dst_ref=recv_p.at[k], send_sem=pp_s.at[k], recv_sem=pp_r.at[k],
            device_id={"floors": other}, device_id_type=MESH,
        )

    per_step = step_t // LANES * splits

    @pl.when(z == 0)
    def _():
        rin[...] = jnp.zeros_like(rin)

    @pl.when(z == nz - 1)
    def _():
        lin[...] = jnp.zeros_like(lin)

    def line_copy(k, right):
        src, dst, ss, rs = (rout, rin, r_s, r_r) if right else (lout, lin, l_s, l_r)
        to = jnp.minimum(z + 1, nz - 1) if right else jnp.maximum(z - 1, 0)
        return pltpu.make_async_remote_copy(
            src_ref=src.at[k], dst_ref=dst.at[k], send_sem=ss.at[k], recv_sem=rs.at[k],
            device_id={"taps": to}, device_id_type=MESH,
        )

    def line_step(s, carry):
        for right in (True, False):
            hop = z if right else nz - 1 - z
            k = s - LAG * hop
            came, out = (rin, rout) if right else (lin, lout)

            @pl.when(jnp.logical_and(k >= 0, k < nch))
            def _():
                @pl.when(hop > 0)
                def _():
                    line_copy(k, right).wait_recv()

                @pl.when(hop < nz - 1)
                def _():
                    out[k] = mine[k] + came[k]
                    line_copy(k, right).start()

        return carry

    def merge(b):
        for k in range(b * per_step, (b + 1) * per_step):
            pair_copy(k).wait_recv()
            mine[k] = mine[k] + recv_p[k]

    for b in range(per_half):
        sums(b, 0, send_p)
        if b == 0:
            pl.semaphore_wait(barrier, owners - 1 + ntm - 1)
        for k in range(b * per_step, (b + 1) * per_step):
            pair_copy(k).start()
        if b > 0:
            merge(b - 1)
        if b == 1:
            lax.fori_loop(0, min(LAG, per_step), line_step, 0)
        sums(b, 1, mine)
    merge(per_half - 1)
    first = min(LAG, per_step) if per_half > 1 else 0
    early = min(LAG, nch)
    lax.fori_loop(first, early, line_step, 0)

    for cp in small[3:]:
        cp.wait()
    order_col[...] = jnp.transpose(jnp.broadcast_to(order_ref[...].astype(f32), (LANES, modes)))
    mode_ids = lax.broadcasted_iota(jnp.int32, (md, modes), 1).astype(f32)

    def pick(owner):
        return order_col[pl.ds(pl.multiple_of(owner * md, md), md), 0:1] == mode_ids

    def shapes(hot):
        return dot_nt(hot.astype(f32).astype(bf16), shape_ref[...]).astype(bf16)

    hot_me = pick(me)
    hot_other = pick(z * nc + other)
    g_both = jnp.concatenate([shapes(hot_other), shapes(hot_me)], axis=0)
    d = jnp.sum(jnp.where(hot_me, decay_ref[...], 0.0), axis=1, keepdims=True)
    w = jnp.sum(jnp.where(hot_me, freq_ref[...], 0.0), axis=1, keepdims=True)
    ls = dot_nt(fshape_ref[...], hot_me.astype(f32).astype(bf16)).astype(bf16)
    e2 = 2.0 * d
    poly = jnp.full_like(e2, 1.0 / 40320.0)
    for coef in (1.0 / 5040, 1.0 / 720, 1.0 / 120, 1.0 / 24, 1.0 / 6, 0.5, 1.0):
        poly = coef - e2 * poly
    gain = jnp.sqrt(e2 * poly)
    lane = lax.broadcasted_iota(jnp.int32, (md, LANES), 1)
    ahead = (lane + 1).astype(f32)
    mag = jnp.exp(-d * ahead)
    t_re = mag * jnp.cos(w * ahead)
    t_im = mag * jnp.sin(w * ahead)
    tabs[0] = t_re
    tabs[1] = t_im
    hops = []
    step = 1
    while step < LANES:
        i = 2 + 2 * len(hops)
        tabs[i] = jnp.where(lane >= step, t_re[:, step - 1 : step], 0.0)
        tabs[i + 1] = jnp.where(lane >= step, t_im[:, step - 1 : step], 0.0)
        hops.append(step)
        step *= 2

    floor_row = lax.broadcasted_iota(jnp.int32, (floors, LANES), 0)

    def load_row(q, row):
        return jnp.sum(jnp.where(floor_row == row, q, 0.0), axis=0, keepdims=True)

    def exchange(tb):
        return pltpu.make_async_remote_copy(
            src_ref=xs.at[tb], dst_ref=fb.at[c * tblocks + tb],
            send_sem=x_s.at[tb], recv_sem=x_r.at[tb],
            device_id={"floors": other}, device_id_type=MESH,
        )

    def forces(tb):
        q = jnp.concatenate(
            [mine[k] + rin[k] + lin[k] for k in range(tb * splits, (tb + 1) * splits)], axis=0
        )
        both = dot_split(g_both, q[:panels])
        blk = c * tblocks + tb
        pad = [jnp.zeros((xs.shape[1] - md - fd, LANES), f32)] if xs.shape[1] > md + fd else []
        theirs = [load_row(q[panels:], (z * nc + other) * fd + r) for r in range(fd)]
        ours = [load_row(q[panels:], me * fd + r) for r in range(fd)]
        xs[tb] = jnp.concatenate([both[:md]] + theirs + pad, axis=0)
        exchange(tb).start()
        fb[blk] = jnp.concatenate([both[md:]] + ours + pad, axis=0)

    def at_rest(blk):
        re = gain * fb[blk, 0:md, :]
        im = None
        for i, step in enumerate(hops):
            a, b = tabs[2 + 2 * i], tabs[3 + 2 * i]
            rr = pltpu.roll(re, step, 1)
            if im is None:
                re, im = re + a * rr, b * rr
            else:
                ri = pltpu.roll(im, step, 1)
                re, im = re + a * rr - b * ri, im + a * ri + b * rr
        loc[blk] = re
        loc_im[blk] = im

    done = early
    for tb in range(tblocks):
        upto = (tb + 1) * splits + LAG * (nz - 1)
        lax.fori_loop(done, upto, line_step, 0)
        done = upto
        forces(tb)
        at_rest(c * tblocks + tb)
        if tb > 0:
            exchange(tb - 1).wait_recv()
            at_rest(other * tblocks + tb - 1)
    exchange(tblocks - 1).wait_recv()
    at_rest(other * tblocks + tblocks - 1)
    nb = time_dev // LANES
    end_re = [loc[blk][:, LANES - 1 :] for blk in range(nb)]
    end_im = [loc_im[blk][:, LANES - 1 :] for blk in range(nb)]

    zb_re, zb_im = t_re[:, LANES - 1 :], t_im[:, LANES - 1 :]
    s_re, s_im = end_re[0], end_im[0]
    for blk in range(1, nb):
        s_re, s_im = (
            zb_re * s_re - zb_im * s_im + end_re[blk],
            zb_im * s_re + zb_re * s_im + end_im[blk],
        )

    def state_copy(to, src):
        return pltpu.make_async_remote_copy(
            src_ref=st_send, dst_ref=st_recv.at[src], send_sem=t_s.at[to], recv_sem=t_r.at[src],
            device_id={"tm": to}, device_id_type=MESH,
        )

    st_send[...] = jnp.where(lane == 0, s_re, s_im)
    in_re = jnp.zeros((md, 1), f32)
    in_im = jnp.zeros((md, 1), f32)
    if ntm > 1:
        for to in range(1, ntm):

            @pl.when(x < to)
            def _():
                state_copy(to, jnp.minimum(x, ntm - 2)).start()

        for src in range(ntm - 1):

            @pl.when(x > src)
            def _():
                state_copy(lax.rem(x + 1, ntm), src).wait_recv()

            @pl.when(x <= src)
            def _():
                st_recv[src] = jnp.zeros_like(st_send)

            got_re, got_im = st_recv[src][:, 0:1], st_recv[src][:, 1:2]
            if ntm == 2:
                in_re, in_im = got_re, got_im
                continue
            length = (jnp.maximum(x - 1 - src, 0) * time_dev).astype(f32)
            pm = jnp.exp(-d * length)
            pr, pi = pm * jnp.cos(w * length), pm * jnp.sin(w * length)
            in_re = in_re + pr * got_re - pi * got_im
            in_im = in_im + pi * got_re + pr * got_im

    t_re, t_im = tabs[0], tabs[1]
    for blk in range(nb):
        y = loc[blk] + t_re * in_re - t_im * in_im
        cols = slice(blk * LANES, (blk + 1) * LANES)
        y_ref[:, cols] = y
        in_re, in_im = (
            zb_re * in_re - zb_im * in_im + end_re[blk],
            zb_im * in_re + zb_re * in_im + end_im[blk],
        )
    part = dot_split(ls, y_ref[...])
    for j in range(owners):
        fs[j] = part[j * fd : (j + 1) * fd]

    def motion_copy(k):
        j = lax.rem(me + k, owners)
        return pltpu.make_async_remote_copy(
            src_ref=fs.at[j], dst_ref=fr.at[me], send_sem=f_s.at[k], recv_sem=f_r.at[k],
            device_id={"taps": j // nc, "floors": lax.rem(j, nc)}, device_id_type=MESH,
        )

    def motion_start(k, carry):
        motion_copy(k).start()
        return carry

    def motion_recv(k, total):
        motion_copy(k).wait_recv()
        return total + fr[lax.rem(me + owners - k, owners)]

    def motion_sent(k, carry):
        motion_copy(k).wait_send()
        return carry

    lax.fori_loop(1, owners, motion_start, 0)
    load_scale = (floors / (taps * owners)) ** 0.5
    for blk in range(nb):
        fl_ref[:, blk * LANES : (blk + 1) * LANES] = fb[blk, md : md + fd, :] * load_scale

    for k in range(nch):
        pair_copy(k).wait_send()

    def line_sent(k, carry):
        @pl.when(z < nz - 1)
        def _():
            line_copy(k, True).wait_send()

        @pl.when(z > 0)
        def _():
            line_copy(k, False).wait_send()

        return carry

    lax.fori_loop(0, nch, line_sent, 0)
    for tb in range(tblocks):
        exchange(tb).wait_send()
    for to in range(1, ntm):

        @pl.when(x < to)
        def _():
            state_copy(to, jnp.minimum(x, ntm - 2)).wait_send()

    fm_ref[...] = lax.fori_loop(1, owners, motion_recv, fs[me])
    lax.fori_loop(1, owners, motion_sent, 0)


def two_stage(
    cfg,
    p_hbm, area_h, panel_h, floor_h, shape_h, fshape_h, order_h, decay_h, freq_h,
    y_ref, fm_ref, fl_ref,
    area_ref, panel_ref, floor_ref, shape_ref, fshape_ref, order_ref, decay_ref, freq_ref, order_col,
    pv, w_ref, g_ref, send_p, recv_p, mine, up, sx, fx, si, fi, sp, fb, tabs, loc, loc_im, ends, st_send, st_recv,
    fls, flr, fs, fr, cs, cr,
    in_sem, p_sem, pp_s, pp_r, u_s, u_r, x_s, x_r, i_s, i_r, e_s, e_r, fl_s, fl_r, t_s, t_r, f_s, f_r, c_s, c_r, known,
):
    nz, nc, ntm, pieces = cfg
    owners = nz * nc
    z = lax.axis_index("taps")
    c = lax.axis_index("floors")
    x = lax.axis_index("tm")
    me = z * nc + c
    other = nc - 1 - c
    side = z // 2
    mate = z + 1 - 2 * lax.rem(z, 2)
    far = nz - 1 - z
    inner = jnp.logical_or(z == 1, z == 2)
    time_dev, taps = pv.shape
    panels, modes = shape_ref.shape
    floors = fshape_ref.shape[0]
    rows = panels + floors
    th = time_dev // nc
    tblocks = th // LANES
    md = modes // owners
    fd = floors // owners
    f32 = jnp.float32
    bf16 = jnp.bfloat16

    small = [
        pltpu.make_async_copy(src, dst, in_sem.at[i])
        for i, (src, dst) in enumerate(
            (
                (area_h, area_ref), (panel_h, panel_ref), (floor_h, floor_ref), (shape_h, shape_ref),
                (fshape_h, fshape_ref), (order_h, order_ref), (decay_h, decay_ref), (freq_h, freq_ref),
            )
        )
    ]
    for cp in small[:3]:
        cp.start()
    loads = []
    for i, (b, n) in enumerate(pieces):
        for h, half in enumerate((other, c)):
            off = pl.multiple_of(half * th + b * LANES, LANES)
            cp = pltpu.make_async_copy(
                p_hbm.at[pl.ds(off, n * LANES)], pv.at[pl.ds(off, n * LANES)], p_sem.at[2 * i + h]
            )
            cp.start()
            loads.append((cp, off))
    for cp in small[3:]:
        cp.start()

    barrier = pltpu.get_barrier_semaphore()

    def greet(**to):
        pl.semaphore_signal(barrier, inc=1, device_id=to, device_id_type=MESH)

    greet(floors=other)
    greet(taps=mate)
    for k in range(1, ntm):
        greet(tm=lax.rem(x + k, ntm))

    @pl.when(inner)
    def _():
        greet(taps=far)

    for cp in small[:3]:
        cp.wait()
    ids = lax.broadcasted_iota(jnp.int32, (panels, LANES), 0)
    fids = lax.broadcasted_iota(jnp.int32, (floors, LANES), 0)
    area = area_ref[...].astype(f32)
    for r in range(taps // LANES):
        cols = slice(r * LANES, (r + 1) * LANES)
        row = area[r : r + 1, :]
        w_ref[0:panels, cols] = jnp.where(panel_ref[:, cols] == ids, row, 0.0).astype(bf16)
        w_ref[panels:rows, cols] = jnp.where(floor_ref[:, cols] == fids, row, 0.0).astype(bf16)

    def sums(i, h, dst):
        b, n = pieces[i]
        cp, off = loads[2 * i + h]
        cp.wait()
        q = dot_nt(w_ref[...], pv[pl.ds(off, n * LANES), :])
        for k in range(n):
            dst[b + k] = q[:, k * LANES : (k + 1) * LANES]

    def pair_copy(k):
        return pltpu.make_async_remote_copy(
            src_ref=send_p.at[k], dst_ref=recv_p.at[k], send_sem=pp_s, recv_sem=pp_r.at[k],
            device_id={"floors": other}, device_id_type=MESH,
        )

    def up_copy(k):
        return pltpu.make_async_remote_copy(
            src_ref=mine.at[k, pl.ds(0, panels)], dst_ref=up.at[k], send_sem=u_s, recv_sem=u_r.at[k],
            device_id={"taps": mate}, device_id_type=MESH,
        )

    def merge(i):
        b, n = pieces[i]
        for k in range(b, b + n):
            pair_copy(k).wait_recv()
            mine[k] = mine[k] + recv_p[k]

            @pl.when(jnp.logical_not(inner))
            def _():
                up_copy(k).start()

    for i, (b, n) in enumerate(pieces):
        sums(i, 0, send_p)
        if i == 0:

            @pl.when(inner)
            def _():
                pl.semaphore_wait(barrier, 3 + ntm - 1)

            @pl.when(jnp.logical_not(inner))
            def _():
                pl.semaphore_wait(barrier, 2 + ntm - 1)

        for k in range(b, b + n):
            pair_copy(k).start()
        sums(i, 1, mine)
        merge(i)

    @pl.when(inner)
    def _():
        pl.semaphore_signal(known, inc=1, device_id={"taps": far}, device_id_type=MESH)

    for cp in small[3:]:
        cp.wait()
    order_col[...] = jnp.transpose(jnp.broadcast_to(order_ref[...].astype(f32), (LANES, modes)))

    def pick(off, n):
        mode_ids = lax.broadcasted_iota(jnp.int32, (n, modes), 1).astype(f32)
        return order_col[pl.ds(pl.multiple_of(off, n), n), 0:1] == mode_ids

    for r in range(owners):
        hot = pick(r * md, md).astype(f32).astype(bf16)
        g_ref[r * md : (r + 1) * md] = dot_nt(hot, shape_ref[...]).astype(bf16)

    def project(chip, n, q):
        size = n * nc * md
        return dot_split(g_ref[pl.ds(pl.multiple_of(chip * nc * md, size), size), :], q)

    def cross_copy(k, i):
        return pltpu.make_async_remote_copy(
            src_ref=sx.at[k, i], dst_ref=fx.at[k, c], send_sem=x_s, recv_sem=x_r.at[k],
            device_id={"taps": 2 * (1 - side) + i // nc, "floors": i % nc}, device_id_type=MESH,
        )

    def mate_copy(k, i):
        return pltpu.make_async_remote_copy(
            src_ref=si.at[k, i], dst_ref=fi.at[k, c], send_sem=i_s, recv_sem=i_r.at[k],
            device_id={"taps": mate, "floors": i}, device_id_type=MESH,
        )

    def exchange(k):
        return pltpu.make_async_remote_copy(
            src_ref=sp.at[k], dst_ref=fb.at[c * tblocks + k], send_sem=e_s, recv_sem=e_r.at[k],
            device_id={"floors": other}, device_id_type=MESH,
        )

    def keep(k, both):
        both = both.reshape(nc, md, LANES)
        sp[k] = jnp.where(c == 0, both[1], both[0])
        exchange(k).start()
        fb[c * tblocks + k] = jnp.where(c == 0, both[0], both[1])

    @pl.when(inner)
    def _():
        for k in range(tblocks):
            si[k] = project(mate, 1, mine[k, 0:panels]).reshape(nc, md, LANES)
            for i in range(nc):
                mate_copy(k, i).start()

    @pl.when(jnp.logical_not(inner))
    def _():
        for k in range(tblocks):
            keep(k, project(z, 1, mine[k, 0:panels]))

    for k in range(tblocks):
        part = mine[k, panels:rows]
        for j in range(owners):
            fls[j, :, k * LANES : (k + 1) * LANES] = part[j * fd : (j + 1) * fd]

    hot_me = pick(me * md, md)
    d = jnp.sum(jnp.where(hot_me, decay_ref[...], 0.0), axis=1, keepdims=True)
    w = jnp.sum(jnp.where(hot_me, freq_ref[...], 0.0), axis=1, keepdims=True)
    ls = dot_nt(fshape_ref[...], hot_me.astype(f32).astype(bf16)).astype(bf16)
    e2 = 2.0 * d
    poly = jnp.full_like(e2, 1.0 / 40320.0)
    for coef in (1.0 / 5040, 1.0 / 720, 1.0 / 120, 1.0 / 24, 1.0 / 6, 0.5, 1.0):
        poly = coef - e2 * poly
    gain = jnp.sqrt(e2 * poly)
    nb = time_dev // LANES
    lane = lax.broadcasted_iota(jnp.int32, (md, LANES), 1)
    steps = lane.astype(f32)
    cos, sin = jnp.cos(w * steps), jnp.sin(w * steps)
    grow = gain * jnp.exp(d * steps)
    decay = jnp.exp(-d * steps)
    t_re, t_im = decay * cos, decay * sin
    for i, table in enumerate((t_re, t_im, grow * cos, -grow * sin)):
        tabs[i] = table
    upto = lax.broadcasted_iota(jnp.int32, (LANES, 2 * LANES), 0) <= lax.broadcasted_iota(
        jnp.int32, (LANES, 2 * LANES), 1
    )
    upto = upto.astype(f32).astype(bf16)

    def times(a_re, a_im, b_re, b_im):
        return a_re * b_re - a_im * b_im, a_re * b_im + a_im * b_re

    def wide(v):
        return jnp.broadcast_to(v, (md, LANES))

    last = LANES - 1
    for i, table in enumerate(
        times(t_re[:, 1:2], t_im[:, 1:2], t_re[:, last:], t_im[:, last:])
    ):
        tabs[4 + i] = wide(table)

    def turn(re, im):
        return times(tabs[4], tabs[5], re, im)

    @pl.when(inner)
    def _():
        pl.semaphore_wait(known, 1)
        pl.semaphore_signal(known, inc=1, device_id={"taps": mate}, device_id_type=MESH)
        for k in range(tblocks):
            up_copy(k).wait_recv()
            total = mine[k, 0:panels] + up[k]
            sx[k] = project(2 * (1 - side), 2, total).reshape(2 * nc, md, LANES)
            for i in range(2 * nc):
                cross_copy(k, i).start()
            keep(k, project(z, 1, total))

    @pl.when(jnp.logical_not(inner))
    def _():
        pl.semaphore_wait(known, 1)

    def load_copy(k):
        j = lax.rem(me + k, owners)
        return pltpu.make_async_remote_copy(
            src_ref=fls.at[j], dst_ref=flr.at[k - 1], send_sem=fl_s, recv_sem=fl_r,
            device_id={"taps": j // nc, "floors": lax.rem(j, nc)}, device_id_type=MESH,
        )

    def load_start(k, carry):
        load_copy(k).start()
        return carry

    lax.fori_loop(1, owners, load_start, 0)

    def prefix(blks):
        parts = [fb[blk] * tabs[2 + i] for blk in blks for i in range(2)]
        v = jnp.concatenate(parts, axis=0)
        hi = v.astype(bf16)
        lo = (v - hi.astype(f32)).astype(bf16)
        v = jnp.dot(hi, upto, preferred_element_type=f32) + jnp.dot(
            lo, upto, preferred_element_type=f32
        )
        for n, blk in enumerate(blks):
            for i, dst in enumerate((loc, loc_im)):
                part = v[(2 * n + i) * md : (2 * n + i + 1) * md]
                dst[blk] = part[:, :LANES]
                ends[blk, i] = part[:, LANES:]

    def response(blk, re, im):
        return tabs[0] * (loc[blk] + re) - tabs[1] * (loc_im[blk] + im)

    def state_copy(to, src):
        return pltpu.make_async_remote_copy(
            src_ref=st_send, dst_ref=st_recv.at[src], send_sem=t_s.at[to], recv_sem=t_r.at[src],
            device_id={"tm": to}, device_id_type=MESH,
        )

    def carry_copy(to, src, j):
        return pltpu.make_async_remote_copy(
            src_ref=cs.at[to - 1, j], dst_ref=cr.at[src, me], send_sem=c_s.at[to], recv_sem=c_r.at[src],
            device_id={"tm": to, "taps": j // nc, "floors": j % nc}, device_id_type=MESH,
        )

    for k in range(tblocks):
        exchange(k).wait_recv()

        @pl.when(jnp.logical_not(inner))
        def _():
            pltpu.make_async_copy(fi.at[k], fi.at[k], i_r.at[k]).wait()
            for h in range(nc):
                fb[h * tblocks + k] = fb[h * tblocks + k] + fi[k, h]

        pltpu.make_async_copy(fx.at[k], fx.at[k], x_r.at[k]).wait()
        for h in range(nc):
            fb[h * tblocks + k] = fb[h * tblocks + k] + fx[k, h]
        prefix([h * tblocks + k for h in range(nc)])

    re, im = jnp.zeros((md, LANES), f32), jnp.zeros((md, LANES), f32)
    ys = []
    for blk in range(nb):
        ys.append(response(blk, re, im))
        re, im = turn(ends[blk, 0] + re, ends[blk, 1] + im)
    y = jnp.concatenate(ys, axis=1)
    y_ref[...] = y
    part = dot_split(ls, y)
    for j in range(owners):
        fs[j] = part[j * fd : (j + 1) * fd]

    def motion_copy(k):
        j = lax.rem(me + k, owners)
        return pltpu.make_async_remote_copy(
            src_ref=fs.at[j], dst_ref=fr.at[k - 1], send_sem=f_s, recv_sem=f_r,
            device_id={"taps": j // nc, "floors": lax.rem(j, nc)}, device_id_type=MESH,
        )

    def motion_start(k, carry):
        motion_copy(k).start()
        return carry

    lax.fori_loop(1, owners, motion_start, 0)
    s_re, s_im = re, im
    for to in range(1, ntm):

        @pl.when(x < to)
        def _():
            src = jnp.minimum(x, ntm - 2)
            re, im = s_re, s_im
            if ntm > 2:
                gap = ((to - 1 - x) * time_dev).astype(f32)
                pm = jnp.exp(-d * gap)
                re, im = times(pm * jnp.cos(w * gap), pm * jnp.sin(w * gap), re, im)
            ys = []
            for blk in range(nb):
                ys.append(tabs[0] * re - tabs[1] * im)
                re, im = turn(re, im)
            part = dot_split(ls, jnp.concatenate(ys, axis=1))
            for j in range(owners):
                cs[to - 1, j] = part[j * fd : (j + 1) * fd]
            for j in range(owners):
                carry_copy(to, src, j).start()
            st_send[...] = jnp.where(lane == 0, s_re, s_im)
            state_copy(to, src).start()

    in_re = jnp.zeros((md, LANES), f32)
    in_im = jnp.zeros((md, LANES), f32)
    for src in range(ntm - 1):

        @pl.when(x > src)
        def _():
            state_copy(lax.rem(x + 1, ntm), src).wait_recv()

        @pl.when(x <= src)
        def _():
            st_recv[src] = jnp.zeros_like(st_send)

        got_re, got_im = wide(st_recv[src][:, 0:1]), wide(st_recv[src][:, 1:2])
        if ntm == 2:
            in_re, in_im = got_re, got_im
            continue
        length = (jnp.maximum(x - 1 - src, 0) * time_dev).astype(f32)
        pm = jnp.exp(-d * length)
        got_re, got_im = times(pm * jnp.cos(w * length), pm * jnp.sin(w * length), got_re, got_im)
        in_re, in_im = in_re + got_re, in_im + got_im

    @pl.when(x > 0)
    def _():
        re, im = in_re, in_im
        for blk in range(nb):
            cols = slice(blk * LANES, (blk + 1) * LANES)
            y_ref[:, cols] = y_ref[:, cols] + tabs[0] * re - tabs[1] * im
            re, im = turn(re, im)

    def drain(ref, sem):
        pltpu.make_async_copy(ref, ref, sem).wait()

    drain(flr, fl_r)
    load_scale = (floors / (taps * owners)) ** 0.5
    halves = []
    for h in range(nc):
        total = jnp.where(c == h, fls[me], 0.0)
        for k in range(1, owners):
            src = lax.rem(me + owners - k, owners)
            total = total + jnp.where(lax.rem(src, nc) == h, flr[k - 1], 0.0)
        halves.append(total * load_scale)
    for h in range(nc):
        fl_ref[:, h * th : (h + 1) * th] = halves[h]

    drain(send_p, pp_s)

    @pl.when(inner)
    def _():
        drain(si, i_s)
        drain(sx, x_s)

    @pl.when(jnp.logical_not(inner))
    def _():
        drain(up, u_s)

    drain(sp, e_s)
    drain(flr, fl_s)
    for to in range(1, ntm):

        @pl.when(x < to)
        def _():
            state_copy(to, jnp.minimum(x, ntm - 2)).wait_send()

    drain(fr, f_r)
    total = fs[me]
    for k in range(1, owners):
        total = total + fr[k - 1]
    fm_ref[...] = total
    drain(fr, f_s)
    for src in range(ntm - 1):

        @pl.when(x > src)
        def _():
            drain(cr.at[src], c_r.at[src])
            carried = fm_ref[...]
            for j in range(owners):
                carried = carried + cr[src, j]
            fm_ref[...] = carried

    for to in range(1, ntm):

        @pl.when(x < to)
        def _():
            drain(cs.at[to - 1], c_s.at[to])


def write_out(y, fm, fl, y_out, fm_out, fl_out, sem):
    copies = [
        pltpu.make_async_copy(src, dst, sem.at[i])
        for i, (src, dst) in enumerate(((y, y_out), (fm, fm_out), (fl, fl_out)))
    ]
    for cp in copies:
        cp.start()
    for cp in copies:
        cp.wait()


def on_device(
    pressures, tap_area, tap_panel, tap_floor, panel_shape, floor_shape, mode_order, mode_decay, mode_freq
):
    nz, nc, ntm = lax.axis_size("taps"), lax.axis_size("floors"), lax.axis_size("tm")
    owners = nz * nc
    time_dev, taps = pressures.shape
    panels, modes = panel_shape.shape
    floors = floor_shape.shape[0]
    rows = panels + floors
    splits = 2
    th = time_dev // nc
    md, fd = modes // owners, floors // owners
    nch = th // LANES * splits
    xrows = md + -(-fd // 8) * 8
    vmem = pl.BlockSpec(memory_space=pltpu.VMEM)
    dma = pltpu.SemaphoreType.DMA
    f32 = jnp.float32
    tb, nb = th // LANES, time_dev // LANES
    inputs = [
        pltpu.VMEM((taps // LANES, LANES), jnp.bfloat16),
        pltpu.VMEM((1, taps), jnp.int32),
        pltpu.VMEM((1, taps), jnp.int32),
        pltpu.VMEM(panel_shape.shape, jnp.bfloat16),
        pltpu.VMEM(floor_shape.shape, jnp.bfloat16),
        pltpu.VMEM((1, modes), jnp.int32),
        pltpu.VMEM((1, modes), f32),
        pltpu.VMEM((1, modes), f32),
        pltpu.VMEM((modes, LANES), f32),
        pltpu.VMEM((time_dev, taps), jnp.bfloat16),
        pltpu.VMEM((rows, taps), jnp.bfloat16),
    ]
    response = [
        pltpu.VMEM((16, md, LANES), f32),
        pltpu.VMEM((nb, md, LANES), f32),
        pltpu.VMEM((nb, md, LANES), f32),
        pltpu.VMEM((md, LANES), f32),
        pltpu.VMEM((max(ntm - 1, 1), md, LANES), f32),
    ]
    if nz == 4 and nc == 2 and tb % 2 == 0:
        block = pltpu.VMEM((tb, rows, LANES), f32)
        pieces = ((0, 1), (1, 1)) + tuple((b, 2) for b in range(2, tb, 2))
        body = functools.partial(two_stage, (nz, nc, ntm, pieces))
        scratch = (
            inputs
            + [pltpu.VMEM((modes, panels), jnp.bfloat16), block, block, block]
            + [
                pltpu.VMEM((tb, panels, LANES), f32),
                pltpu.VMEM((tb, 2 * nc, md, LANES), f32),
                pltpu.VMEM((tb, nc, md, LANES), f32),
                pltpu.VMEM((tb, nc, md, LANES), f32),
                pltpu.VMEM((tb, nc, md, LANES), f32),
                pltpu.VMEM((tb, md, LANES), f32),
                pltpu.VMEM((nb, md, LANES), f32),
            ]
            + response[:3]
            + [pltpu.VMEM((nb, 2, md, LANES), f32)]
            + response[3:]
            + [
                pltpu.VMEM((owners, fd, th), f32),
                pltpu.VMEM((owners - 1, fd, th), f32),
                pltpu.VMEM((owners, fd, time_dev), f32),
                pltpu.VMEM((owners - 1, fd, time_dev), f32),
                pltpu.VMEM((max(ntm - 1, 1), owners, fd, time_dev), f32),
                pltpu.VMEM((max(ntm - 1, 1), owners, fd, time_dev), f32),
                dma((8,)), dma((2 * len(pieces),)),
                dma(()), dma((tb,)), dma(()), dma((tb,)), dma(()), dma((tb,)), dma(()), dma((tb,)),
                dma(()), dma((tb,)), dma(()), dma(()), dma((ntm,)), dma((ntm,)), dma(()), dma(()),
                dma((ntm,)), dma((ntm,)),
                pltpu.SemaphoreType.REGULAR,
            ]
        )
    else:
        chunk = pltpu.VMEM((nch, rows // splits, LANES), f32)
        body = functools.partial(kernel, (nz, nc, ntm, splits))
        scratch = (
            inputs
            + [chunk] * 7
            + [pltpu.VMEM((tb, xrows, LANES), f32), pltpu.VMEM((nb, xrows, LANES), f32)]
            + response
            + [
                pltpu.VMEM((owners, fd, time_dev), f32),
                pltpu.VMEM((owners, fd, time_dev), f32),
                dma((8,)),
                dma((2 * (th // min(256, th)),)),
                dma((nch,)), dma((nch,)), dma((nch,)), dma((nch,)), dma((nch,)), dma((nch,)),
                dma((tb,)), dma((tb,)),
                dma((ntm,)), dma((ntm,)),
                dma((owners,)), dma((owners,)),
            ]
        )
    out = pl.pallas_call(
        body,
        out_shape=(
            pltpu.VMEM((md, time_dev), f32),
            pltpu.VMEM((fd, time_dev), f32),
            pltpu.VMEM((fd, time_dev), f32),
        ),
        in_specs=[pl.BlockSpec(memory_space=pltpu.HBM)] * 9,
        out_specs=(vmem,) * 3,
        scratch_shapes=scratch,
        compiler_params=pltpu.CompilerParams(
            collective_id=0, has_side_effects=True, vmem_limit_bytes=VMEM_LIMIT
        ),
    )(
        *(
            pltpu.with_memory_space_constraint(a, pltpu.HBM)
            for a in (
                pressures,
                tap_area.reshape(taps // LANES, LANES),
                tap_panel.reshape(1, taps),
                tap_floor.reshape(1, taps),
                panel_shape,
                floor_shape,
                mode_order.reshape(1, modes),
                mode_decay.reshape(1, modes),
                mode_freq.reshape(1, modes),
            )
        )
    )
    return pl.pallas_call(
        write_out,
        out_shape=tuple(jax.ShapeDtypeStruct(o.shape, o.dtype) for o in out),
        in_specs=[vmem] * 3,
        out_specs=(pl.BlockSpec(memory_space=pltpu.HBM),) * 3,
        scratch_shapes=[dma((3,))],
        compiler_params=pltpu.CompilerParams(vmem_limit_bytes=VMEM_LIMIT),
    )(*out)


def solution(mesh):
    own = P(("taps", "floors"))
    out_spec = P(("taps", "floors"), ("dirs", "tm"))
    return jax.shard_map(
        on_device,
        mesh=mesh,
        in_specs=(P(("dirs", "tm"), ("taps", "floors")), own, own, own, P(), P(), P(), P(), P()),
        out_specs=(out_spec, out_spec, out_spec),
        check_vma=False,
    )
```

```python
import functools

import jax
import jax.numpy as jnp
from jax import lax
from jax.experimental import pallas as pl
from jax.experimental.pallas import tpu as pltpu
from jax.sharding import PartitionSpec as P

MESH = pl.DeviceIdType.MESH
LANES = 128
LAG = 2
CUT = 2
VMEM_LIMIT = 32 * 1024 * 1024
NT = (((1,), (1,)), ((), ()))


def dot_nt(a, b):
    return lax.dot_general(a, b, NT, preferred_element_type=jnp.float32)


def dot_split(a, b):
    hi = b.astype(jnp.bfloat16)
    lo = (b - hi.astype(jnp.float32)).astype(jnp.bfloat16)
    return jnp.dot(a, hi, preferred_element_type=jnp.float32) + jnp.dot(
        a, lo, preferred_element_type=jnp.float32
    )


def kernel(
    cfg,
    p_hbm, area_h, panel_h, floor_h, shape_h, fshape_h, order_h, decay_h, freq_h,
    y_ref, fm_ref, fl_ref,
    area_ref, panel_ref, floor_ref, shape_ref, fshape_ref, order_ref, decay_ref, freq_ref, order_col,
    pv, w_ref, mine, send_p, recv_p, rin, lin, rout, lout, xs, fb, tabs, loc, loc_im, st_send, st_recv,
    fs, fr,
    in_sem, p_sem, pp_s, pp_r, r_s, r_r, l_s, l_r, x_s, x_r, t_s, t_r, f_s, f_r,
):
    nz, nc, ntm, splits = cfg
    owners = nz * nc
    z = lax.axis_index("taps")
    c = lax.axis_index("floors")
    x = lax.axis_index("tm")
    me = z * nc + c
    other = nc - 1 - c
    time_dev, taps = pv.shape
    panels, modes = shape_ref.shape
    floors = fshape_ref.shape[0]
    rows = panels + floors
    th = time_dev // nc
    tblocks = th // LANES
    crows = rows // splits
    nch = tblocks * splits
    md = modes // owners
    fd = floors // owners
    f32 = jnp.float32
    bf16 = jnp.bfloat16

    small = [
        pltpu.make_async_copy(src, dst, in_sem.at[i])
        for i, (src, dst) in enumerate(
            (
                (area_h, area_ref), (panel_h, panel_ref), (floor_h, floor_ref), (shape_h, shape_ref),
                (fshape_h, fshape_ref), (order_h, order_ref), (decay_h, decay_ref), (freq_h, freq_ref),
            )
        )
    ]
    for cp in small:
        cp.start()

    barrier = pltpu.get_barrier_semaphore()

    def greet(k, carry):
        j = lax.rem(me + k, owners)
        pl.semaphore_signal(
            barrier, inc=1, device_id={"taps": j // nc, "floors": lax.rem(j, nc)}, device_id_type=MESH
        )
        return carry

    lax.fori_loop(1, owners, greet, 0)
    for k in range(1, ntm):
        pl.semaphore_signal(
            barrier, inc=1, device_id={"tm": lax.rem(x + k, ntm)}, device_id_type=MESH
        )

    step_t = min(256, th)
    per_half = th // step_t
    loads = []
    for h in range(2):
        half = other if h == 0 else c
        for b in range(per_half):
            off = pl.multiple_of(half * th + b * step_t, step_t)
            cp = pltpu.make_async_copy(
                p_hbm.at[pl.ds(off, step_t)], pv.at[pl.ds(off, step_t)], p_sem.at[h * per_half + b]
            )
            cp.start()
            loads.append((cp, off))

    for cp in small[:3]:
        cp.wait()
    ids = lax.broadcasted_iota(jnp.int32, (panels, LANES), 0)
    fids = lax.broadcasted_iota(jnp.int32, (floors, LANES), 0)
    area = area_ref[...].astype(f32)
    for r in range(taps // LANES):
        cols = slice(r * LANES, (r + 1) * LANES)
        row = area[r : r + 1, :]
        w_ref[0:panels, cols] = jnp.where(panel_ref[:, cols] == ids, row, 0.0).astype(bf16)
        w_ref[panels:rows, cols] = jnp.where(floor_ref[:, cols] == fids, row, 0.0).astype(bf16)

    def sums(b, h, dst):
        cp, off = loads[h * per_half + b]
        cp.wait()
        q = dot_nt(w_ref[...], pv[pl.ds(off, step_t), :])
        for i in range(step_t // LANES):
            for s in range(splits):
                dst[(b * step_t // LANES + i) * splits + s] = q[
                    s * crows : (s + 1) * crows, i * LANES : (i + 1) * LANES
                ]

    def pair_copy(k):
        return pltpu.make_async_remote_copy(
            src_ref=send_p.at[k], dst_ref=recv_p.at[k], send_sem=pp_s.at[k], recv_sem=pp_r.at[k],
            device_id={"floors": other}, device_id_type=MESH,
        )

    per_step = step_t // LANES * splits

    @pl.when(z == 0)
    def _():
        rin[...] = jnp.zeros_like(rin)

    @pl.when(z == nz - 1)
    def _():
        lin[...] = jnp.zeros_like(lin)

    def line_copy(k, right):
        src, dst, ss, rs = (rout, rin, r_s, r_r) if right else (lout, lin, l_s, l_r)
        to = jnp.minimum(z + 1, nz - 1) if right else jnp.maximum(z - 1, 0)
        return pltpu.make_async_remote_copy(
            src_ref=src.at[k], dst_ref=dst.at[k], send_sem=ss.at[k], recv_sem=rs.at[k],
            device_id={"taps": to}, device_id_type=MESH,
        )

    def line_step(s, carry):
        for right in (True, False):
            hop = z if right else nz - 1 - z
            k = s - LAG * hop
            came, out = (rin, rout) if right else (lin, lout)

            @pl.when(jnp.logical_and(k >= 0, k < nch))
            def _():
                @pl.when(hop > 0)
                def _():
                    line_copy(k, right).wait_recv()

                @pl.when(hop < nz - 1)
                def _():
                    out[k] = mine[k] + came[k]
                    line_copy(k, right).start()

        return carry

    def merge(b):
        for k in range(b * per_step, (b + 1) * per_step):
            pair_copy(k).wait_recv()
            mine[k] = mine[k] + recv_p[k]

    for b in range(per_half):
        sums(b, 0, send_p)
        if b == 0:
            pl.semaphore_wait(barrier, owners - 1 + ntm - 1)
        for k in range(b * per_step, (b + 1) * per_step):
            pair_copy(k).start()
        if b > 0:
            merge(b - 1)
        if b == 1:
            lax.fori_loop(0, min(LAG, per_step), line_step, 0)
        sums(b, 1, mine)
    merge(per_half - 1)
    first = min(LAG, per_step) if per_half > 1 else 0
    early = min(LAG, nch)
    lax.fori_loop(first, early, line_step, 0)

    for cp in small[3:]:
        cp.wait()
    order_col[...] = jnp.transpose(jnp.broadcast_to(order_ref[...].astype(f32), (LANES, modes)))
    mode_ids = lax.broadcasted_iota(jnp.int32, (md, modes), 1).astype(f32)

    def pick(owner):
        return order_col[pl.ds(pl.multiple_of(owner * md, md), md), 0:1] == mode_ids

    def shapes(hot):
        return dot_nt(hot.astype(f32).astype(bf16), shape_ref[...]).astype(bf16)

    hot_me = pick(me)
    hot_other = pick(z * nc + other)
    g_both = jnp.concatenate([shapes(hot_other), shapes(hot_me)], axis=0)
    d = jnp.sum(jnp.where(hot_me, decay_ref[...], 0.0), axis=1, keepdims=True)
    w = jnp.sum(jnp.where(hot_me, freq_ref[...], 0.0), axis=1, keepdims=True)
    ls = dot_nt(fshape_ref[...], hot_me.astype(f32).astype(bf16)).astype(bf16)
    e2 = 2.0 * d
    poly = jnp.full_like(e2, 1.0 / 40320.0)
    for coef in (1.0 / 5040, 1.0 / 720, 1.0 / 120, 1.0 / 24, 1.0 / 6, 0.5, 1.0):
        poly = coef - e2 * poly
    gain = jnp.sqrt(e2 * poly)
    lane = lax.broadcasted_iota(jnp.int32, (md, LANES), 1)
    ahead = (lane + 1).astype(f32)
    mag = jnp.exp(-d * ahead)
    t_re = mag * jnp.cos(w * ahead)
    t_im = mag * jnp.sin(w * ahead)
    tabs[0] = t_re
    tabs[1] = t_im
    hops = []
    step = 1
    while step < LANES:
        i = 2 + 2 * len(hops)
        tabs[i] = jnp.where(lane >= step, t_re[:, step - 1 : step], 0.0)
        tabs[i + 1] = jnp.where(lane >= step, t_im[:, step - 1 : step], 0.0)
        hops.append(step)
        step *= 2

    floor_row = lax.broadcasted_iota(jnp.int32, (floors, LANES), 0)

    def load_row(q, row):
        return jnp.sum(jnp.where(floor_row == row, q, 0.0), axis=0, keepdims=True)

    def exchange(tb):
        return pltpu.make_async_remote_copy(
            src_ref=xs.at[tb], dst_ref=fb.at[c * tblocks + tb],
            send_sem=x_s.at[tb], recv_sem=x_r.at[tb],
            device_id={"floors": other}, device_id_type=MESH,
        )

    def forces(tb):
        q = jnp.concatenate(
            [mine[k] + rin[k] + lin[k] for k in range(tb * splits, (tb + 1) * splits)], axis=0
        )
        both = dot_split(g_both, q[:panels])
        blk = c * tblocks + tb
        pad = [jnp.zeros((xs.shape[1] - md - fd, LANES), f32)] if xs.shape[1] > md + fd else []
        theirs = [load_row(q[panels:], (z * nc + other) * fd + r) for r in range(fd)]
        ours = [load_row(q[panels:], me * fd + r) for r in range(fd)]
        xs[tb] = jnp.concatenate([both[:md]] + theirs + pad, axis=0)
        exchange(tb).start()
        fb[blk] = jnp.concatenate([both[md:]] + ours + pad, axis=0)

    def at_rest(blk):
        re = gain * fb[blk, 0:md, :]
        im = None
        for i, step in enumerate(hops):
            a, b = tabs[2 + 2 * i], tabs[3 + 2 * i]
            rr = pltpu.roll(re, step, 1)
            if im is None:
                re, im = re + a * rr, b * rr
            else:
                ri = pltpu.roll(im, step, 1)
                re, im = re + a * rr - b * ri, im + a * ri + b * rr
        loc[blk] = re
        loc_im[blk] = im

    done = early
    for tb in range(tblocks):
        upto = (tb + 1) * splits + LAG * (nz - 1)
        lax.fori_loop(done, upto, line_step, 0)
        done = upto
        forces(tb)
        at_rest(c * tblocks + tb)
        if tb > 0:
            exchange(tb - 1).wait_recv()
            at_rest(other * tblocks + tb - 1)
    exchange(tblocks - 1).wait_recv()
    at_rest(other * tblocks + tblocks - 1)
    nb = time_dev // LANES
    end_re = [loc[blk][:, LANES - 1 :] for blk in range(nb)]
    end_im = [loc_im[blk][:, LANES - 1 :] for blk in range(nb)]

    zb_re, zb_im = t_re[:, LANES - 1 :], t_im[:, LANES - 1 :]
    s_re, s_im = end_re[0], end_im[0]
    for blk in range(1, nb):
        s_re, s_im = (
            zb_re * s_re - zb_im * s_im + end_re[blk],
            zb_im * s_re + zb_re * s_im + end_im[blk],
        )

    def state_copy(to, src):
        return pltpu.make_async_remote_copy(
            src_ref=st_send, dst_ref=st_recv.at[src], send_sem=t_s.at[to], recv_sem=t_r.at[src],
            device_id={"tm": to}, device_id_type=MESH,
        )

    st_send[...] = jnp.where(lane == 0, s_re, s_im)
    in_re = jnp.zeros((md, 1), f32)
    in_im = jnp.zeros((md, 1), f32)
    if ntm > 1:
        for to in range(1, ntm):

            @pl.when(x < to)
            def _():
                state_copy(to, jnp.minimum(x, ntm - 2)).start()

        for src in range(ntm - 1):

            @pl.when(x > src)
            def _():
                state_copy(lax.rem(x + 1, ntm), src).wait_recv()

            @pl.when(x <= src)
            def _():
                st_recv[src] = jnp.zeros_like(st_send)

            got_re, got_im = st_recv[src][:, 0:1], st_recv[src][:, 1:2]
            if ntm == 2:
                in_re, in_im = got_re, got_im
                continue
            length = (jnp.maximum(x - 1 - src, 0) * time_dev).astype(f32)
            pm = jnp.exp(-d * length)
            pr, pi = pm * jnp.cos(w * length), pm * jnp.sin(w * length)
            in_re = in_re + pr * got_re - pi * got_im
            in_im = in_im + pi * got_re + pr * got_im

    t_re, t_im = tabs[0], tabs[1]
    for blk in range(nb):
        y = loc[blk] + t_re * in_re - t_im * in_im
        cols = slice(blk * LANES, (blk + 1) * LANES)
        y_ref[:, cols] = y
        in_re, in_im = (
            zb_re * in_re - zb_im * in_im + end_re[blk],
            zb_im * in_re + zb_re * in_im + end_im[blk],
        )
    part = dot_split(ls, y_ref[...])
    for j in range(owners):
        fs[j] = part[j * fd : (j + 1) * fd]

    def motion_copy(k):
        j = lax.rem(me + k, owners)
        return pltpu.make_async_remote_copy(
            src_ref=fs.at[j], dst_ref=fr.at[me], send_sem=f_s.at[k], recv_sem=f_r.at[k],
            device_id={"taps": j // nc, "floors": lax.rem(j, nc)}, device_id_type=MESH,
        )

    def motion_start(k, carry):
        motion_copy(k).start()
        return carry

    def motion_recv(k, total):
        motion_copy(k).wait_recv()
        return total + fr[lax.rem(me + owners - k, owners)]

    def motion_sent(k, carry):
        motion_copy(k).wait_send()
        return carry

    lax.fori_loop(1, owners, motion_start, 0)
    load_scale = (floors / (taps * owners)) ** 0.5
    for blk in range(nb):
        fl_ref[:, blk * LANES : (blk + 1) * LANES] = fb[blk, md : md + fd, :] * load_scale

    for k in range(nch):
        pair_copy(k).wait_send()

    def line_sent(k, carry):
        @pl.when(z < nz - 1)
        def _():
            line_copy(k, True).wait_send()

        @pl.when(z > 0)
        def _():
            line_copy(k, False).wait_send()

        return carry

    lax.fori_loop(0, nch, line_sent, 0)
    for tb in range(tblocks):
        exchange(tb).wait_send()
    for to in range(1, ntm):

        @pl.when(x < to)
        def _():
            state_copy(to, jnp.minimum(x, ntm - 2)).wait_send()

    fm_ref[...] = lax.fori_loop(1, owners, motion_recv, fs[me])
    lax.fori_loop(1, owners, motion_sent, 0)


def two_stage(
    cfg,
    p_hbm, area_h, panel_h, floor_h, shape_h, fshape_h, order_h, decay_h, freq_h,
    y_ref, fm_ref, fl_ref,
    area_ref, panel_ref, floor_ref, shape_ref, fshape_ref, order_ref, decay_ref, freq_ref, order_col,
    pv, w_ref, g_ref, send_p, recv_p, mine, mp, up, sx, fx, si, fi, sp, fb, tabs, loc, loc_im, ends, st_send, st_recv,
    fls, flr, fs, fr, cs, cr,
    in_sem, p_sem, pp_s, pp_r, u_s, u_r, x_s, x_r, i_s, i_r, e_s, e_r, fl_s, fl_r, t_s, t_r, f_s, f_r, c_s, c_r, known,
):
    nz, nc, ntm, cut = cfg
    owners = nz * nc
    z = lax.axis_index("taps")
    c = lax.axis_index("floors")
    x = lax.axis_index("tm")
    me = z * nc + c
    other = nc - 1 - c
    side = z // 2
    mate = z + 1 - 2 * lax.rem(z, 2)
    far = nz - 1 - z
    inner = jnp.logical_or(z == 1, z == 2)
    time_dev = y_ref.shape[1]
    taps = w_ref.shape[1]
    panels, modes = shape_ref.shape
    floors = fshape_ref.shape[0]
    rows = panels + floors
    th = time_dev // nc
    tblocks = th // LANES
    md = modes // owners
    fd = floors // owners
    f32 = jnp.float32
    bf16 = jnp.bfloat16

    small = [
        pltpu.make_async_copy(src, dst, in_sem.at[i])
        for i, (src, dst) in enumerate(
            (
                (area_h, area_ref), (panel_h, panel_ref), (floor_h, floor_ref), (shape_h, shape_ref),
                (fshape_h, fshape_ref), (order_h, order_ref), (decay_h, decay_ref), (freq_h, freq_ref),
            )
        )
    ]
    for cp in small[:3]:
        cp.start()
    for k in range(tblocks):
        for h, half in enumerate((other, c)):
            off = pl.multiple_of(half * th + k * LANES, LANES)
            pltpu.make_async_copy(
                p_hbm.at[pl.ds(off, LANES)],
                pv.at[k, pl.ds(h * LANES, LANES)],
                p_sem.at[k + 1 if k + h else 0],
            ).start()
    for cp in small[3:]:
        cp.start()

    barrier = pltpu.get_barrier_semaphore()

    def greet(**to):
        pl.semaphore_signal(barrier, inc=1, device_id=to, device_id_type=MESH)

    greet(floors=other)
    greet(taps=mate)
    for k in range(1, ntm):
        greet(tm=lax.rem(x + k, ntm))

    @pl.when(inner)
    def _():
        greet(taps=far)

    for cp in small[:3]:
        cp.wait()
    ids = lax.broadcasted_iota(jnp.int32, (panels, LANES), 0)
    fids = lax.broadcasted_iota(jnp.int32, (floors, LANES), 0)
    area = area_ref[...].astype(f32)
    for r in range(taps // LANES):
        cols = slice(r * LANES, (r + 1) * LANES)
        row = area[r : r + 1, :]
        w_ref[0:panels, cols] = jnp.where(panel_ref[:, cols] == ids, row, 0.0).astype(bf16)
        w_ref[panels:rows, cols] = jnp.where(floor_ref[:, cols] == fids, row, 0.0).astype(bf16)

    def sums(k):
        loaded(pv.at[k], k + 1)
        q = dot_nt(w_ref[...], pv[k])
        send_p[k] = q[:, :LANES]
        mine[k] = q[:, LANES:]

    def loaded(ref, i):
        pltpu.make_async_copy(ref, ref, p_sem.at[i]).wait()

    def pair_copy(k):
        return pltpu.make_async_remote_copy(
            src_ref=send_p.at[k], dst_ref=recv_p.at[k], send_sem=pp_s, recv_sem=pp_r.at[k],
            device_id={"floors": other}, device_id_type=MESH,
        )

    def up_copy(i):
        return pltpu.make_async_remote_copy(
            src_ref=mp.at[i], dst_ref=up.at[i], send_sem=u_s, recv_sem=u_r.at[i],
            device_id={"taps": mate}, device_id_type=MESH,
        )

    width = LANES // cut

    def moved(v, groups):
        shift = groups * width % LANES
        return pltpu.roll(v, shift, 1) if shift else v

    def packed(parts, j):
        group = lax.broadcasted_iota(jnp.int32, parts[0].shape, 1) // width
        out = moved(parts[0], -j)
        for g in range(1, cut):
            out = jnp.where(group == g, moved(parts[g], g - j), out)
        return out

    def split(v):
        n = v.shape[0] // cut
        return [v[g * n : (g + 1) * n] for g in range(cut)]

    def merge(k):
        pair_copy(k).wait_recv()
        total = mine[k] + recv_p[k]
        mine[k] = total
        for j in range(cut):
            mp[k * cut + j] = packed(split(total[:panels]), j)

            @pl.when(jnp.logical_not(inner))
            def _():
                up_copy(k * cut + j).start()

    def pick(off, n):
        mode_ids = lax.broadcasted_iota(jnp.int32, (n, modes), 1).astype(f32)
        return order_col[pl.ds(pl.multiple_of(off, n), n), 0:1] == mode_ids

    def prepare():
        for cp in small[3:]:
            cp.wait()
        order_col[...] = jnp.transpose(jnp.broadcast_to(order_ref[...].astype(f32), (LANES, modes)))

        n = modes // 2
        for r in range(2):
            hot = pick(r * n, n).astype(f32).astype(bf16)
            g_ref[r * n : (r + 1) * n] = dot_nt(hot, shape_ref[...]).astype(bf16)

    def project(chip, n, q):
        size = n * nc * md
        return dot_split(g_ref[pl.ds(pl.multiple_of(chip * nc * md, size), size), :], q)

    def mate_copy(k, i):
        return pltpu.make_async_remote_copy(
            src_ref=si.at[k, i], dst_ref=fi.at[k, c], send_sem=i_s, recv_sem=i_r.at[k],
            device_id={"taps": mate, "floors": i}, device_id_type=MESH,
        )

    def cross_copy(k, i):
        return pltpu.make_async_remote_copy(
            src_ref=sx.at[k, i], dst_ref=fx.at[k, c], send_sem=x_s, recv_sem=x_r.at[k],
            device_id={"taps": 2 * (1 - side) + i // nc, "floors": i % nc}, device_id_type=MESH,
        )

    def exchange(k):
        return pltpu.make_async_remote_copy(
            src_ref=sp.at[k], dst_ref=fb.at[c * tblocks + k], send_sem=e_s, recv_sem=e_r.at[k],
            device_id={"floors": other}, device_id_type=MESH,
        )

    def keep(k, both):
        both = both.reshape(nc, md, LANES)
        sp[k] = jnp.where(c == 0, both[1], both[0])
        exchange(k).start()
        fb[c * tblocks + k] = jnp.where(c == 0, both[0], both[1])

    def across(k):
        got = []
        for j in range(cut):
            n = k * cut + j
            up_copy(n).wait_recv()
            total = mp[n] + up[n]
            got.append(total)
            total = jnp.concatenate([moved(total, j - g) for g in range(cut)], axis=0)
            f = project(2 * (1 - side), 2, total).reshape(2 * nc, cut, md // cut, LANES)
            f = packed([f[:, g].reshape(2 * nc * md // cut, LANES) for g in range(cut)], j)
            sx[n] = f.reshape(2 * nc, md // cut, LANES)
            for i in range(2 * nc):
                cross_copy(n, i).start()
        keep(k, project(z, 1, jnp.concatenate([packed(got, g) for g in range(cut)], axis=0)))

    head = pl.ds(0, LANES)
    loaded(pv.at[0, head], 0)
    send_p[0] = dot_nt(w_ref[...], pv[0, head])

    @pl.when(inner)
    def _():
        pl.semaphore_wait(barrier, 3 + ntm - 1)

    @pl.when(jnp.logical_not(inner))
    def _():
        pl.semaphore_wait(barrier, 2 + ntm - 1)

    pair_copy(0).start()
    rest = pl.ds(LANES, LANES)
    loaded(pv.at[0, rest], 1)
    mine[0] = dot_nt(w_ref[...], pv[0, rest])
    merge(0)

    @pl.when(inner)
    def _():
        pl.semaphore_signal(known, inc=1, device_id={"taps": far}, device_id_type=MESH)

    prepare()

    def aside(k):
        si[k] = project(mate, 1, mine[k, 0:panels]).reshape(nc, md, LANES)
        for j in range(nc):
            mate_copy(k, j).start()

    for k in range(1, tblocks):
        sums(k)
        pair_copy(k).start()
        if k == 1:

            @pl.when(inner)
            def _():
                aside(0)

    @pl.when(inner)
    def _():
        for k in range(1, tblocks):
            if k == tblocks - 1:
                pl.semaphore_wait(known, 1)
                pl.semaphore_signal(known, inc=1, device_id={"taps": mate}, device_id_type=MESH)
                across(0)
            merge(k)
            aside(k)

    @pl.when(jnp.logical_not(inner))
    def _():
        for k in range(1, tblocks):
            merge(k)

    @pl.when(jnp.logical_not(inner))
    def _():
        for k in range(tblocks):
            keep(k, project(z, 1, mine[k, 0:panels]))

    for k in range(tblocks):
        part = mine[k, panels:rows]
        for j in range(owners):
            fls[j, :, k * LANES : (k + 1) * LANES] = part[j * fd : (j + 1) * fd]

    hot_me = pick(me * md, md)
    d = jnp.sum(jnp.where(hot_me, decay_ref[...], 0.0), axis=1, keepdims=True)
    w = jnp.sum(jnp.where(hot_me, freq_ref[...], 0.0), axis=1, keepdims=True)
    ls = dot_nt(fshape_ref[...], hot_me.astype(f32).astype(bf16)).astype(bf16)
    e2 = 2.0 * d
    poly = jnp.full_like(e2, 1.0 / 40320.0)
    for coef in (1.0 / 5040, 1.0 / 720, 1.0 / 120, 1.0 / 24, 1.0 / 6, 0.5, 1.0):
        poly = coef - e2 * poly
    gain = jnp.sqrt(e2 * poly)
    nb = time_dev // LANES
    lane = lax.broadcasted_iota(jnp.int32, (md, LANES), 1)
    steps = lane.astype(f32)
    cos, sin = jnp.cos(w * steps), jnp.sin(w * steps)
    grow = gain * jnp.exp(d * steps)
    decay = jnp.exp(-d * steps)
    t_re, t_im = decay * cos, decay * sin
    for i, table in enumerate((t_re, t_im, grow * cos, -grow * sin)):
        tabs[i] = table
    upto = lax.broadcasted_iota(jnp.int32, (LANES, 2 * LANES), 0) <= lax.broadcasted_iota(
        jnp.int32, (LANES, 2 * LANES), 1
    )
    upto = upto.astype(f32).astype(bf16)

    def times(a_re, a_im, b_re, b_im):
        return a_re * b_re - a_im * b_im, a_re * b_im + a_im * b_re

    def wide(v):
        return jnp.broadcast_to(v, (md, LANES))

    last = LANES - 1
    for i, table in enumerate(
        times(t_re[:, 1:2], t_im[:, 1:2], t_re[:, last:], t_im[:, last:])
    ):
        tabs[4 + i] = wide(table)

    def turn(re, im):
        return times(tabs[4], tabs[5], re, im)

    @pl.when(inner)
    def _():
        for k in range(1, tblocks):
            across(k)

    @pl.when(jnp.logical_not(inner))
    def _():
        pl.semaphore_wait(known, 1)

    def load_copy(k):
        j = lax.rem(me + k, owners)
        return pltpu.make_async_remote_copy(
            src_ref=fls.at[j], dst_ref=flr.at[k - 1], send_sem=fl_s, recv_sem=fl_r,
            device_id={"taps": j // nc, "floors": lax.rem(j, nc)}, device_id_type=MESH,
        )

    def load_start(k, carry):
        load_copy(k).start()
        return carry

    lax.fori_loop(1, owners, load_start, 0)

    def prefix(blks):
        parts = [fb[blk] * tabs[2 + i] for blk in blks for i in range(2)]
        v = jnp.concatenate(parts, axis=0)
        hi = v.astype(bf16)
        lo = (v - hi.astype(f32)).astype(bf16)
        v = jnp.dot(hi, upto, preferred_element_type=f32) + jnp.dot(
            lo, upto, preferred_element_type=f32
        )
        for n, blk in enumerate(blks):
            for i, dst in enumerate((loc, loc_im)):
                part = v[(2 * n + i) * md : (2 * n + i + 1) * md]
                dst[blk] = part[:, :LANES]
                ends[blk, i] = part[:, LANES:]

    def response(blk, re, im):
        return tabs[0] * (loc[blk] + re) - tabs[1] * (loc_im[blk] + im)

    def state_copy(to, src):
        return pltpu.make_async_remote_copy(
            src_ref=st_send, dst_ref=st_recv.at[src], send_sem=t_s.at[to], recv_sem=t_r.at[src],
            device_id={"tm": to}, device_id_type=MESH,
        )

    def carry_copy(to, src, j):
        return pltpu.make_async_remote_copy(
            src_ref=cs.at[to - 1, j], dst_ref=cr.at[src, me], send_sem=c_s.at[to], recv_sem=c_r.at[src],
            device_id={"tm": to, "taps": j // nc, "floors": j % nc}, device_id_type=MESH,
        )

    for k in range(tblocks):
        exchange(k).wait_recv()

        @pl.when(jnp.logical_not(inner))
        def _():
            pltpu.make_async_copy(fi.at[k], fi.at[k], i_r.at[k]).wait()
            for h in range(nc):
                fb[h * tblocks + k] = fb[h * tblocks + k] + fi[k, h]

        for n in range(k * cut, (k + 1) * cut):
            pltpu.make_async_copy(fx.at[n], fx.at[n], x_r.at[n]).wait()
        for h in range(nc):
            parts = [fx[k * cut + j, h] for j in range(cut)]
            come = jnp.concatenate([packed(parts, g) for g in range(cut)], axis=0)
            fb[h * tblocks + k] = fb[h * tblocks + k] + come
        prefix([h * tblocks + k for h in range(nc)])

    re, im = jnp.zeros((md, LANES), f32), jnp.zeros((md, LANES), f32)
    ys = []
    for blk in range(nb):
        ys.append(response(blk, re, im))
        re, im = turn(ends[blk, 0] + re, ends[blk, 1] + im)
    y = jnp.concatenate(ys, axis=1)
    y_ref[...] = y
    part = dot_split(ls, y)
    for j in range(owners):
        fs[j] = part[j * fd : (j + 1) * fd]

    def motion_copy(k):
        j = lax.rem(me + k, owners)
        return pltpu.make_async_remote_copy(
            src_ref=fs.at[j], dst_ref=fr.at[k - 1], send_sem=f_s, recv_sem=f_r,
            device_id={"taps": j // nc, "floors": lax.rem(j, nc)}, device_id_type=MESH,
        )

    def motion_start(k, carry):
        motion_copy(k).start()
        return carry

    lax.fori_loop(1, owners, motion_start, 0)
    s_re, s_im = re, im
    for to in range(1, ntm):

        @pl.when(x < to)
        def _():
            src = jnp.minimum(x, ntm - 2)
            re, im = s_re, s_im
            if ntm > 2:
                gap = ((to - 1 - x) * time_dev).astype(f32)
                pm = jnp.exp(-d * gap)
                re, im = times(pm * jnp.cos(w * gap), pm * jnp.sin(w * gap), re, im)
            ys = []
            for blk in range(nb):
                ys.append(tabs[0] * re - tabs[1] * im)
                re, im = turn(re, im)
            part = dot_split(ls, jnp.concatenate(ys, axis=1))
            for j in range(owners):
                cs[to - 1, j] = part[j * fd : (j + 1) * fd]
            for j in range(owners):
                carry_copy(to, src, j).start()
            st_send[...] = jnp.where(lane == 0, s_re, s_im)
            state_copy(to, src).start()

    in_re = jnp.zeros((md, LANES), f32)
    in_im = jnp.zeros((md, LANES), f32)
    for src in range(ntm - 1):

        @pl.when(x > src)
        def _():
            state_copy(lax.rem(x + 1, ntm), src).wait_recv()

        @pl.when(x <= src)
        def _():
            st_recv[src] = jnp.zeros_like(st_send)

        got_re, got_im = wide(st_recv[src][:, 0:1]), wide(st_recv[src][:, 1:2])
        if ntm == 2:
            in_re, in_im = got_re, got_im
            continue
        length = (jnp.maximum(x - 1 - src, 0) * time_dev).astype(f32)
        pm = jnp.exp(-d * length)
        got_re, got_im = times(pm * jnp.cos(w * length), pm * jnp.sin(w * length), got_re, got_im)
        in_re, in_im = in_re + got_re, in_im + got_im

    @pl.when(x > 0)
    def _():
        re, im = in_re, in_im
        for blk in range(nb):
            cols = slice(blk * LANES, (blk + 1) * LANES)
            y_ref[:, cols] = y_ref[:, cols] + tabs[0] * re - tabs[1] * im
            re, im = turn(re, im)

    def drain(ref, sem):
        pltpu.make_async_copy(ref, ref, sem).wait()

    drain(flr, fl_r)
    load_scale = (floors / (taps * owners)) ** 0.5
    halves = []
    for h in range(nc):
        total = jnp.where(c == h, fls[me], 0.0)
        for k in range(1, owners):
            src = lax.rem(me + owners - k, owners)
            total = total + jnp.where(lax.rem(src, nc) == h, flr[k - 1], 0.0)
        halves.append(total * load_scale)
    for h in range(nc):
        fl_ref[:, h * th : (h + 1) * th] = halves[h]

    drain(send_p, pp_s)

    @pl.when(inner)
    def _():
        drain(si, i_s)
        drain(sx, x_s)

    @pl.when(jnp.logical_not(inner))
    def _():
        drain(up, u_s)

    drain(sp, e_s)
    drain(flr, fl_s)
    for to in range(1, ntm):

        @pl.when(x < to)
        def _():
            state_copy(to, jnp.minimum(x, ntm - 2)).wait_send()

    drain(fr, f_r)
    total = fs[me]
    for k in range(1, owners):
        total = total + fr[k - 1]
    fm_ref[...] = total
    drain(fr, f_s)
    for src in range(ntm - 1):

        @pl.when(x > src)
        def _():
            drain(cr.at[src], c_r.at[src])
            carried = fm_ref[...]
            for j in range(owners):
                carried = carried + cr[src, j]
            fm_ref[...] = carried

    for to in range(1, ntm):

        @pl.when(x < to)
        def _():
            drain(cs.at[to - 1], c_s.at[to])


def write_out(y, fm, fl, y_out, fm_out, fl_out, sem):
    copies = [
        pltpu.make_async_copy(src, dst, sem.at[i])
        for i, (src, dst) in enumerate(((y, y_out), (fm, fm_out), (fl, fl_out)))
    ]
    for cp in copies:
        cp.start()
    for cp in copies:
        cp.wait()


def on_device(
    pressures, tap_area, tap_panel, tap_floor, panel_shape, floor_shape, mode_order, mode_decay, mode_freq
):
    nz, nc, ntm = lax.axis_size("taps"), lax.axis_size("floors"), lax.axis_size("tm")
    owners = nz * nc
    time_dev, taps = pressures.shape
    panels, modes = panel_shape.shape
    floors = floor_shape.shape[0]
    rows = panels + floors
    splits = 2
    th = time_dev // nc
    md, fd = modes // owners, floors // owners
    nch = th // LANES * splits
    xrows = md + -(-fd // 8) * 8
    vmem = pl.BlockSpec(memory_space=pltpu.VMEM)
    dma = pltpu.SemaphoreType.DMA
    f32 = jnp.float32
    tb, nb = th // LANES, time_dev // LANES
    inputs = [
        pltpu.VMEM((taps // LANES, LANES), jnp.bfloat16),
        pltpu.VMEM((1, taps), jnp.int32),
        pltpu.VMEM((1, taps), jnp.int32),
        pltpu.VMEM(panel_shape.shape, jnp.bfloat16),
        pltpu.VMEM(floor_shape.shape, jnp.bfloat16),
        pltpu.VMEM((1, modes), jnp.int32),
        pltpu.VMEM((1, modes), f32),
        pltpu.VMEM((1, modes), f32),
        pltpu.VMEM((modes, LANES), f32),
        pltpu.VMEM((time_dev, taps), jnp.bfloat16),
        pltpu.VMEM((rows, taps), jnp.bfloat16),
    ]
    response = [
        pltpu.VMEM((16, md, LANES), f32),
        pltpu.VMEM((nb, md, LANES), f32),
        pltpu.VMEM((nb, md, LANES), f32),
        pltpu.VMEM((md, LANES), f32),
        pltpu.VMEM((max(ntm - 1, 1), md, LANES), f32),
    ]
    if nz == 4 and nc == 2:
        block = pltpu.VMEM((tb, rows, LANES), f32)
        body = functools.partial(two_stage, (nz, nc, ntm, CUT))
        scratch = (
            inputs[:-2]
            + [pltpu.VMEM((tb, nc * LANES, taps), jnp.bfloat16), inputs[-1]]
            + [pltpu.VMEM((modes, panels), jnp.bfloat16), block, block, block]
            + [
                pltpu.VMEM((tb * CUT, panels // CUT, LANES), f32),
                pltpu.VMEM((tb * CUT, panels // CUT, LANES), f32),
                pltpu.VMEM((tb * CUT, 2 * nc, md // CUT, LANES), f32),
                pltpu.VMEM((tb * CUT, nc, md // CUT, LANES), f32),
                pltpu.VMEM((tb, nc, md, LANES), f32),
                pltpu.VMEM((tb, nc, md, LANES), f32),
                pltpu.VMEM((tb, md, LANES), f32),
                pltpu.VMEM((nb, md, LANES), f32),
            ]
            + response[:3]
            + [pltpu.VMEM((nb, 2, md, LANES), f32)]
            + response[3:]
            + [
                pltpu.VMEM((owners, fd, th), f32),
                pltpu.VMEM((owners - 1, fd, th), f32),
                pltpu.VMEM((owners, fd, time_dev), f32),
                pltpu.VMEM((owners - 1, fd, time_dev), f32),
                pltpu.VMEM((max(ntm - 1, 1), owners, fd, time_dev), f32),
                pltpu.VMEM((max(ntm - 1, 1), owners, fd, time_dev), f32),
                dma((8,)), dma((tb + 1,)),
                dma(()), dma((tb,)), dma(()), dma((tb * CUT,)), dma(()), dma((tb * CUT,)),
                dma(()), dma((tb,)),
                dma(()), dma((tb,)), dma(()), dma(()), dma((ntm,)), dma((ntm,)), dma(()), dma(()),
                dma((ntm,)), dma((ntm,)),
                pltpu.SemaphoreType.REGULAR,
            ]
        )
    else:
        chunk = pltpu.VMEM((nch, rows // splits, LANES), f32)
        body = functools.partial(kernel, (nz, nc, ntm, splits))
        scratch = (
            inputs
            + [chunk] * 7
            + [pltpu.VMEM((tb, xrows, LANES), f32), pltpu.VMEM((nb, xrows, LANES), f32)]
            + response
            + [
                pltpu.VMEM((owners, fd, time_dev), f32),
                pltpu.VMEM((owners, fd, time_dev), f32),
                dma((8,)),
                dma((2 * (th // min(256, th)),)),
                dma((nch,)), dma((nch,)), dma((nch,)), dma((nch,)), dma((nch,)), dma((nch,)),
                dma((tb,)), dma((tb,)),
                dma((ntm,)), dma((ntm,)),
                dma((owners,)), dma((owners,)),
            ]
        )
    out = pl.pallas_call(
        body,
        out_shape=(
            pltpu.VMEM((md, time_dev), f32),
            pltpu.VMEM((fd, time_dev), f32),
            pltpu.VMEM((fd, time_dev), f32),
        ),
        in_specs=[pl.BlockSpec(memory_space=pltpu.HBM)] * 9,
        out_specs=(vmem,) * 3,
        scratch_shapes=scratch,
        compiler_params=pltpu.CompilerParams(
            collective_id=0, has_side_effects=True, vmem_limit_bytes=VMEM_LIMIT
        ),
    )(
        *(
            pltpu.with_memory_space_constraint(a, pltpu.HBM)
            for a in (
                pressures,
                tap_area.reshape(taps // LANES, LANES),
                tap_panel.reshape(1, taps),
                tap_floor.reshape(1, taps),
                panel_shape,
                floor_shape,
                mode_order.reshape(1, modes),
                mode_decay.reshape(1, modes),
                mode_freq.reshape(1, modes),
            )
        )
    )
    return pl.pallas_call(
        write_out,
        out_shape=tuple(jax.ShapeDtypeStruct(o.shape, o.dtype) for o in out),
        in_specs=[vmem] * 3,
        out_specs=(pl.BlockSpec(memory_space=pltpu.HBM),) * 3,
        scratch_shapes=[dma((3,))],
        compiler_params=pltpu.CompilerParams(vmem_limit_bytes=VMEM_LIMIT),
    )(*out)


def solution(mesh):
    own = P(("taps", "floors"))
    out_spec = P(("taps", "floors"), ("dirs", "tm"))
    return jax.shard_map(
        on_device,
        mesh=mesh,
        in_specs=(P(("dirs", "tm"), ("taps", "floors")), own, own, own, P(), P(), P(), P(), P()),
        out_specs=(out_spec, out_spec, out_spec),
        check_vma=False,
    )
```

```python
import functools

import jax
import jax.numpy as jnp
from jax import lax
from jax.experimental import pallas as pl
from jax.experimental.pallas import tpu as pltpu
from jax.sharding import PartitionSpec as P

MESH = pl.DeviceIdType.MESH
LANES = 128
LAG = 2
CUT = 4
VMEM_LIMIT = 32 * 1024 * 1024
NT = (((1,), (1,)), ((), ()))


def dot_nt(a, b):
    return lax.dot_general(a, b, NT, preferred_element_type=jnp.float32)


def dot_split(a, b):
    hi = b.astype(jnp.bfloat16)
    lo = (b - hi.astype(jnp.float32)).astype(jnp.bfloat16)
    return jnp.dot(a, hi, preferred_element_type=jnp.float32) + jnp.dot(
        a, lo, preferred_element_type=jnp.float32
    )


def kernel(
    cfg,
    p_hbm, area_h, panel_h, floor_h, shape_h, fshape_h, order_h, decay_h, freq_h,
    y_ref, fm_ref, fl_ref,
    area_ref, panel_ref, floor_ref, shape_ref, fshape_ref, order_ref, decay_ref, freq_ref, order_col,
    pv, w_ref, mine, send_p, recv_p, rin, lin, rout, lout, xs, fb, tabs, loc, loc_im, st_send, st_recv,
    fs, fr,
    in_sem, p_sem, pp_s, pp_r, r_s, r_r, l_s, l_r, x_s, x_r, t_s, t_r, f_s, f_r,
):
    nz, nc, ntm, splits = cfg
    owners = nz * nc
    z = lax.axis_index("taps")
    c = lax.axis_index("floors")
    x = lax.axis_index("tm")
    me = z * nc + c
    other = nc - 1 - c
    time_dev, taps = pv.shape
    panels, modes = shape_ref.shape
    floors = fshape_ref.shape[0]
    rows = panels + floors
    th = time_dev // nc
    tblocks = th // LANES
    crows = rows // splits
    nch = tblocks * splits
    md = modes // owners
    fd = floors // owners
    f32 = jnp.float32
    bf16 = jnp.bfloat16

    small = [
        pltpu.make_async_copy(src, dst, in_sem.at[i])
        for i, (src, dst) in enumerate(
            (
                (area_h, area_ref), (panel_h, panel_ref), (floor_h, floor_ref), (shape_h, shape_ref),
                (fshape_h, fshape_ref), (order_h, order_ref), (decay_h, decay_ref), (freq_h, freq_ref),
            )
        )
    ]
    for cp in small:
        cp.start()

    barrier = pltpu.get_barrier_semaphore()

    def greet(k, carry):
        j = lax.rem(me + k, owners)
        pl.semaphore_signal(
            barrier, inc=1, device_id={"taps": j // nc, "floors": lax.rem(j, nc)}, device_id_type=MESH
        )
        return carry

    lax.fori_loop(1, owners, greet, 0)
    for k in range(1, ntm):
        pl.semaphore_signal(
            barrier, inc=1, device_id={"tm": lax.rem(x + k, ntm)}, device_id_type=MESH
        )

    step_t = min(256, th)
    per_half = th // step_t
    loads = []
    for h in range(2):
        half = other if h == 0 else c
        for b in range(per_half):
            off = pl.multiple_of(half * th + b * step_t, step_t)
            cp = pltpu.make_async_copy(
                p_hbm.at[pl.ds(off, step_t)], pv.at[pl.ds(off, step_t)], p_sem.at[h * per_half + b]
            )
            cp.start()
            loads.append((cp, off))

    for cp in small[:3]:
        cp.wait()
    ids = lax.broadcasted_iota(jnp.int32, (panels, LANES), 0)
    fids = lax.broadcasted_iota(jnp.int32, (floors, LANES), 0)
    area = area_ref[...].astype(f32)
    for r in range(taps // LANES):
        cols = slice(r * LANES, (r + 1) * LANES)
        row = area[r : r + 1, :]
        w_ref[0:panels, cols] = jnp.where(panel_ref[:, cols] == ids, row, 0.0).astype(bf16)
        w_ref[panels:rows, cols] = jnp.where(floor_ref[:, cols] == fids, row, 0.0).astype(bf16)

    def sums(b, h, dst):
        cp, off = loads[h * per_half + b]
        cp.wait()
        q = dot_nt(w_ref[...], pv[pl.ds(off, step_t), :])
        for i in range(step_t // LANES):
            for s in range(splits):
                dst[(b * step_t // LANES + i) * splits + s] = q[
                    s * crows : (s + 1) * crows, i * LANES : (i + 1) * LANES
                ]

    def pair_copy(k):
        return pltpu.make_async_remote_copy(
            src_ref=send_p.at[k], dst_ref=recv_p.at[k], send_sem=pp_s.at[k], recv_sem=pp_r.at[k],
            device_id={"floors": other}, device_id_type=MESH,
        )

    per_step = step_t // LANES * splits

    @pl.when(z == 0)
    def _():
        rin[...] = jnp.zeros_like(rin)

    @pl.when(z == nz - 1)
    def _():
        lin[...] = jnp.zeros_like(lin)

    def line_copy(k, right):
        src, dst, ss, rs = (rout, rin, r_s, r_r) if right else (lout, lin, l_s, l_r)
        to = jnp.minimum(z + 1, nz - 1) if right else jnp.maximum(z - 1, 0)
        return pltpu.make_async_remote_copy(
            src_ref=src.at[k], dst_ref=dst.at[k], send_sem=ss.at[k], recv_sem=rs.at[k],
            device_id={"taps": to}, device_id_type=MESH,
        )

    def line_step(s, carry):
        for right in (True, False):
            hop = z if right else nz - 1 - z
            k = s - LAG * hop
            came, out = (rin, rout) if right else (lin, lout)

            @pl.when(jnp.logical_and(k >= 0, k < nch))
            def _():
                @pl.when(hop > 0)
                def _():
                    line_copy(k, right).wait_recv()

                @pl.when(hop < nz - 1)
                def _():
                    out[k] = mine[k] + came[k]
                    line_copy(k, right).start()

        return carry

    def merge(b):
        for k in range(b * per_step, (b + 1) * per_step):
            pair_copy(k).wait_recv()
            mine[k] = mine[k] + recv_p[k]

    for b in range(per_half):
        sums(b, 0, send_p)
        if b == 0:
            pl.semaphore_wait(barrier, owners - 1 + ntm - 1)
        for k in range(b * per_step, (b + 1) * per_step):
            pair_copy(k).start()
        if b > 0:
            merge(b - 1)
        if b == 1:
            lax.fori_loop(0, min(LAG, per_step), line_step, 0)
        sums(b, 1, mine)
    merge(per_half - 1)
    first = min(LAG, per_step) if per_half > 1 else 0
    early = min(LAG, nch)
    lax.fori_loop(first, early, line_step, 0)

    for cp in small[3:]:
        cp.wait()
    order_col[...] = jnp.transpose(jnp.broadcast_to(order_ref[...].astype(f32), (LANES, modes)))
    mode_ids = lax.broadcasted_iota(jnp.int32, (md, modes), 1).astype(f32)

    def pick(owner):
        return order_col[pl.ds(pl.multiple_of(owner * md, md), md), 0:1] == mode_ids

    def shapes(hot):
        return dot_nt(hot.astype(f32).astype(bf16), shape_ref[...]).astype(bf16)

    hot_me = pick(me)
    hot_other = pick(z * nc + other)
    g_both = jnp.concatenate([shapes(hot_other), shapes(hot_me)], axis=0)
    d = jnp.sum(jnp.where(hot_me, decay_ref[...], 0.0), axis=1, keepdims=True)
    w = jnp.sum(jnp.where(hot_me, freq_ref[...], 0.0), axis=1, keepdims=True)
    ls = dot_nt(fshape_ref[...], hot_me.astype(f32).astype(bf16)).astype(bf16)
    e2 = 2.0 * d
    poly = jnp.full_like(e2, 1.0 / 40320.0)
    for coef in (1.0 / 5040, 1.0 / 720, 1.0 / 120, 1.0 / 24, 1.0 / 6, 0.5, 1.0):
        poly = coef - e2 * poly
    gain = jnp.sqrt(e2 * poly)
    lane = lax.broadcasted_iota(jnp.int32, (md, LANES), 1)
    ahead = (lane + 1).astype(f32)
    mag = jnp.exp(-d * ahead)
    t_re = mag * jnp.cos(w * ahead)
    t_im = mag * jnp.sin(w * ahead)
    tabs[0] = t_re
    tabs[1] = t_im
    hops = []
    step = 1
    while step < LANES:
        i = 2 + 2 * len(hops)
        tabs[i] = jnp.where(lane >= step, t_re[:, step - 1 : step], 0.0)
        tabs[i + 1] = jnp.where(lane >= step, t_im[:, step - 1 : step], 0.0)
        hops.append(step)
        step *= 2

    floor_row = lax.broadcasted_iota(jnp.int32, (floors, LANES), 0)

    def load_row(q, row):
        return jnp.sum(jnp.where(floor_row == row, q, 0.0), axis=0, keepdims=True)

    def exchange(tb):
        return pltpu.make_async_remote_copy(
            src_ref=xs.at[tb], dst_ref=fb.at[c * tblocks + tb],
            send_sem=x_s.at[tb], recv_sem=x_r.at[tb],
            device_id={"floors": other}, device_id_type=MESH,
        )

    def forces(tb):
        q = jnp.concatenate(
            [mine[k] + rin[k] + lin[k] for k in range(tb * splits, (tb + 1) * splits)], axis=0
        )
        both = dot_split(g_both, q[:panels])
        blk = c * tblocks + tb
        pad = [jnp.zeros((xs.shape[1] - md - fd, LANES), f32)] if xs.shape[1] > md + fd else []
        theirs = [load_row(q[panels:], (z * nc + other) * fd + r) for r in range(fd)]
        ours = [load_row(q[panels:], me * fd + r) for r in range(fd)]
        xs[tb] = jnp.concatenate([both[:md]] + theirs + pad, axis=0)
        exchange(tb).start()
        fb[blk] = jnp.concatenate([both[md:]] + ours + pad, axis=0)

    def at_rest(blk):
        re = gain * fb[blk, 0:md, :]
        im = None
        for i, step in enumerate(hops):
            a, b = tabs[2 + 2 * i], tabs[3 + 2 * i]
            rr = pltpu.roll(re, step, 1)
            if im is None:
                re, im = re + a * rr, b * rr
            else:
                ri = pltpu.roll(im, step, 1)
                re, im = re + a * rr - b * ri, im + a * ri + b * rr
        loc[blk] = re
        loc_im[blk] = im

    done = early
    for tb in range(tblocks):
        upto = (tb + 1) * splits + LAG * (nz - 1)
        lax.fori_loop(done, upto, line_step, 0)
        done = upto
        forces(tb)
        at_rest(c * tblocks + tb)
        if tb > 0:
            exchange(tb - 1).wait_recv()
            at_rest(other * tblocks + tb - 1)
    exchange(tblocks - 1).wait_recv()
    at_rest(other * tblocks + tblocks - 1)
    nb = time_dev // LANES
    end_re = [loc[blk][:, LANES - 1 :] for blk in range(nb)]
    end_im = [loc_im[blk][:, LANES - 1 :] for blk in range(nb)]

    zb_re, zb_im = t_re[:, LANES - 1 :], t_im[:, LANES - 1 :]
    s_re, s_im = end_re[0], end_im[0]
    for blk in range(1, nb):
        s_re, s_im = (
            zb_re * s_re - zb_im * s_im + end_re[blk],
            zb_im * s_re + zb_re * s_im + end_im[blk],
        )

    def state_copy(to, src):
        return pltpu.make_async_remote_copy(
            src_ref=st_send, dst_ref=st_recv.at[src], send_sem=t_s.at[to], recv_sem=t_r.at[src],
            device_id={"tm": to}, device_id_type=MESH,
        )

    st_send[...] = jnp.where(lane == 0, s_re, s_im)
    in_re = jnp.zeros((md, 1), f32)
    in_im = jnp.zeros((md, 1), f32)
    if ntm > 1:
        for to in range(1, ntm):

            @pl.when(x < to)
            def _():
                state_copy(to, jnp.minimum(x, ntm - 2)).start()

        for src in range(ntm - 1):

            @pl.when(x > src)
            def _():
                state_copy(lax.rem(x + 1, ntm), src).wait_recv()

            @pl.when(x <= src)
            def _():
                st_recv[src] = jnp.zeros_like(st_send)

            got_re, got_im = st_recv[src][:, 0:1], st_recv[src][:, 1:2]
            if ntm == 2:
                in_re, in_im = got_re, got_im
                continue
            length = (jnp.maximum(x - 1 - src, 0) * time_dev).astype(f32)
            pm = jnp.exp(-d * length)
            pr, pi = pm * jnp.cos(w * length), pm * jnp.sin(w * length)
            in_re = in_re + pr * got_re - pi * got_im
            in_im = in_im + pi * got_re + pr * got_im

    t_re, t_im = tabs[0], tabs[1]
    for blk in range(nb):
        y = loc[blk] + t_re * in_re - t_im * in_im
        cols = slice(blk * LANES, (blk + 1) * LANES)
        y_ref[:, cols] = y
        in_re, in_im = (
            zb_re * in_re - zb_im * in_im + end_re[blk],
            zb_im * in_re + zb_re * in_im + end_im[blk],
        )
    part = dot_split(ls, y_ref[...])
    for j in range(owners):
        fs[j] = part[j * fd : (j + 1) * fd]

    def motion_copy(k):
        j = lax.rem(me + k, owners)
        return pltpu.make_async_remote_copy(
            src_ref=fs.at[j], dst_ref=fr.at[me], send_sem=f_s.at[k], recv_sem=f_r.at[k],
            device_id={"taps": j // nc, "floors": lax.rem(j, nc)}, device_id_type=MESH,
        )

    def motion_start(k, carry):
        motion_copy(k).start()
        return carry

    def motion_recv(k, total):
        motion_copy(k).wait_recv()
        return total + fr[lax.rem(me + owners - k, owners)]

    def motion_sent(k, carry):
        motion_copy(k).wait_send()
        return carry

    lax.fori_loop(1, owners, motion_start, 0)
    load_scale = (floors / (taps * owners)) ** 0.5
    for blk in range(nb):
        fl_ref[:, blk * LANES : (blk + 1) * LANES] = fb[blk, md : md + fd, :] * load_scale

    for k in range(nch):
        pair_copy(k).wait_send()

    def line_sent(k, carry):
        @pl.when(z < nz - 1)
        def _():
            line_copy(k, True).wait_send()

        @pl.when(z > 0)
        def _():
            line_copy(k, False).wait_send()

        return carry

    lax.fori_loop(0, nch, line_sent, 0)
    for tb in range(tblocks):
        exchange(tb).wait_send()
    for to in range(1, ntm):

        @pl.when(x < to)
        def _():
            state_copy(to, jnp.minimum(x, ntm - 2)).wait_send()

    fm_ref[...] = lax.fori_loop(1, owners, motion_recv, fs[me])
    lax.fori_loop(1, owners, motion_sent, 0)


def two_stage(
    cfg,
    p_hbm, area_h, panel_h, floor_h, shape_h, fshape_h, order_h, decay_h, freq_h,
    y_ref, fm_ref, fl_ref,
    area_ref, panel_ref, floor_ref, shape_ref, fshape_ref, order_ref, decay_ref, freq_ref, order_col,
    pv, w_ref, g_ref, send_p, recv_p, mine, mp, up, sx, fx, si, fi, sp, fb, tabs, loc, loc_im, ends, st_send, st_recv,
    fls, flr, fs, fr, cs, cr,
    in_sem, p_sem, pp_r, u_r, x_r, i_r, e_r, fl_r, t_s, t_r, f_r, c_s, c_r, known,
):
    nz, nc, ntm, cut = cfg
    pp_s, u_s, i_s, x_s, e_s, fl_s, f_s = (in_sem.at[i] for i in range(7))
    owners = nz * nc
    z = lax.axis_index("taps")
    c = lax.axis_index("floors")
    x = lax.axis_index("tm")
    me = z * nc + c
    other = nc - 1 - c
    side = z // 2
    mate = z + 1 - 2 * lax.rem(z, 2)
    far = nz - 1 - z
    inner = jnp.logical_or(z == 1, z == 2)
    time_dev = y_ref.shape[1]
    taps = w_ref.shape[1]
    panels, modes = shape_ref.shape
    floors = fshape_ref.shape[0]
    rows = panels + floors
    th = time_dev // nc
    tblocks = th // LANES
    md = modes // owners
    fd = floors // owners
    f32 = jnp.float32
    bf16 = jnp.bfloat16

    small = [
        pltpu.make_async_copy(src, dst, in_sem.at[i])
        for i, (src, dst) in enumerate(
            (
                (area_h, area_ref), (panel_h, panel_ref), (floor_h, floor_ref), (shape_h, shape_ref),
                (fshape_h, fshape_ref), (order_h, order_ref), (decay_h, decay_ref), (freq_h, freq_ref),
            )
        )
    ]
    for cp in small[:3]:
        cp.start()
    for k in range(tblocks):
        for h, half in enumerate((other, c)):
            off = pl.multiple_of(half * th + k * LANES, LANES)
            pltpu.make_async_copy(
                p_hbm.at[pl.ds(off, LANES)],
                pv.at[k, pl.ds(h * LANES, LANES)],
                p_sem.at[k + 1 if k + h else 0],
            ).start()
    for cp in small[3:]:
        cp.start()

    barrier = pltpu.get_barrier_semaphore()

    def greet(**to):
        pl.semaphore_signal(barrier, inc=1, device_id=to, device_id_type=MESH)

    greet(floors=other)
    greet(taps=mate)
    for k in range(1, ntm):
        greet(tm=lax.rem(x + k, ntm))

    @pl.when(inner)
    def _():
        greet(taps=far)

    for cp in small[:3]:
        cp.wait()
    ids = lax.broadcasted_iota(jnp.int32, (panels, LANES), 0)
    fids = lax.broadcasted_iota(jnp.int32, (floors, LANES), 0)
    area = area_ref[...].astype(f32)
    def sums(k):
        loaded(pv.at[k], k + 1)
        q = dot_nt(w_ref[...], pv[k])
        send_p[k] = q[:, :LANES]
        mine[k] = q[:, LANES:]

    def loaded(ref, i):
        pltpu.make_async_copy(ref, ref, p_sem.at[i]).wait()

    def pair_copy(k):
        return pltpu.make_async_remote_copy(
            src_ref=send_p.at[k], dst_ref=recv_p.at[k], send_sem=pp_s, recv_sem=pp_r.at[k],
            device_id={"floors": other}, device_id_type=MESH,
        )

    def up_copy(i):
        return pltpu.make_async_remote_copy(
            src_ref=mp.at[i], dst_ref=up.at[i], send_sem=u_s, recv_sem=u_r.at[i],
            device_id={"taps": mate}, device_id_type=MESH,
        )

    width = LANES // cut

    def moved(v, groups):
        shift = groups * width % LANES
        return pltpu.roll(v, shift, 1) if shift else v

    def packed(parts, j):
        group = lax.broadcasted_iota(jnp.int32, parts[0].shape, 1) // width
        out = moved(parts[0], -j)
        for g in range(1, cut):
            out = jnp.where(group == g, moved(parts[g], g - j), out)
        return out

    def split(v):
        n = v.shape[0] // cut
        return [v[g * n : (g + 1) * n] for g in range(cut)]

    def merge(k):
        pair_copy(k).wait_recv()
        total = mine[k] + recv_p[k]
        mine[k] = total
        for j in range(cut):
            mp[k * cut + j] = packed(split(total[:panels]), j)

            @pl.when(jnp.logical_not(inner))
            def _():
                up_copy(k * cut + j).start()

    def pick(off, n):
        mode_ids = lax.broadcasted_iota(jnp.int32, (n, modes), 1).astype(f32)
        return order_col[pl.ds(pl.multiple_of(off, n), n), 0:1] == mode_ids

    def prepare():
        for cp in small[3:]:
            cp.wait()
        order_col[...] = jnp.transpose(jnp.broadcast_to(order_ref[...].astype(f32), (LANES, modes)))

        n = modes // 2
        for r in range(2):
            hot = pick(r * n, n).astype(f32).astype(bf16)
            g_ref[r * n : (r + 1) * n] = dot_nt(hot, shape_ref[...]).astype(bf16)

    def project(chip, n, q):
        size = n * nc * md
        return dot_split(g_ref[pl.ds(pl.multiple_of(chip * nc * md, size), size), :], q)

    def mate_copy(k, i):
        return pltpu.make_async_remote_copy(
            src_ref=si.at[k, i], dst_ref=fi.at[k, c], send_sem=i_s, recv_sem=i_r,
            device_id={"taps": mate, "floors": i}, device_id_type=MESH,
        )

    def cross_copy(k, i):
        chip = lax.rem(i // nc + 1 - side, 2)
        return pltpu.make_async_remote_copy(
            src_ref=sx.at[k, chip * nc + i % nc], dst_ref=fx.at[k // cut, k % cut, c],
            send_sem=x_s, recv_sem=x_r.at[k // cut],
            device_id={"taps": 2 * (1 - side) + chip, "floors": i % nc}, device_id_type=MESH,
        )

    def exchange(k):
        return pltpu.make_async_remote_copy(
            src_ref=sp.at[k], dst_ref=fb.at[c * tblocks + k], send_sem=e_s, recv_sem=e_r.at[k],
            device_id={"floors": other}, device_id_type=MESH,
        )

    def keep(k, both):
        both = both.reshape(nc, md, LANES)
        sp[k] = jnp.where(c == 0, both[1], both[0])
        exchange(k).start()
        fb[c * tblocks + k] = jnp.where(c == 0, both[0], both[1])

    def across(k):
        got = []
        for j in range(cut):
            n = k * cut + j
            up_copy(n).wait_recv()
            total = mp[n] + up[n]
            got.append(total)
            total = jnp.concatenate([moved(total, j - g) for g in range(cut)], axis=0)
            f = project(2 * (1 - side), 2, total).reshape(2 * nc, cut, md // cut, LANES)
            f = packed([f[:, g].reshape(2 * nc * md // cut, LANES) for g in range(cut)], j)
            sx[n] = f.reshape(2 * nc, md // cut, LANES)
            for i in range(2 * nc):
                cross_copy(n, i).start()
        keep(k, project(z, 1, jnp.concatenate([packed(got, g) for g in range(cut)], axis=0)))

    head = pl.ds(0, LANES)
    loaded(pv.at[0, head], 0)
    chunk = 4 * LANES
    first = jnp.zeros((rows, LANES), f32)
    for start in range(0, taps, chunk):
        for r in range(start // LANES, (start + chunk) // LANES):
            cols = slice(r * LANES, (r + 1) * LANES)
            row = area[r : r + 1, :]
            w_ref[0:panels, cols] = jnp.where(panel_ref[:, cols] == ids, row, 0.0).astype(bf16)
            w_ref[panels:rows, cols] = jnp.where(floor_ref[:, cols] == fids, row, 0.0).astype(bf16)
        cols = slice(start, start + chunk)
        first = first + dot_nt(w_ref[:, cols], pv[0, head, cols])
    send_p[0] = first

    @pl.when(inner)
    def _():
        pl.semaphore_wait(barrier, 3 + ntm - 1)

    @pl.when(jnp.logical_not(inner))
    def _():
        pl.semaphore_wait(barrier, 2 + ntm - 1)

    pair_copy(0).start()
    rest = pl.ds(LANES, LANES)
    loaded(pv.at[0, rest], 1)
    mine[0] = dot_nt(w_ref[...], pv[0, rest])
    merge(0)

    @pl.when(inner)
    def _():
        pl.semaphore_signal(known, inc=1, device_id={"taps": far}, device_id_type=MESH)

    prepare()

    def aside(k):
        si[k] = project(mate, 1, mine[k, 0:panels]).reshape(nc, md, LANES)
        for j in range(nc):
            mate_copy(k, j).start()

    for k in range(1, tblocks):
        sums(k)
        pair_copy(k).start()
        if k == 1:

            @pl.when(inner)
            def _():
                aside(0)

    @pl.when(inner)
    def _():
        for k in range(1, tblocks):
            if k == tblocks - 1:
                pl.semaphore_wait(known, 1)
                pl.semaphore_signal(known, inc=1, device_id={"taps": mate}, device_id_type=MESH)
                across(0)
            merge(k)
            aside(k)
        across(1)

    @pl.when(jnp.logical_not(inner))
    def _():
        for k in range(1, tblocks):
            merge(k)

    @pl.when(jnp.logical_not(inner))
    def _():
        for k in range(tblocks):
            keep(k, project(z, 1, mine[k, 0:panels]))

    for k in range(tblocks):
        part = mine[k, panels:rows]
        for j in range(owners):
            fls[j, :, k * LANES : (k + 1) * LANES] = part[j * fd : (j + 1) * fd]

    hot_me = pick(me * md, md)
    d = jnp.sum(jnp.where(hot_me, decay_ref[...], 0.0), axis=1, keepdims=True)
    w = jnp.sum(jnp.where(hot_me, freq_ref[...], 0.0), axis=1, keepdims=True)
    ls = dot_nt(fshape_ref[...], hot_me.astype(f32).astype(bf16)).astype(bf16)
    e2 = 2.0 * d
    poly = jnp.full_like(e2, 1.0 / 40320.0)
    for coef in (1.0 / 5040, 1.0 / 720, 1.0 / 120, 1.0 / 24, 1.0 / 6, 0.5, 1.0):
        poly = coef - e2 * poly
    gain = jnp.sqrt(e2 * poly)
    nb = time_dev // LANES
    lane = lax.broadcasted_iota(jnp.int32, (md, LANES), 1)
    steps = lane.astype(f32)
    cos, sin = jnp.cos(w * steps), jnp.sin(w * steps)
    grow = gain * jnp.exp(d * steps)
    decay = jnp.exp(-d * steps)
    t_re, t_im = decay * cos, decay * sin
    for i, table in enumerate((t_re, t_im, grow * cos, -grow * sin)):
        tabs[i] = table
    upto = lax.broadcasted_iota(jnp.int32, (LANES, 2 * LANES), 0) <= lax.broadcasted_iota(
        jnp.int32, (LANES, 2 * LANES), 1
    )
    upto = upto.astype(f32).astype(bf16)

    def times(a_re, a_im, b_re, b_im):
        return a_re * b_re - a_im * b_im, a_re * b_im + a_im * b_re

    def wide(v):
        return jnp.broadcast_to(v, (md, LANES))

    last = LANES - 1
    for i, table in enumerate(
        times(t_re[:, 1:2], t_im[:, 1:2], t_re[:, last:], t_im[:, last:])
    ):
        tabs[4 + i] = wide(table)

    def turn(re, im):
        return times(tabs[4], tabs[5], re, im)

    @pl.when(inner)
    def _():
        for k in range(2, tblocks):
            across(k)

    @pl.when(jnp.logical_not(inner))
    def _():
        pl.semaphore_wait(known, 1)

    def load_copy(k):
        j = lax.rem(me + k, owners)
        return pltpu.make_async_remote_copy(
            src_ref=fls.at[j], dst_ref=flr.at[k - 1], send_sem=fl_s, recv_sem=fl_r,
            device_id={"taps": j // nc, "floors": lax.rem(j, nc)}, device_id_type=MESH,
        )

    def load_start(k, carry):
        load_copy(k).start()
        return carry

    def prefix(blks):
        parts = [fb[blk] * tabs[2 + i] for blk in blks for i in range(2)]
        v = jnp.concatenate(parts, axis=0)
        hi = v.astype(bf16)
        lo = (v - hi.astype(f32)).astype(bf16)
        v = jnp.dot(hi, upto, preferred_element_type=f32) + jnp.dot(
            lo, upto, preferred_element_type=f32
        )
        for n, blk in enumerate(blks):
            for i, dst in enumerate((loc, loc_im)):
                part = v[(2 * n + i) * md : (2 * n + i + 1) * md]
                dst[blk] = part[:, :LANES]
                ends[blk, i] = part[:, LANES:]

    def response(blk, re, im):
        return tabs[0] * (loc[blk] + re) - tabs[1] * (loc_im[blk] + im)

    def state_copy(to, src):
        return pltpu.make_async_remote_copy(
            src_ref=st_send, dst_ref=st_recv.at[src], send_sem=t_s.at[to], recv_sem=t_r.at[src],
            device_id={"tm": to}, device_id_type=MESH,
        )

    def carry_copy(to, src, j):
        return pltpu.make_async_remote_copy(
            src_ref=cs.at[to - 1, j], dst_ref=cr.at[src, me], send_sem=c_s.at[to], recv_sem=c_r.at[src],
            device_id={"tm": to, "taps": j // nc, "floors": j % nc}, device_id_type=MESH,
        )

    @pl.when(jnp.logical_not(inner))
    def _():
        pltpu.make_async_copy(fi, fi, i_r).wait()

    for k in range(tblocks):
        exchange(k).wait_recv()

        @pl.when(jnp.logical_not(inner))
        def _():
            for h in range(nc):
                fb[h * tblocks + k] = fb[h * tblocks + k] + fi[k, h]

        pltpu.make_async_copy(fx.at[k], fx.at[k], x_r.at[k]).wait()
        for h in range(nc):
            parts = [fx[k, j, h] for j in range(cut)]
            come = jnp.concatenate([packed(parts, g) for g in range(cut)], axis=0)
            fb[h * tblocks + k] = fb[h * tblocks + k] + come
        prefix([h * tblocks + k for h in range(nc)])
        if k == tblocks - 2:
            lax.fori_loop(1, owners, load_start, 0)

    re, im = jnp.zeros((md, LANES), f32), jnp.zeros((md, LANES), f32)
    ys = []
    for blk in range(nb):
        ys.append(response(blk, re, im))
        re, im = turn(ends[blk, 0] + re, ends[blk, 1] + im)
    y = jnp.concatenate(ys, axis=1)
    y_ref[...] = y
    part = dot_split(ls, y)
    for j in range(owners):
        fs[j] = part[j * fd : (j + 1) * fd]

    def motion_copy(k):
        j = lax.rem(me + k, owners)
        return pltpu.make_async_remote_copy(
            src_ref=fs.at[j], dst_ref=fr.at[k - 1], send_sem=f_s, recv_sem=f_r,
            device_id={"taps": j // nc, "floors": lax.rem(j, nc)}, device_id_type=MESH,
        )

    def motion_start(k, carry):
        motion_copy(k).start()
        return carry

    lax.fori_loop(1, owners, motion_start, 0)
    s_re, s_im = re, im
    for to in range(1, ntm):

        @pl.when(x < to)
        def _():
            src = jnp.minimum(x, ntm - 2)
            re, im = s_re, s_im
            if ntm > 2:
                gap = ((to - 1 - x) * time_dev).astype(f32)
                pm = jnp.exp(-d * gap)
                re, im = times(pm * jnp.cos(w * gap), pm * jnp.sin(w * gap), re, im)
            ys = []
            for blk in range(nb):
                ys.append(tabs[0] * re - tabs[1] * im)
                re, im = turn(re, im)
            part = dot_split(ls, jnp.concatenate(ys, axis=1))
            for j in range(owners):
                cs[to - 1, j] = part[j * fd : (j + 1) * fd]
            for j in range(owners):
                carry_copy(to, src, j).start()
            st_send[...] = jnp.where(lane == 0, s_re, s_im)
            state_copy(to, src).start()

    in_re = jnp.zeros((md, LANES), f32)
    in_im = jnp.zeros((md, LANES), f32)
    for src in range(ntm - 1):

        @pl.when(x > src)
        def _():
            state_copy(lax.rem(x + 1, ntm), src).wait_recv()

        @pl.when(x <= src)
        def _():
            st_recv[src] = jnp.zeros_like(st_send)

        got_re, got_im = wide(st_recv[src][:, 0:1]), wide(st_recv[src][:, 1:2])
        if ntm == 2:
            in_re, in_im = got_re, got_im
            continue
        length = (jnp.maximum(x - 1 - src, 0) * time_dev).astype(f32)
        pm = jnp.exp(-d * length)
        got_re, got_im = times(pm * jnp.cos(w * length), pm * jnp.sin(w * length), got_re, got_im)
        in_re, in_im = in_re + got_re, in_im + got_im

    @pl.when(x > 0)
    def _():
        re, im = in_re, in_im
        for blk in range(nb):
            cols = slice(blk * LANES, (blk + 1) * LANES)
            y_ref[:, cols] = y_ref[:, cols] + tabs[0] * re - tabs[1] * im
            re, im = turn(re, im)

    def drain(ref, sem):
        pltpu.make_async_copy(ref, ref, sem).wait()

    drain(flr, fl_r)
    load_scale = (floors / (taps * owners)) ** 0.5
    halves = []
    for h in range(nc):
        total = jnp.where(c == h, fls[me], 0.0)
        for k in range(1, owners):
            src = lax.rem(me + owners - k, owners)
            total = total + jnp.where(lax.rem(src, nc) == h, flr[k - 1], 0.0)
        halves.append(total * load_scale)
    for h in range(nc):
        fl_ref[:, h * th : (h + 1) * th] = halves[h]

    drain(send_p, pp_s)

    @pl.when(inner)
    def _():
        drain(si, i_s)
        drain(sx, x_s)

    @pl.when(jnp.logical_not(inner))
    def _():
        drain(up, u_s)

    drain(sp, e_s)
    drain(flr, fl_s)
    for to in range(1, ntm):

        @pl.when(x < to)
        def _():
            state_copy(to, jnp.minimum(x, ntm - 2)).wait_send()

    drain(fr, f_r)
    total = fs[me]
    for k in range(1, owners):
        total = total + fr[k - 1]
    fm_ref[...] = total
    drain(fr, f_s)
    for src in range(ntm - 1):

        @pl.when(x > src)
        def _():
            drain(cr.at[src], c_r.at[src])
            carried = fm_ref[...]
            for j in range(owners):
                carried = carried + cr[src, j]
            fm_ref[...] = carried

    for to in range(1, ntm):

        @pl.when(x < to)
        def _():
            drain(cs.at[to - 1], c_s.at[to])


def write_out(y, fm, fl, y_out, fm_out, fl_out, sem):
    copies = [
        pltpu.make_async_copy(src, dst, sem.at[i])
        for i, (src, dst) in enumerate(((y, y_out), (fm, fm_out), (fl, fl_out)))
    ]
    for cp in copies:
        cp.start()
    for cp in copies:
        cp.wait()


def on_device(
    pressures, tap_area, tap_panel, tap_floor, panel_shape, floor_shape, mode_order, mode_decay, mode_freq
):
    nz, nc, ntm = lax.axis_size("taps"), lax.axis_size("floors"), lax.axis_size("tm")
    owners = nz * nc
    time_dev, taps = pressures.shape
    panels, modes = panel_shape.shape
    floors = floor_shape.shape[0]
    rows = panels + floors
    splits = 2
    th = time_dev // nc
    md, fd = modes // owners, floors // owners
    nch = th // LANES * splits
    xrows = md + -(-fd // 8) * 8
    vmem = pl.BlockSpec(memory_space=pltpu.VMEM)
    dma = pltpu.SemaphoreType.DMA
    f32 = jnp.float32
    tb, nb = th // LANES, time_dev // LANES
    inputs = [
        pltpu.VMEM((taps // LANES, LANES), jnp.bfloat16),
        pltpu.VMEM((1, taps), jnp.int32),
        pltpu.VMEM((1, taps), jnp.int32),
        pltpu.VMEM(panel_shape.shape, jnp.bfloat16),
        pltpu.VMEM(floor_shape.shape, jnp.bfloat16),
        pltpu.VMEM((1, modes), jnp.int32),
        pltpu.VMEM((1, modes), f32),
        pltpu.VMEM((1, modes), f32),
        pltpu.VMEM((modes, LANES), f32),
        pltpu.VMEM((time_dev, taps), jnp.bfloat16),
        pltpu.VMEM((rows, taps), jnp.bfloat16),
    ]
    response = [
        pltpu.VMEM((16, md, LANES), f32),
        pltpu.VMEM((nb, md, LANES), f32),
        pltpu.VMEM((nb, md, LANES), f32),
        pltpu.VMEM((md, LANES), f32),
        pltpu.VMEM((max(ntm - 1, 1), md, LANES), f32),
    ]
    if nz == 4 and nc == 2 and tb > 2:
        block = pltpu.VMEM((tb, rows, LANES), f32)
        body = functools.partial(two_stage, (nz, nc, ntm, CUT))
        scratch = (
            inputs[:-2]
            + [pltpu.VMEM((tb, nc * LANES, taps), jnp.bfloat16), inputs[-1]]
            + [pltpu.VMEM((modes, panels), jnp.bfloat16), block, block, block]
            + [
                pltpu.VMEM((tb * CUT, panels // CUT, LANES), f32),
                pltpu.VMEM((tb * CUT, panels // CUT, LANES), f32),
                pltpu.VMEM((tb * CUT, 2 * nc, md // CUT, LANES), f32),
                pltpu.VMEM((tb, CUT, nc, md // CUT, LANES), f32),
                pltpu.VMEM((tb, nc, md, LANES), f32),
                pltpu.VMEM((tb, nc, md, LANES), f32),
                pltpu.VMEM((tb, md, LANES), f32),
                pltpu.VMEM((nb, md, LANES), f32),
            ]
            + response[:3]
            + [pltpu.VMEM((nb, 2, md, LANES), f32)]
            + response[3:]
            + [
                pltpu.VMEM((owners, fd, th), f32),
                pltpu.VMEM((owners - 1, fd, th), f32),
                pltpu.VMEM((owners, fd, time_dev), f32),
                pltpu.VMEM((owners - 1, fd, time_dev), f32),
                pltpu.VMEM((max(ntm - 1, 1), owners, fd, time_dev), f32),
                pltpu.VMEM((max(ntm - 1, 1), owners, fd, time_dev), f32),
                dma((8,)), dma((tb + 1,)), dma((tb,)), dma((tb * CUT,)), dma((tb,)),
                dma(()), dma((tb,)), dma(()), dma((ntm,)), dma((ntm,)), dma(()),
                dma((ntm,)), dma((ntm,)),
                pltpu.SemaphoreType.REGULAR,
            ]
        )
    else:
        chunk = pltpu.VMEM((nch, rows // splits, LANES), f32)
        body = functools.partial(kernel, (nz, nc, ntm, splits))
        scratch = (
            inputs
            + [chunk] * 7
            + [pltpu.VMEM((tb, xrows, LANES), f32), pltpu.VMEM((nb, xrows, LANES), f32)]
            + response
            + [
                pltpu.VMEM((owners, fd, time_dev), f32),
                pltpu.VMEM((owners, fd, time_dev), f32),
                dma((8,)),
                dma((2 * (th // min(256, th)),)),
                dma((nch,)), dma((nch,)), dma((nch,)), dma((nch,)), dma((nch,)), dma((nch,)),
                dma((tb,)), dma((tb,)),
                dma((ntm,)), dma((ntm,)),
                dma((owners,)), dma((owners,)),
            ]
        )
    out = pl.pallas_call(
        body,
        out_shape=(
            pltpu.VMEM((md, time_dev), f32),
            pltpu.VMEM((fd, time_dev), f32),
            pltpu.VMEM((fd, time_dev), f32),
        ),
        in_specs=[pl.BlockSpec(memory_space=pltpu.HBM)] * 9,
        out_specs=(vmem,) * 3,
        scratch_shapes=scratch,
        compiler_params=pltpu.CompilerParams(
            collective_id=0, has_side_effects=True, vmem_limit_bytes=VMEM_LIMIT
        ),
    )(
        *(
            pltpu.with_memory_space_constraint(a, pltpu.HBM)
            for a in (
                pressures,
                tap_area.reshape(taps // LANES, LANES),
                tap_panel.reshape(1, taps),
                tap_floor.reshape(1, taps),
                panel_shape,
                floor_shape,
                mode_order.reshape(1, modes),
                mode_decay.reshape(1, modes),
                mode_freq.reshape(1, modes),
            )
        )
    )
    return pl.pallas_call(
        write_out,
        out_shape=tuple(jax.ShapeDtypeStruct(o.shape, o.dtype) for o in out),
        in_specs=[vmem] * 3,
        out_specs=(pl.BlockSpec(memory_space=pltpu.HBM),) * 3,
        scratch_shapes=[dma((3,))],
        compiler_params=pltpu.CompilerParams(vmem_limit_bytes=VMEM_LIMIT),
    )(*out)


def solution(mesh):
    own = P(("taps", "floors"))
    out_spec = P(("taps", "floors"), ("dirs", "tm"))
    return jax.shard_map(
        on_device,
        mesh=mesh,
        in_specs=(P(("dirs", "tm"), ("taps", "floors")), own, own, own, P(), P(), P(), P(), P()),
        out_specs=(out_spec, out_spec, out_spec),
        check_vma=False,
    )
```

```python
import functools

import jax
import jax.numpy as jnp
from jax import lax
from jax.experimental import pallas as pl
from jax.experimental.pallas import tpu as pltpu
from jax.sharding import PartitionSpec as P

MESH = pl.DeviceIdType.MESH
LANES = 128
LAG = 2
CUT = 4
VMEM_LIMIT = 32 * 1024 * 1024
NT = (((1,), (1,)), ((), ()))


def dot_nt(a, b):
    return lax.dot_general(a, b, NT, preferred_element_type=jnp.float32)


def dot_split(a, b):
    hi = b.astype(jnp.bfloat16)
    lo = (b - hi.astype(jnp.float32)).astype(jnp.bfloat16)
    return jnp.dot(a, hi, preferred_element_type=jnp.float32) + jnp.dot(
        a, lo, preferred_element_type=jnp.float32
    )


def hi_lo(b):
    hi = b.astype(jnp.bfloat16)
    return hi, (b - hi.astype(jnp.float32)).astype(jnp.bfloat16)


def dot_stacked(a, b):
    return jnp.dot(
        jnp.concatenate([a, a], axis=1),
        jnp.concatenate(hi_lo(b), axis=0),
        preferred_element_type=jnp.float32,
    )


def kernel(
    cfg,
    p_hbm, area_h, panel_h, floor_h, shape_h, fshape_h, order_h, decay_h, freq_h,
    y_ref, fm_ref, fl_ref,
    area_ref, panel_ref, floor_ref, shape_ref, fshape_ref, order_ref, decay_ref, freq_ref, order_col,
    pv, w_ref, mine, send_p, recv_p, rin, lin, rout, lout, xs, fb, tabs, loc, loc_im, st_send, st_recv,
    fs, fr,
    in_sem, p_sem, pp_s, pp_r, r_s, r_r, l_s, l_r, x_s, x_r, t_s, t_r, f_s, f_r,
):
    nz, nc, ntm, splits = cfg
    owners = nz * nc
    z = lax.axis_index("taps")
    c = lax.axis_index("floors")
    x = lax.axis_index("tm")
    me = z * nc + c
    other = nc - 1 - c
    time_dev, taps = pv.shape
    panels, modes = shape_ref.shape
    floors = fshape_ref.shape[0]
    rows = panels + floors
    th = time_dev // nc
    tblocks = th // LANES
    crows = rows // splits
    nch = tblocks * splits
    md = modes // owners
    fd = floors // owners
    f32 = jnp.float32
    bf16 = jnp.bfloat16

    small = [
        pltpu.make_async_copy(src, dst, in_sem.at[i])
        for i, (src, dst) in enumerate(
            (
                (area_h, area_ref), (panel_h, panel_ref), (floor_h, floor_ref), (shape_h, shape_ref),
                (fshape_h, fshape_ref), (order_h, order_ref), (decay_h, decay_ref), (freq_h, freq_ref),
            )
        )
    ]
    for cp in small:
        cp.start()

    barrier = pltpu.get_barrier_semaphore()

    def greet(k, carry):
        j = lax.rem(me + k, owners)
        pl.semaphore_signal(
            barrier, inc=1, device_id={"taps": j // nc, "floors": lax.rem(j, nc)}, device_id_type=MESH
        )
        return carry

    lax.fori_loop(1, owners, greet, 0)
    for k in range(1, ntm):
        pl.semaphore_signal(
            barrier, inc=1, device_id={"tm": lax.rem(x + k, ntm)}, device_id_type=MESH
        )

    step_t = min(256, th)
    per_half = th // step_t
    loads = []
    for h in range(2):
        half = other if h == 0 else c
        for b in range(per_half):
            off = pl.multiple_of(half * th + b * step_t, step_t)
            cp = pltpu.make_async_copy(
                p_hbm.at[pl.ds(off, step_t)], pv.at[pl.ds(off, step_t)], p_sem.at[h * per_half + b]
            )
            cp.start()
            loads.append((cp, off))

    for cp in small[:3]:
        cp.wait()
    ids = lax.broadcasted_iota(jnp.int32, (panels, LANES), 0)
    fids = lax.broadcasted_iota(jnp.int32, (floors, LANES), 0)
    area = area_ref[...].astype(f32)
    for r in range(taps // LANES):
        cols = slice(r * LANES, (r + 1) * LANES)
        row = area[r : r + 1, :]
        w_ref[0:panels, cols] = jnp.where(panel_ref[:, cols] == ids, row, 0.0).astype(bf16)
        w_ref[panels:rows, cols] = jnp.where(floor_ref[:, cols] == fids, row, 0.0).astype(bf16)

    def sums(b, h, dst):
        cp, off = loads[h * per_half + b]
        cp.wait()
        q = dot_nt(w_ref[...], pv[pl.ds(off, step_t), :])
        for i in range(step_t // LANES):
            for s in range(splits):
                dst[(b * step_t // LANES + i) * splits + s] = q[
                    s * crows : (s + 1) * crows, i * LANES : (i + 1) * LANES
                ]

    def pair_copy(k):
        return pltpu.make_async_remote_copy(
            src_ref=send_p.at[k], dst_ref=recv_p.at[k], send_sem=pp_s.at[k], recv_sem=pp_r.at[k],
            device_id={"floors": other}, device_id_type=MESH,
        )

    per_step = step_t // LANES * splits

    @pl.when(z == 0)
    def _():
        rin[...] = jnp.zeros_like(rin)

    @pl.when(z == nz - 1)
    def _():
        lin[...] = jnp.zeros_like(lin)

    def line_copy(k, right):
        src, dst, ss, rs = (rout, rin, r_s, r_r) if right else (lout, lin, l_s, l_r)
        to = jnp.minimum(z + 1, nz - 1) if right else jnp.maximum(z - 1, 0)
        return pltpu.make_async_remote_copy(
            src_ref=src.at[k], dst_ref=dst.at[k], send_sem=ss.at[k], recv_sem=rs.at[k],
            device_id={"taps": to}, device_id_type=MESH,
        )

    def line_step(s, carry):
        for right in (True, False):
            hop = z if right else nz - 1 - z
            k = s - LAG * hop
            came, out = (rin, rout) if right else (lin, lout)

            @pl.when(jnp.logical_and(k >= 0, k < nch))
            def _():
                @pl.when(hop > 0)
                def _():
                    line_copy(k, right).wait_recv()

                @pl.when(hop < nz - 1)
                def _():
                    out[k] = mine[k] + came[k]
                    line_copy(k, right).start()

        return carry

    def merge(b):
        for k in range(b * per_step, (b + 1) * per_step):
            pair_copy(k).wait_recv()
            mine[k] = mine[k] + recv_p[k]

    for b in range(per_half):
        sums(b, 0, send_p)
        if b == 0:
            pl.semaphore_wait(barrier, owners - 1 + ntm - 1)
        for k in range(b * per_step, (b + 1) * per_step):
            pair_copy(k).start()
        if b > 0:
            merge(b - 1)
        if b == 1:
            lax.fori_loop(0, min(LAG, per_step), line_step, 0)
        sums(b, 1, mine)
    merge(per_half - 1)
    first = min(LAG, per_step) if per_half > 1 else 0
    early = min(LAG, nch)
    lax.fori_loop(first, early, line_step, 0)

    for cp in small[3:]:
        cp.wait()
    order_col[...] = jnp.transpose(jnp.broadcast_to(order_ref[...].astype(f32), (LANES, modes)))
    mode_ids = lax.broadcasted_iota(jnp.int32, (md, modes), 1).astype(f32)

    def pick(owner):
        return order_col[pl.ds(pl.multiple_of(owner * md, md), md), 0:1] == mode_ids

    def shapes(hot):
        return dot_nt(hot.astype(f32).astype(bf16), shape_ref[...]).astype(bf16)

    hot_me = pick(me)
    hot_other = pick(z * nc + other)
    g_both = jnp.concatenate([shapes(hot_other), shapes(hot_me)], axis=0)
    d = jnp.sum(jnp.where(hot_me, decay_ref[...], 0.0), axis=1, keepdims=True)
    w = jnp.sum(jnp.where(hot_me, freq_ref[...], 0.0), axis=1, keepdims=True)
    ls = dot_nt(fshape_ref[...], hot_me.astype(f32).astype(bf16)).astype(bf16)
    e2 = 2.0 * d
    poly = jnp.full_like(e2, 1.0 / 40320.0)
    for coef in (1.0 / 5040, 1.0 / 720, 1.0 / 120, 1.0 / 24, 1.0 / 6, 0.5, 1.0):
        poly = coef - e2 * poly
    gain = jnp.sqrt(e2 * poly)
    lane = lax.broadcasted_iota(jnp.int32, (md, LANES), 1)
    ahead = (lane + 1).astype(f32)
    mag = jnp.exp(-d * ahead)
    t_re = mag * jnp.cos(w * ahead)
    t_im = mag * jnp.sin(w * ahead)
    tabs[0] = t_re
    tabs[1] = t_im
    hops = []
    step = 1
    while step < LANES:
        i = 2 + 2 * len(hops)
        tabs[i] = jnp.where(lane >= step, t_re[:, step - 1 : step], 0.0)
        tabs[i + 1] = jnp.where(lane >= step, t_im[:, step - 1 : step], 0.0)
        hops.append(step)
        step *= 2

    floor_row = lax.broadcasted_iota(jnp.int32, (floors, LANES), 0)

    def load_row(q, row):
        return jnp.sum(jnp.where(floor_row == row, q, 0.0), axis=0, keepdims=True)

    def exchange(tb):
        return pltpu.make_async_remote_copy(
            src_ref=xs.at[tb], dst_ref=fb.at[c * tblocks + tb],
            send_sem=x_s.at[tb], recv_sem=x_r.at[tb],
            device_id={"floors": other}, device_id_type=MESH,
        )

    def forces(tb):
        q = jnp.concatenate(
            [mine[k] + rin[k] + lin[k] for k in range(tb * splits, (tb + 1) * splits)], axis=0
        )
        both = dot_split(g_both, q[:panels])
        blk = c * tblocks + tb
        pad = [jnp.zeros((xs.shape[1] - md - fd, LANES), f32)] if xs.shape[1] > md + fd else []
        theirs = [load_row(q[panels:], (z * nc + other) * fd + r) for r in range(fd)]
        ours = [load_row(q[panels:], me * fd + r) for r in range(fd)]
        xs[tb] = jnp.concatenate([both[:md]] + theirs + pad, axis=0)
        exchange(tb).start()
        fb[blk] = jnp.concatenate([both[md:]] + ours + pad, axis=0)

    def at_rest(blk):
        re = gain * fb[blk, 0:md, :]
        im = None
        for i, step in enumerate(hops):
            a, b = tabs[2 + 2 * i], tabs[3 + 2 * i]
            rr = pltpu.roll(re, step, 1)
            if im is None:
                re, im = re + a * rr, b * rr
            else:
                ri = pltpu.roll(im, step, 1)
                re, im = re + a * rr - b * ri, im + a * ri + b * rr
        loc[blk] = re
        loc_im[blk] = im

    done = early
    for tb in range(tblocks):
        upto = (tb + 1) * splits + LAG * (nz - 1)
        lax.fori_loop(done, upto, line_step, 0)
        done = upto
        forces(tb)
        at_rest(c * tblocks + tb)
        if tb > 0:
            exchange(tb - 1).wait_recv()
            at_rest(other * tblocks + tb - 1)
    exchange(tblocks - 1).wait_recv()
    at_rest(other * tblocks + tblocks - 1)
    nb = time_dev // LANES
    end_re = [loc[blk][:, LANES - 1 :] for blk in range(nb)]
    end_im = [loc_im[blk][:, LANES - 1 :] for blk in range(nb)]

    zb_re, zb_im = t_re[:, LANES - 1 :], t_im[:, LANES - 1 :]
    s_re, s_im = end_re[0], end_im[0]
    for blk in range(1, nb):
        s_re, s_im = (
            zb_re * s_re - zb_im * s_im + end_re[blk],
            zb_im * s_re + zb_re * s_im + end_im[blk],
        )

    def state_copy(to, src):
        return pltpu.make_async_remote_copy(
            src_ref=st_send, dst_ref=st_recv.at[src], send_sem=t_s.at[to], recv_sem=t_r.at[src],
            device_id={"tm": to}, device_id_type=MESH,
        )

    st_send[...] = jnp.where(lane == 0, s_re, s_im)
    in_re = jnp.zeros((md, 1), f32)
    in_im = jnp.zeros((md, 1), f32)
    if ntm > 1:
        for to in range(1, ntm):

            @pl.when(x < to)
            def _():
                state_copy(to, jnp.minimum(x, ntm - 2)).start()

        for src in range(ntm - 1):

            @pl.when(x > src)
            def _():
                state_copy(lax.rem(x + 1, ntm), src).wait_recv()

            @pl.when(x <= src)
            def _():
                st_recv[src] = jnp.zeros_like(st_send)

            got_re, got_im = st_recv[src][:, 0:1], st_recv[src][:, 1:2]
            if ntm == 2:
                in_re, in_im = got_re, got_im
                continue
            length = (jnp.maximum(x - 1 - src, 0) * time_dev).astype(f32)
            pm = jnp.exp(-d * length)
            pr, pi = pm * jnp.cos(w * length), pm * jnp.sin(w * length)
            in_re = in_re + pr * got_re - pi * got_im
            in_im = in_im + pi * got_re + pr * got_im

    t_re, t_im = tabs[0], tabs[1]
    for blk in range(nb):
        y = loc[blk] + t_re * in_re - t_im * in_im
        cols = slice(blk * LANES, (blk + 1) * LANES)
        y_ref[:, cols] = y
        in_re, in_im = (
            zb_re * in_re - zb_im * in_im + end_re[blk],
            zb_im * in_re + zb_re * in_im + end_im[blk],
        )
    part = dot_split(ls, y_ref[...])
    for j in range(owners):
        fs[j] = part[j * fd : (j + 1) * fd]

    def motion_copy(k):
        j = lax.rem(me + k, owners)
        return pltpu.make_async_remote_copy(
            src_ref=fs.at[j], dst_ref=fr.at[me], send_sem=f_s.at[k], recv_sem=f_r.at[k],
            device_id={"taps": j // nc, "floors": lax.rem(j, nc)}, device_id_type=MESH,
        )

    def motion_start(k, carry):
        motion_copy(k).start()
        return carry

    def motion_recv(k, total):
        motion_copy(k).wait_recv()
        return total + fr[lax.rem(me + owners - k, owners)]

    def motion_sent(k, carry):
        motion_copy(k).wait_send()
        return carry

    lax.fori_loop(1, owners, motion_start, 0)
    load_scale = (floors / (taps * owners)) ** 0.5
    for blk in range(nb):
        fl_ref[:, blk * LANES : (blk + 1) * LANES] = fb[blk, md : md + fd, :] * load_scale

    for k in range(nch):
        pair_copy(k).wait_send()

    def line_sent(k, carry):
        @pl.when(z < nz - 1)
        def _():
            line_copy(k, True).wait_send()

        @pl.when(z > 0)
        def _():
            line_copy(k, False).wait_send()

        return carry

    lax.fori_loop(0, nch, line_sent, 0)
    for tb in range(tblocks):
        exchange(tb).wait_send()
    for to in range(1, ntm):

        @pl.when(x < to)
        def _():
            state_copy(to, jnp.minimum(x, ntm - 2)).wait_send()

    fm_ref[...] = lax.fori_loop(1, owners, motion_recv, fs[me])
    lax.fori_loop(1, owners, motion_sent, 0)


def two_stage(
    cfg,
    p_hbm, area_h, panel_h, floor_h, shape_h, fshape_h, order_h, decay_h, freq_h,
    y_ref, fm_ref, fl_ref,
    area_ref, panel_ref, floor_ref, shape_ref, fshape_ref, order_ref, decay_ref, freq_ref, order_col,
    pv, w_ref, g_ref, send_p, recv_p, mine, mp, up, sx, fx, si, fi, sp, fb, tabs, loc, loc_im, ends, st_send, st_recv,
    fls, flr, fs, fr, cs, cr,
    in_sem, p_sem, pp_r, u_r, x_r, i_r, e_r, fl_r, t_s, t_r, f_r, c_s, c_r, known,
):
    nz, nc, ntm, cut = cfg
    pp_s, u_s, i_s, x_s, e_s, fl_s, f_s = (in_sem.at[i] for i in range(7))
    owners = nz * nc
    z = lax.axis_index("taps")
    c = lax.axis_index("floors")
    x = lax.axis_index("tm")
    me = z * nc + c
    other = nc - 1 - c
    side = z // 2
    mate = z + 1 - 2 * lax.rem(z, 2)
    far = nz - 1 - z
    inner = jnp.logical_or(z == 1, z == 2)
    time_dev = y_ref.shape[1]
    taps = w_ref.shape[1]
    panels, modes = shape_ref.shape
    floors = fshape_ref.shape[0]
    rows = panels + floors
    th = time_dev // nc
    tblocks = th // LANES
    md = modes // owners
    fd = floors // owners
    f32 = jnp.float32
    bf16 = jnp.bfloat16

    small = [
        pltpu.make_async_copy(src, dst, in_sem.at[i])
        for i, (src, dst) in enumerate(
            (
                (area_h, area_ref), (panel_h, panel_ref), (floor_h, floor_ref), (shape_h, shape_ref),
                (fshape_h, fshape_ref), (order_h, order_ref), (decay_h, decay_ref), (freq_h, freq_ref),
            )
        )
    ]
    for cp in small[:3]:
        cp.start()
    for k in range(tblocks):
        for h, half in enumerate((other, c)):
            off = pl.multiple_of(half * th + k * LANES, LANES)
            pltpu.make_async_copy(
                p_hbm.at[pl.ds(off, LANES)],
                pv.at[k, pl.ds(h * LANES, LANES)],
                p_sem.at[k + 1 if k + h else 0],
            ).start()
    for cp in small[3:]:
        cp.start()

    barrier = pltpu.get_barrier_semaphore()

    def greet(**to):
        pl.semaphore_signal(barrier, inc=1, device_id=to, device_id_type=MESH)

    greet(floors=other)
    greet(taps=mate)
    for k in range(1, ntm):
        greet(tm=lax.rem(x + k, ntm))

    @pl.when(inner)
    def _():
        greet(taps=far)

    for cp in small[:3]:
        cp.wait()
    ids = lax.broadcasted_iota(jnp.int32, (panels, LANES), 0)
    fids = lax.broadcasted_iota(jnp.int32, (floors, LANES), 0)
    area = area_ref[...].astype(f32)
    def sums(k):
        loaded(pv.at[k], k + 1)
        q = dot_nt(w_ref[...], pv[k])
        send_p[k] = q[:, :LANES]
        mine[k] = q[:, LANES:]

    def loaded(ref, i):
        pltpu.make_async_copy(ref, ref, p_sem.at[i]).wait()

    def pair_copy(k):
        return pltpu.make_async_remote_copy(
            src_ref=send_p.at[k], dst_ref=recv_p.at[k], send_sem=pp_s, recv_sem=pp_r.at[k],
            device_id={"floors": other}, device_id_type=MESH,
        )

    def up_copy(i):
        return pltpu.make_async_remote_copy(
            src_ref=mp.at[i], dst_ref=up.at[i], send_sem=u_s, recv_sem=u_r.at[i],
            device_id={"taps": mate}, device_id_type=MESH,
        )

    width = LANES // cut

    def moved(v, groups):
        shift = groups * width % LANES
        return pltpu.roll(v, shift, 1) if shift else v

    def packed(parts, j):
        group = lax.broadcasted_iota(jnp.int32, parts[0].shape, 1) // width
        out = moved(parts[0], -j)
        for g in range(1, cut):
            out = jnp.where(group == g, moved(parts[g], g - j), out)
        return out

    def split(v):
        n = v.shape[0] // cut
        return [v[g * n : (g + 1) * n] for g in range(cut)]

    def merge(k):
        pair_copy(k).wait_recv()
        total = mine[k] + recv_p[k]
        mine[k] = total
        for j in range(cut):
            mp[k * cut + j] = packed(split(total[:panels]), j)

            @pl.when(jnp.logical_not(inner))
            def _():
                up_copy(k * cut + j).start()

    def pick(off, n):
        mode_ids = lax.broadcasted_iota(jnp.int32, (n, modes), 1).astype(f32)
        return order_col[pl.ds(pl.multiple_of(off, n), n), 0:1] == mode_ids

    def prepare():
        for cp in small[3:]:
            cp.wait()
        order_col[...] = jnp.transpose(jnp.broadcast_to(order_ref[...].astype(f32), (LANES, modes)))

        n = modes // 2
        for r in range(2):
            hot = pick(r * n, n).astype(f32).astype(bf16)
            g_ref[r * n : (r + 1) * n] = dot_nt(hot, shape_ref[...]).astype(bf16)

    def project(chip, n, q):
        size = n * nc * md
        return dot_split(g_ref[pl.ds(pl.multiple_of(chip * nc * md, size), size), :], q)

    def mate_copy(k, i):
        return pltpu.make_async_remote_copy(
            src_ref=si.at[k, i], dst_ref=fi.at[k, c], send_sem=i_s, recv_sem=i_r,
            device_id={"taps": mate, "floors": i}, device_id_type=MESH,
        )

    def cross_copy(k, i):
        chip = lax.rem(i // nc + 1 - side, 2)
        return pltpu.make_async_remote_copy(
            src_ref=sx.at[k, chip * nc + i % nc], dst_ref=fx.at[k // cut, k % cut, c],
            send_sem=x_s, recv_sem=x_r.at[k // cut],
            device_id={"taps": 2 * (1 - side) + chip, "floors": i % nc}, device_id_type=MESH,
        )

    def exchange(k):
        return pltpu.make_async_remote_copy(
            src_ref=sp.at[k], dst_ref=fb.at[c * tblocks + k], send_sem=e_s, recv_sem=e_r.at[k],
            device_id={"floors": other}, device_id_type=MESH,
        )

    def keep(k, both):
        both = both.reshape(nc, md, LANES)
        sp[k] = jnp.where(c == 0, both[1], both[0])
        exchange(k).start()
        fb[c * tblocks + k] = jnp.where(c == 0, both[0], both[1])

    def across(k):
        got = []
        for j in range(cut):
            n = k * cut + j
            up_copy(n).wait_recv()
            total = mp[n] + up[n]
            got.append(total)
            total = jnp.concatenate([moved(total, j - g) for g in range(cut)], axis=0)
            f = project(2 * (1 - side), 2, total).reshape(2 * nc, cut, md // cut, LANES)
            f = packed([f[:, g].reshape(2 * nc * md // cut, LANES) for g in range(cut)], j)
            sx[n] = f.reshape(2 * nc, md // cut, LANES)
            for i in range(2 * nc):
                cross_copy(n, i).start()
        keep(k, project(z, 1, jnp.concatenate([packed(got, g) for g in range(cut)], axis=0)))

    head = pl.ds(0, LANES)
    loaded(pv.at[0, head], 0)
    chunk = 4 * LANES
    first = jnp.zeros((rows, LANES), f32)
    for start in range(0, taps, chunk):
        for r in range(start // LANES, (start + chunk) // LANES):
            cols = slice(r * LANES, (r + 1) * LANES)
            row = area[r : r + 1, :]
            w_ref[0:panels, cols] = jnp.where(panel_ref[:, cols] == ids, row, 0.0).astype(bf16)
            w_ref[panels:rows, cols] = jnp.where(floor_ref[:, cols] == fids, row, 0.0).astype(bf16)
        cols = slice(start, start + chunk)
        first = first + dot_nt(w_ref[:, cols], pv[0, head, cols])
    send_p[0] = first

    @pl.when(inner)
    def _():
        pl.semaphore_wait(barrier, 3 + ntm - 1)

    @pl.when(jnp.logical_not(inner))
    def _():
        pl.semaphore_wait(barrier, 2 + ntm - 1)

    pair_copy(0).start()
    rest = pl.ds(LANES, LANES)
    loaded(pv.at[0, rest], 1)
    mine[0] = dot_nt(w_ref[...], pv[0, rest])
    merge(0)

    @pl.when(inner)
    def _():
        pl.semaphore_signal(known, inc=1, device_id={"taps": far}, device_id_type=MESH)

    prepare()

    def aside(k):
        si[k] = project(mate, 1, mine[k, 0:panels]).reshape(nc, md, LANES)
        for j in range(nc):
            mate_copy(k, j).start()

    for k in range(1, tblocks):
        sums(k)
        pair_copy(k).start()
        if k == 1:

            @pl.when(inner)
            def _():
                aside(0)

    @pl.when(inner)
    def _():
        for k in range(1, tblocks):
            if k == tblocks - 1:
                pl.semaphore_wait(known, 1)
                pl.semaphore_signal(known, inc=1, device_id={"taps": mate}, device_id_type=MESH)
                across(0)
            merge(k)
            aside(k)
        across(1)

    @pl.when(jnp.logical_not(inner))
    def _():
        for k in range(1, tblocks):
            merge(k)

    @pl.when(jnp.logical_not(inner))
    def _():
        for k in range(tblocks):
            keep(k, project(z, 1, mine[k, 0:panels]))

    for k in range(tblocks):
        part = mine[k, panels:rows]
        for j in range(owners):
            fls[j, :, k * LANES : (k + 1) * LANES] = part[j * fd : (j + 1) * fd]

    hot_me = pick(me * md, md)
    d = jnp.sum(jnp.where(hot_me, decay_ref[...], 0.0), axis=1, keepdims=True)
    w = jnp.sum(jnp.where(hot_me, freq_ref[...], 0.0), axis=1, keepdims=True)
    ls = dot_nt(fshape_ref[...], hot_me.astype(f32).astype(bf16)).astype(bf16)
    e2 = 2.0 * d
    poly = jnp.full_like(e2, 1.0 / 40320.0)
    for coef in (1.0 / 5040, 1.0 / 720, 1.0 / 120, 1.0 / 24, 1.0 / 6, 0.5, 1.0):
        poly = coef - e2 * poly
    gain = jnp.sqrt(e2 * poly)
    nb = time_dev // LANES
    lane = lax.broadcasted_iota(jnp.int32, (md, LANES), 1)
    steps = lane.astype(f32)
    cos, sin = jnp.cos(w * steps), jnp.sin(w * steps)
    grow = gain * jnp.exp(d * steps)
    decay = jnp.exp(-d * steps)
    t_re, t_im = decay * cos, decay * sin
    for i, table in enumerate((t_re, t_im, grow * cos, -grow * sin)):
        tabs[i] = table
    upto = lax.broadcasted_iota(jnp.int32, (LANES, 2 * LANES), 0) <= lax.broadcasted_iota(
        jnp.int32, (LANES, 2 * LANES), 1
    )
    upto = upto.astype(f32).astype(bf16)

    def times(a_re, a_im, b_re, b_im):
        return a_re * b_re - a_im * b_im, a_re * b_im + a_im * b_re

    def wide(v):
        return jnp.broadcast_to(v, (md, LANES))

    last = LANES - 1
    for i, table in enumerate(
        times(t_re[:, 1:2], t_im[:, 1:2], t_re[:, last:], t_im[:, last:])
    ):
        tabs[4 + i] = wide(table)

    def turn(re, im):
        return times(tabs[4], tabs[5], re, im)

    @pl.when(inner)
    def _():
        for k in range(2, tblocks):
            across(k)

    @pl.when(jnp.logical_not(inner))
    def _():
        pl.semaphore_wait(known, 1)

    def load_copy(k):
        j = lax.rem(me + k, owners)
        return pltpu.make_async_remote_copy(
            src_ref=fls.at[j], dst_ref=flr.at[k - 1], send_sem=fl_s, recv_sem=fl_r,
            device_id={"taps": j // nc, "floors": lax.rem(j, nc)}, device_id_type=MESH,
        )

    def prefix(blks):
        parts = [fb[blk] * tabs[2 + i] for blk in blks for i in range(2)]
        v = jnp.concatenate(parts, axis=0)
        v = jnp.dot(
            jnp.concatenate(hi_lo(v), axis=1),
            jnp.concatenate([upto, upto], axis=0),
            preferred_element_type=f32,
        )
        for n, blk in enumerate(blks):
            for i, dst in enumerate((loc, loc_im)):
                part = v[(2 * n + i) * md : (2 * n + i + 1) * md]
                dst[blk] = part[:, :LANES]
                ends[blk, i] = part[:, LANES:]

    def response(blk, re, im):
        return tabs[0] * (loc[blk] + re) - tabs[1] * (loc_im[blk] + im)

    def respond(start, stop, re, im):
        ys = []
        for blk in range(start, stop):
            ys.append(response(blk, re, im))
            re, im = turn(ends[blk, 0] + re, ends[blk, 1] + im)
        y = jnp.concatenate(ys, axis=1)
        cols = slice(start * LANES, stop * LANES)
        part = dot_stacked(ls, y)
        for j in range(owners):
            fs[j, :, cols] = part[j * fd : (j + 1) * fd]
        y_ref[:, cols] = y
        return re, im

    def state_copy(to, src):
        return pltpu.make_async_remote_copy(
            src_ref=st_send, dst_ref=st_recv.at[src], send_sem=t_s.at[to - 1], recv_sem=t_r.at[src],
            device_id={"tm": to}, device_id_type=MESH,
        )

    def carry_copy(to, src, j):
        return pltpu.make_async_remote_copy(
            src_ref=cs.at[to - 1, j], dst_ref=cr.at[src, me], send_sem=c_s.at[to - 1], recv_sem=c_r.at[src],
            device_id={"tm": to, "taps": j // nc, "floors": j % nc}, device_id_type=MESH,
        )

    @pl.when(jnp.logical_not(inner))
    def _():
        pltpu.make_async_copy(fi, fi, i_r).wait()

    for k in range(tblocks):
        exchange(k).wait_recv()

        @pl.when(jnp.logical_not(inner))
        def _():
            for h in range(nc):
                fb[h * tblocks + k] = fb[h * tblocks + k] + fi[k, h]

        pltpu.make_async_copy(fx.at[k], fx.at[k], x_r.at[k]).wait()
        for h in range(nc):
            parts = [fx[k, j, h] for j in range(cut)]
            come = jnp.concatenate([packed(parts, g) for g in range(cut)], axis=0)
            fb[h * tblocks + k] = fb[h * tblocks + k] + come
        prefix([h * tblocks + k for h in range(nc)])
        if k == tblocks - 2:
            for i in range(1, owners):
                load_copy(i).start()
            re, im = respond(0, k + 1, jnp.zeros((md, LANES), f32), jnp.zeros((md, LANES), f32))

    re, im = respond(tblocks - 1, nb, re, im)

    def motion_copy(k):
        j = lax.rem(me + k, owners)
        return pltpu.make_async_remote_copy(
            src_ref=fs.at[j], dst_ref=fr.at[k - 1], send_sem=f_s, recv_sem=f_r,
            device_id={"taps": j // nc, "floors": lax.rem(j, nc)}, device_id_type=MESH,
        )

    for k in range(1, owners):
        motion_copy(k).start()
    s_re, s_im = re, im
    for to in range(1, ntm):

        @pl.when(x < to)
        def _():
            src = jnp.minimum(x, ntm - 2)
            re, im = s_re, s_im
            if ntm > 2:
                gap = ((to - 1 - x) * time_dev).astype(f32)
                pm = jnp.exp(-d * gap)
                re, im = times(pm * jnp.cos(w * gap), pm * jnp.sin(w * gap), re, im)
            ys = []
            for blk in range(nb):
                ys.append(tabs[0] * re - tabs[1] * im)
                re, im = turn(re, im)
            part = dot_stacked(ls, jnp.concatenate(ys, axis=1))
            for j in range(owners):
                cs[to - 1, j] = part[j * fd : (j + 1) * fd]
            for j in range(owners):
                carry_copy(to, src, j).start()
            st_send[...] = jnp.where(lane == 0, s_re, s_im)
            state_copy(to, src).start()

    in_re = jnp.zeros((md, LANES), f32)
    in_im = jnp.zeros((md, LANES), f32)
    for src in range(ntm - 1):

        @pl.when(x > src)
        def _():
            state_copy(lax.rem(x + 1, ntm), src).wait_recv()

        @pl.when(x <= src)
        def _():
            st_recv[src] = jnp.zeros_like(st_send)

        got_re, got_im = wide(st_recv[src][:, 0:1]), wide(st_recv[src][:, 1:2])
        if ntm == 2:
            in_re, in_im = got_re, got_im
            continue
        length = (jnp.maximum(x - 1 - src, 0) * time_dev).astype(f32)
        pm = jnp.exp(-d * length)
        got_re, got_im = times(pm * jnp.cos(w * length), pm * jnp.sin(w * length), got_re, got_im)
        in_re, in_im = in_re + got_re, in_im + got_im

    @pl.when(x > 0)
    def _():
        re, im = in_re, in_im
        for blk in range(nb):
            cols = slice(blk * LANES, (blk + 1) * LANES)
            y_ref[:, cols] = y_ref[:, cols] + tabs[0] * re - tabs[1] * im
            re, im = turn(re, im)

    def drain(ref, sem):
        pltpu.make_async_copy(ref, ref, sem).wait()

    drain(flr, fl_r)
    load_scale = (floors / (taps * owners)) ** 0.5
    halves = []
    for h in range(nc):
        total = jnp.where(c == h, fls[me], 0.0)
        for k in range(1, owners):
            src = lax.rem(me + owners - k, owners)
            total = total + jnp.where(lax.rem(src, nc) == h, flr[k - 1], 0.0)
        halves.append(total * load_scale)
    for h in range(nc):
        fl_ref[:, h * th : (h + 1) * th] = halves[h]

    drain(send_p, pp_s)

    @pl.when(inner)
    def _():
        drain(si, i_s)
        drain(sx, x_s)

    @pl.when(jnp.logical_not(inner))
    def _():
        drain(up, u_s)

    drain(sp, e_s)
    drain(flr, fl_s)
    for to in range(1, ntm):

        @pl.when(x < to)
        def _():
            state_copy(to, jnp.minimum(x, ntm - 2)).wait_send()

    drain(fr, f_r)
    total = fs[me]
    for k in range(1, owners):
        total = total + fr[k - 1]
    fm_ref[...] = total
    drain(fr, f_s)
    for src in range(ntm - 1):

        @pl.when(x > src)
        def _():
            drain(cr.at[src], c_r.at[src])
            carried = fm_ref[...]
            for j in range(owners):
                carried = carried + cr[src, j]
            fm_ref[...] = carried

    for to in range(1, ntm):

        @pl.when(x < to)
        def _():
            drain(cs.at[to - 1], c_s.at[to - 1])


def write_out(y, fm, fl, y_out, fm_out, fl_out, sem):
    copies = [
        pltpu.make_async_copy(src, dst, sem.at[i])
        for i, (src, dst) in enumerate(((y, y_out), (fm, fm_out), (fl, fl_out)))
    ]
    for cp in copies:
        cp.start()
    for cp in copies:
        cp.wait()


def on_device(
    pressures, tap_area, tap_panel, tap_floor, panel_shape, floor_shape, mode_order, mode_decay, mode_freq
):
    nz, nc, ntm = lax.axis_size("taps"), lax.axis_size("floors"), lax.axis_size("tm")
    owners = nz * nc
    time_dev, taps = pressures.shape
    panels, modes = panel_shape.shape
    floors = floor_shape.shape[0]
    rows = panels + floors
    splits = 2
    th = time_dev // nc
    md, fd = modes // owners, floors // owners
    nch = th // LANES * splits
    xrows = md + -(-fd // 8) * 8
    vmem = pl.BlockSpec(memory_space=pltpu.VMEM)
    dma = pltpu.SemaphoreType.DMA
    f32 = jnp.float32
    tb, nb = th // LANES, time_dev // LANES
    inputs = [
        pltpu.VMEM((taps // LANES, LANES), jnp.bfloat16),
        pltpu.VMEM((1, taps), jnp.int32),
        pltpu.VMEM((1, taps), jnp.int32),
        pltpu.VMEM(panel_shape.shape, jnp.bfloat16),
        pltpu.VMEM(floor_shape.shape, jnp.bfloat16),
        pltpu.VMEM((1, modes), jnp.int32),
        pltpu.VMEM((1, modes), f32),
        pltpu.VMEM((1, modes), f32),
        pltpu.VMEM((modes, LANES), f32),
        pltpu.VMEM((time_dev, taps), jnp.bfloat16),
        pltpu.VMEM((rows, taps), jnp.bfloat16),
    ]
    response = [
        pltpu.VMEM((16, md, LANES), f32),
        pltpu.VMEM((nb, md, LANES), f32),
        pltpu.VMEM((nb, md, LANES), f32),
        pltpu.VMEM((md, LANES), f32),
        pltpu.VMEM((max(ntm - 1, 1), md, LANES), f32),
    ]
    if nz == 4 and nc == 2 and tb > 2:
        block = pltpu.VMEM((tb, rows, LANES), f32)
        later = dma((max(ntm - 1, 1),))
        body = functools.partial(two_stage, (nz, nc, ntm, CUT))
        scratch = (
            inputs[:-2]
            + [pltpu.VMEM((tb, nc * LANES, taps), jnp.bfloat16), inputs[-1]]
            + [pltpu.VMEM((modes, panels), jnp.bfloat16), block, block, block]
            + [
                pltpu.VMEM((tb * CUT, panels // CUT, LANES), f32),
                pltpu.VMEM((tb * CUT, panels // CUT, LANES), f32),
                pltpu.VMEM((tb * CUT, 2 * nc, md // CUT, LANES), f32),
                pltpu.VMEM((tb, CUT, nc, md // CUT, LANES), f32),
                pltpu.VMEM((tb, nc, md, LANES), f32),
                pltpu.VMEM((tb, nc, md, LANES), f32),
                pltpu.VMEM((tb, md, LANES), f32),
                pltpu.VMEM((nb, md, LANES), f32),
            ]
            + response[:3]
            + [pltpu.VMEM((nb, 2, md, LANES), f32)]
            + response[3:]
            + [
                pltpu.VMEM((owners, fd, th), f32),
                pltpu.VMEM((owners - 1, fd, th), f32),
                pltpu.VMEM((owners, fd, time_dev), f32),
                pltpu.VMEM((owners - 1, fd, time_dev), f32),
                pltpu.VMEM((max(ntm - 1, 1), owners, fd, time_dev), f32),
                pltpu.VMEM((max(ntm - 1, 1), owners, fd, time_dev), f32),
                dma((8,)), dma((tb + 1,)), dma((tb,)), dma((tb * CUT,)), dma((tb,)),
                dma(()), dma((tb,)), dma(()), later, later, dma(()), later, later,
                pltpu.SemaphoreType.REGULAR,
            ]
        )
    else:
        chunk = pltpu.VMEM((nch, rows // splits, LANES), f32)
        body = functools.partial(kernel, (nz, nc, ntm, splits))
        scratch = (
            inputs
            + [chunk] * 7
            + [pltpu.VMEM((tb, xrows, LANES), f32), pltpu.VMEM((nb, xrows, LANES), f32)]
            + response
            + [
                pltpu.VMEM((owners, fd, time_dev), f32),
                pltpu.VMEM((owners, fd, time_dev), f32),
                dma((8,)),
                dma((2 * (th // min(256, th)),)),
                dma((nch,)), dma((nch,)), dma((nch,)), dma((nch,)), dma((nch,)), dma((nch,)),
                dma((tb,)), dma((tb,)),
                dma((ntm,)), dma((ntm,)),
                dma((owners,)), dma((owners,)),
            ]
        )
    out = pl.pallas_call(
        body,
        out_shape=(
            pltpu.VMEM((md, time_dev), f32),
            pltpu.VMEM((fd, time_dev), f32),
            pltpu.VMEM((fd, time_dev), f32),
        ),
        in_specs=[pl.BlockSpec(memory_space=pltpu.HBM)] * 9,
        out_specs=(vmem,) * 3,
        scratch_shapes=scratch,
        compiler_params=pltpu.CompilerParams(
            collective_id=0, has_side_effects=True, vmem_limit_bytes=VMEM_LIMIT
        ),
    )(
        *(
            pltpu.with_memory_space_constraint(a, pltpu.HBM)
            for a in (
                pressures,
                tap_area.reshape(taps // LANES, LANES),
                tap_panel.reshape(1, taps),
                tap_floor.reshape(1, taps),
                panel_shape,
                floor_shape,
                mode_order.reshape(1, modes),
                mode_decay.reshape(1, modes),
                mode_freq.reshape(1, modes),
            )
        )
    )
    return pl.pallas_call(
        write_out,
        out_shape=tuple(jax.ShapeDtypeStruct(o.shape, o.dtype) for o in out),
        in_specs=[vmem] * 3,
        out_specs=(pl.BlockSpec(memory_space=pltpu.HBM),) * 3,
        scratch_shapes=[dma((3,))],
        compiler_params=pltpu.CompilerParams(vmem_limit_bytes=VMEM_LIMIT),
    )(*out)


def solution(mesh):
    own = P(("taps", "floors"))
    out_spec = P(("taps", "floors"), ("dirs", "tm"))
    return jax.shard_map(
        on_device,
        mesh=mesh,
        in_specs=(P(("dirs", "tm"), ("taps", "floors")), own, own, own, P(), P(), P(), P(), P()),
        out_specs=(out_spec, out_spec, out_spec),
        check_vma=False,
    )
```

```python
import functools

import jax
import jax.numpy as jnp
from jax import lax
from jax.experimental import pallas as pl
from jax.experimental.pallas import tpu as pltpu
from jax.sharding import PartitionSpec as P

MESH = pl.DeviceIdType.MESH
LANES = 128
LAG = 2
CUT = 4
VMEM_LIMIT = 32 * 1024 * 1024
NT = (((1,), (1,)), ((), ()))


def dot_nt(a, b):
    return lax.dot_general(a, b, NT, preferred_element_type=jnp.float32)


def dot_split(a, b):
    hi = b.astype(jnp.bfloat16)
    lo = (b - hi.astype(jnp.float32)).astype(jnp.bfloat16)
    return jnp.dot(a, hi, preferred_element_type=jnp.float32) + jnp.dot(
        a, lo, preferred_element_type=jnp.float32
    )


def hi_lo(b):
    hi = b.astype(jnp.bfloat16)
    return hi, (b - hi.astype(jnp.float32)).astype(jnp.bfloat16)


def dot_stacked(a, b):
    return jnp.dot(
        jnp.concatenate([a, a], axis=1),
        jnp.concatenate(hi_lo(b), axis=0),
        preferred_element_type=jnp.float32,
    )


def kernel(
    cfg,
    p_hbm, area_h, panel_h, floor_h, shape_h, fshape_h, order_h, decay_h, freq_h,
    y_ref, fm_ref, fl_ref,
    area_ref, panel_ref, floor_ref, shape_ref, fshape_ref, order_ref, decay_ref, freq_ref, order_col,
    pv, w_ref, mine, send_p, recv_p, rin, lin, rout, lout, xs, fb, tabs, loc, loc_im, st_send, st_recv,
    fs, fr,
    in_sem, p_sem, pp_s, pp_r, r_s, r_r, l_s, l_r, x_s, x_r, t_s, t_r, f_s, f_r,
):
    nz, nc, ntm, splits = cfg
    owners = nz * nc
    z = lax.axis_index("taps")
    c = lax.axis_index("floors")
    x = lax.axis_index("tm")
    me = z * nc + c
    other = nc - 1 - c
    time_dev, taps = pv.shape
    panels, modes = shape_ref.shape
    floors = fshape_ref.shape[0]
    rows = panels + floors
    th = time_dev // nc
    tblocks = th // LANES
    crows = rows // splits
    nch = tblocks * splits
    md = modes // owners
    fd = floors // owners
    f32 = jnp.float32
    bf16 = jnp.bfloat16

    small = [
        pltpu.make_async_copy(src, dst, in_sem.at[i])
        for i, (src, dst) in enumerate(
            (
                (area_h, area_ref), (panel_h, panel_ref), (floor_h, floor_ref), (shape_h, shape_ref),
                (fshape_h, fshape_ref), (order_h, order_ref), (decay_h, decay_ref), (freq_h, freq_ref),
            )
        )
    ]
    for cp in small:
        cp.start()

    barrier = pltpu.get_barrier_semaphore()

    def greet(k, carry):
        j = lax.rem(me + k, owners)
        pl.semaphore_signal(
            barrier, inc=1, device_id={"taps": j // nc, "floors": lax.rem(j, nc)}, device_id_type=MESH
        )
        return carry

    lax.fori_loop(1, owners, greet, 0)
    for k in range(1, ntm):
        pl.semaphore_signal(
            barrier, inc=1, device_id={"tm": lax.rem(x + k, ntm)}, device_id_type=MESH
        )

    step_t = min(256, th)
    per_half = th // step_t
    loads = []
    for h in range(2):
        half = other if h == 0 else c
        for b in range(per_half):
            off = pl.multiple_of(half * th + b * step_t, step_t)
            cp = pltpu.make_async_copy(
                p_hbm.at[pl.ds(off, step_t)], pv.at[pl.ds(off, step_t)], p_sem.at[h * per_half + b]
            )
            cp.start()
            loads.append((cp, off))

    for cp in small[:3]:
        cp.wait()
    ids = lax.broadcasted_iota(jnp.int32, (panels, LANES), 0)
    fids = lax.broadcasted_iota(jnp.int32, (floors, LANES), 0)
    area = area_ref[...].astype(f32)
    for r in range(taps // LANES):
        cols = slice(r * LANES, (r + 1) * LANES)
        row = area[r : r + 1, :]
        w_ref[0:panels, cols] = jnp.where(panel_ref[:, cols] == ids, row, 0.0).astype(bf16)
        w_ref[panels:rows, cols] = jnp.where(floor_ref[:, cols] == fids, row, 0.0).astype(bf16)

    def sums(b, h, dst):
        cp, off = loads[h * per_half + b]
        cp.wait()
        q = dot_nt(w_ref[...], pv[pl.ds(off, step_t), :])
        for i in range(step_t // LANES):
            for s in range(splits):
                dst[(b * step_t // LANES + i) * splits + s] = q[
                    s * crows : (s + 1) * crows, i * LANES : (i + 1) * LANES
                ]

    def pair_copy(k):
        return pltpu.make_async_remote_copy(
            src_ref=send_p.at[k], dst_ref=recv_p.at[k], send_sem=pp_s.at[k], recv_sem=pp_r.at[k],
            device_id={"floors": other}, device_id_type=MESH,
        )

    per_step = step_t // LANES * splits

    @pl.when(z == 0)
    def _():
        rin[...] = jnp.zeros_like(rin)

    @pl.when(z == nz - 1)
    def _():
        lin[...] = jnp.zeros_like(lin)

    def line_copy(k, right):
        src, dst, ss, rs = (rout, rin, r_s, r_r) if right else (lout, lin, l_s, l_r)
        to = jnp.minimum(z + 1, nz - 1) if right else jnp.maximum(z - 1, 0)
        return pltpu.make_async_remote_copy(
            src_ref=src.at[k], dst_ref=dst.at[k], send_sem=ss.at[k], recv_sem=rs.at[k],
            device_id={"taps": to}, device_id_type=MESH,
        )

    def line_step(s, carry):
        for right in (True, False):
            hop = z if right else nz - 1 - z
            k = s - LAG * hop
            came, out = (rin, rout) if right else (lin, lout)

            @pl.when(jnp.logical_and(k >= 0, k < nch))
            def _():
                @pl.when(hop > 0)
                def _():
                    line_copy(k, right).wait_recv()

                @pl.when(hop < nz - 1)
                def _():
                    out[k] = mine[k] + came[k]
                    line_copy(k, right).start()

        return carry

    def merge(b):
        for k in range(b * per_step, (b + 1) * per_step):
            pair_copy(k).wait_recv()
            mine[k] = mine[k] + recv_p[k]

    for b in range(per_half):
        sums(b, 0, send_p)
        if b == 0:
            pl.semaphore_wait(barrier, owners - 1 + ntm - 1)
        for k in range(b * per_step, (b + 1) * per_step):
            pair_copy(k).start()
        if b > 0:
            merge(b - 1)
        if b == 1:
            lax.fori_loop(0, min(LAG, per_step), line_step, 0)
        sums(b, 1, mine)
    merge(per_half - 1)
    first = min(LAG, per_step) if per_half > 1 else 0
    early = min(LAG, nch)
    lax.fori_loop(first, early, line_step, 0)

    for cp in small[3:]:
        cp.wait()
    order_col[...] = jnp.transpose(jnp.broadcast_to(order_ref[...].astype(f32), (LANES, modes)))
    mode_ids = lax.broadcasted_iota(jnp.int32, (md, modes), 1).astype(f32)

    def pick(owner):
        return order_col[pl.ds(pl.multiple_of(owner * md, md), md), 0:1] == mode_ids

    def shapes(hot):
        return dot_nt(hot.astype(f32).astype(bf16), shape_ref[...]).astype(bf16)

    hot_me = pick(me)
    hot_other = pick(z * nc + other)
    g_both = jnp.concatenate([shapes(hot_other), shapes(hot_me)], axis=0)
    d = jnp.sum(jnp.where(hot_me, decay_ref[...], 0.0), axis=1, keepdims=True)
    w = jnp.sum(jnp.where(hot_me, freq_ref[...], 0.0), axis=1, keepdims=True)
    ls = dot_nt(fshape_ref[...], hot_me.astype(f32).astype(bf16)).astype(bf16)
    e2 = 2.0 * d
    poly = jnp.full_like(e2, 1.0 / 40320.0)
    for coef in (1.0 / 5040, 1.0 / 720, 1.0 / 120, 1.0 / 24, 1.0 / 6, 0.5, 1.0):
        poly = coef - e2 * poly
    gain = jnp.sqrt(e2 * poly)
    lane = lax.broadcasted_iota(jnp.int32, (md, LANES), 1)
    ahead = (lane + 1).astype(f32)
    mag = jnp.exp(-d * ahead)
    t_re = mag * jnp.cos(w * ahead)
    t_im = mag * jnp.sin(w * ahead)
    tabs[0] = t_re
    tabs[1] = t_im
    hops = []
    step = 1
    while step < LANES:
        i = 2 + 2 * len(hops)
        tabs[i] = jnp.where(lane >= step, t_re[:, step - 1 : step], 0.0)
        tabs[i + 1] = jnp.where(lane >= step, t_im[:, step - 1 : step], 0.0)
        hops.append(step)
        step *= 2

    floor_row = lax.broadcasted_iota(jnp.int32, (floors, LANES), 0)

    def load_row(q, row):
        return jnp.sum(jnp.where(floor_row == row, q, 0.0), axis=0, keepdims=True)

    def exchange(tb):
        return pltpu.make_async_remote_copy(
            src_ref=xs.at[tb], dst_ref=fb.at[c * tblocks + tb],
            send_sem=x_s.at[tb], recv_sem=x_r.at[tb],
            device_id={"floors": other}, device_id_type=MESH,
        )

    def forces(tb):
        q = jnp.concatenate(
            [mine[k] + rin[k] + lin[k] for k in range(tb * splits, (tb + 1) * splits)], axis=0
        )
        both = dot_split(g_both, q[:panels])
        blk = c * tblocks + tb
        pad = [jnp.zeros((xs.shape[1] - md - fd, LANES), f32)] if xs.shape[1] > md + fd else []
        theirs = [load_row(q[panels:], (z * nc + other) * fd + r) for r in range(fd)]
        ours = [load_row(q[panels:], me * fd + r) for r in range(fd)]
        xs[tb] = jnp.concatenate([both[:md]] + theirs + pad, axis=0)
        exchange(tb).start()
        fb[blk] = jnp.concatenate([both[md:]] + ours + pad, axis=0)

    def at_rest(blk):
        re = gain * fb[blk, 0:md, :]
        im = None
        for i, step in enumerate(hops):
            a, b = tabs[2 + 2 * i], tabs[3 + 2 * i]
            rr = pltpu.roll(re, step, 1)
            if im is None:
                re, im = re + a * rr, b * rr
            else:
                ri = pltpu.roll(im, step, 1)
                re, im = re + a * rr - b * ri, im + a * ri + b * rr
        loc[blk] = re
        loc_im[blk] = im

    done = early
    for tb in range(tblocks):
        upto = (tb + 1) * splits + LAG * (nz - 1)
        lax.fori_loop(done, upto, line_step, 0)
        done = upto
        forces(tb)
        at_rest(c * tblocks + tb)
        if tb > 0:
            exchange(tb - 1).wait_recv()
            at_rest(other * tblocks + tb - 1)
    exchange(tblocks - 1).wait_recv()
    at_rest(other * tblocks + tblocks - 1)
    nb = time_dev // LANES
    end_re = [loc[blk][:, LANES - 1 :] for blk in range(nb)]
    end_im = [loc_im[blk][:, LANES - 1 :] for blk in range(nb)]

    zb_re, zb_im = t_re[:, LANES - 1 :], t_im[:, LANES - 1 :]
    s_re, s_im = end_re[0], end_im[0]
    for blk in range(1, nb):
        s_re, s_im = (
            zb_re * s_re - zb_im * s_im + end_re[blk],
            zb_im * s_re + zb_re * s_im + end_im[blk],
        )

    def state_copy(to, src):
        return pltpu.make_async_remote_copy(
            src_ref=st_send, dst_ref=st_recv.at[src], send_sem=t_s.at[to], recv_sem=t_r.at[src],
            device_id={"tm": to}, device_id_type=MESH,
        )

    st_send[...] = jnp.where(lane == 0, s_re, s_im)
    in_re = jnp.zeros((md, 1), f32)
    in_im = jnp.zeros((md, 1), f32)
    if ntm > 1:
        for to in range(1, ntm):

            @pl.when(x < to)
            def _():
                state_copy(to, jnp.minimum(x, ntm - 2)).start()

        for src in range(ntm - 1):

            @pl.when(x > src)
            def _():
                state_copy(lax.rem(x + 1, ntm), src).wait_recv()

            @pl.when(x <= src)
            def _():
                st_recv[src] = jnp.zeros_like(st_send)

            got_re, got_im = st_recv[src][:, 0:1], st_recv[src][:, 1:2]
            if ntm == 2:
                in_re, in_im = got_re, got_im
                continue
            length = (jnp.maximum(x - 1 - src, 0) * time_dev).astype(f32)
            pm = jnp.exp(-d * length)
            pr, pi = pm * jnp.cos(w * length), pm * jnp.sin(w * length)
            in_re = in_re + pr * got_re - pi * got_im
            in_im = in_im + pi * got_re + pr * got_im

    t_re, t_im = tabs[0], tabs[1]
    for blk in range(nb):
        y = loc[blk] + t_re * in_re - t_im * in_im
        cols = slice(blk * LANES, (blk + 1) * LANES)
        y_ref[:, cols] = y
        in_re, in_im = (
            zb_re * in_re - zb_im * in_im + end_re[blk],
            zb_im * in_re + zb_re * in_im + end_im[blk],
        )
    part = dot_split(ls, y_ref[...])
    for j in range(owners):
        fs[j] = part[j * fd : (j + 1) * fd]

    def motion_copy(k):
        j = lax.rem(me + k, owners)
        return pltpu.make_async_remote_copy(
            src_ref=fs.at[j], dst_ref=fr.at[me], send_sem=f_s.at[k], recv_sem=f_r.at[k],
            device_id={"taps": j // nc, "floors": lax.rem(j, nc)}, device_id_type=MESH,
        )

    def motion_start(k, carry):
        motion_copy(k).start()
        return carry

    def motion_recv(k, total):
        motion_copy(k).wait_recv()
        return total + fr[lax.rem(me + owners - k, owners)]

    def motion_sent(k, carry):
        motion_copy(k).wait_send()
        return carry

    lax.fori_loop(1, owners, motion_start, 0)
    load_scale = (floors / (taps * owners)) ** 0.5
    for blk in range(nb):
        fl_ref[:, blk * LANES : (blk + 1) * LANES] = fb[blk, md : md + fd, :] * load_scale

    for k in range(nch):
        pair_copy(k).wait_send()

    def line_sent(k, carry):
        @pl.when(z < nz - 1)
        def _():
            line_copy(k, True).wait_send()

        @pl.when(z > 0)
        def _():
            line_copy(k, False).wait_send()

        return carry

    lax.fori_loop(0, nch, line_sent, 0)
    for tb in range(tblocks):
        exchange(tb).wait_send()
    for to in range(1, ntm):

        @pl.when(x < to)
        def _():
            state_copy(to, jnp.minimum(x, ntm - 2)).wait_send()

    fm_ref[...] = lax.fori_loop(1, owners, motion_recv, fs[me])
    lax.fori_loop(1, owners, motion_sent, 0)


def two_stage(
    cfg,
    p_hbm, area_h, panel_h, floor_h, shape_h, fshape_h, order_h, decay_h, freq_h,
    y_ref, fm_ref, fl_ref,
    area_ref, panel_ref, floor_ref, shape_ref, fshape_ref, order_ref, decay_ref, freq_ref, order_col,
    pv, w_ref, g_ref, send_p, recv_p, mine, mp, up, sx, fx, si, fi, sp, fb, tabs, loc, loc_im, ends, st_send, st_recv,
    fls, flr, fs, fr, cs, cr,
    in_sem, p_sem, pp_r, u_r, x_r, i_r, e_r, fl_r, t_s, t_r, f_r, c_s, c_r, known,
):
    nz, nc, ntm, cut = cfg
    pp_s, u_s, i_s, x_s, e_s, fl_s, f_s = (in_sem.at[i] for i in range(7))
    owners = nz * nc
    z = lax.axis_index("taps")
    c = lax.axis_index("floors")
    x = lax.axis_index("tm")
    me = z * nc + c
    other = nc - 1 - c
    side = z // 2
    mate = z + 1 - 2 * lax.rem(z, 2)
    far = nz - 1 - z
    inner = jnp.logical_or(z == 1, z == 2)
    time_dev = y_ref.shape[1]
    taps = w_ref.shape[1]
    panels, modes = shape_ref.shape
    floors = fshape_ref.shape[0]
    rows = panels + floors
    th = time_dev // nc
    tblocks = th // LANES
    md = modes // owners
    fd = floors // owners
    f32 = jnp.float32
    bf16 = jnp.bfloat16

    small = [
        pltpu.make_async_copy(src, dst, in_sem.at[i])
        for i, (src, dst) in enumerate(
            (
                (area_h, area_ref), (panel_h, panel_ref), (floor_h, floor_ref), (shape_h, shape_ref),
                (fshape_h, fshape_ref), (order_h, order_ref), (decay_h, decay_ref), (freq_h, freq_ref),
            )
        )
    ]
    for cp in small[:3]:
        cp.start()
    for k in range(tblocks):
        for h, half in enumerate((other, c)):
            off = pl.multiple_of(half * th + k * LANES, LANES)
            pltpu.make_async_copy(
                p_hbm.at[pl.ds(off, LANES)],
                pv.at[k, pl.ds(h * LANES, LANES)],
                p_sem.at[k + 1 if k + h else 0],
            ).start()
    for cp in small[3:]:
        cp.start()

    barrier = pltpu.get_barrier_semaphore()

    def greet(**to):
        pl.semaphore_signal(barrier, inc=1, device_id=to, device_id_type=MESH)

    greet(floors=other)
    greet(taps=mate)
    for k in range(1, ntm):
        greet(tm=lax.rem(x + k, ntm))

    @pl.when(inner)
    def _():
        greet(taps=far)

    for cp in small[:3]:
        cp.wait()
    ids = lax.broadcasted_iota(jnp.int32, (panels, LANES), 0)
    fids = lax.broadcasted_iota(jnp.int32, (floors, LANES), 0)
    area = area_ref[...].astype(f32)
    def sums(k):
        loaded(pv.at[k], k + 1)
        q = dot_nt(w_ref[...], pv[k])
        send_p[k] = q[:, :LANES]
        mine[k] = q[:, LANES:]

    def loaded(ref, i):
        pltpu.make_async_copy(ref, ref, p_sem.at[i]).wait()

    def pair_copy(k):
        return pltpu.make_async_remote_copy(
            src_ref=send_p.at[k], dst_ref=recv_p.at[k], send_sem=pp_s, recv_sem=pp_r.at[k],
            device_id={"floors": other}, device_id_type=MESH,
        )

    def up_copy(i):
        return pltpu.make_async_remote_copy(
            src_ref=mp.at[i], dst_ref=up.at[i], send_sem=u_s, recv_sem=u_r.at[i],
            device_id={"taps": mate}, device_id_type=MESH,
        )

    width = LANES // cut

    def moved(v, groups):
        shift = groups * width % LANES
        return pltpu.roll(v, shift, 1) if shift else v

    def packed(parts, j):
        group = lax.broadcasted_iota(jnp.int32, parts[0].shape, 1) // width
        out = moved(parts[0], -j)
        for g in range(1, cut):
            out = jnp.where(group == g, moved(parts[g], g - j), out)
        return out

    def split(v):
        n = v.shape[0] // cut
        return [v[g * n : (g + 1) * n] for g in range(cut)]

    def merge(k):
        pair_copy(k).wait_recv()
        total = mine[k] + recv_p[k]
        mine[k] = total
        for j in range(cut):
            mp[k * cut + j] = packed(split(total[:panels]), j)

            @pl.when(jnp.logical_not(inner))
            def _():
                up_copy(k * cut + j).start()

    def pick(off, n):
        mode_ids = lax.broadcasted_iota(jnp.int32, (n, modes), 1).astype(f32)
        return order_col[pl.ds(pl.multiple_of(off, n), n), 0:1] == mode_ids

    def prepare():
        for cp in small[3:]:
            cp.wait()
        order_col[...] = jnp.transpose(jnp.broadcast_to(order_ref[...].astype(f32), (LANES, modes)))

        n = modes // 2
        for r in range(2):
            hot = pick(r * n, n).astype(f32).astype(bf16)
            g_ref[r * n : (r + 1) * n] = dot_nt(hot, shape_ref[...]).astype(bf16)

    def project(chip, n, q):
        size = n * nc * md
        return dot_split(g_ref[pl.ds(pl.multiple_of(chip * nc * md, size), size), :], q)

    def mate_copy(k, i):
        return pltpu.make_async_remote_copy(
            src_ref=si.at[k, i], dst_ref=fi.at[k, c], send_sem=i_s, recv_sem=i_r,
            device_id={"taps": mate, "floors": i}, device_id_type=MESH,
        )

    def cross_copy(k, i):
        chip = lax.rem(i // nc + 1 - side, 2)
        return pltpu.make_async_remote_copy(
            src_ref=sx.at[k, chip * nc + i % nc], dst_ref=fx.at[k // cut, k % cut, c],
            send_sem=x_s, recv_sem=x_r.at[k // cut],
            device_id={"taps": 2 * (1 - side) + chip, "floors": i % nc}, device_id_type=MESH,
        )

    def exchange(k):
        return pltpu.make_async_remote_copy(
            src_ref=sp.at[k], dst_ref=fb.at[c * tblocks + k], send_sem=e_s, recv_sem=e_r.at[k],
            device_id={"floors": other}, device_id_type=MESH,
        )

    def keep(k, both):
        both = both.reshape(nc, md, LANES)
        sp[k] = jnp.where(c == 0, both[1], both[0])
        exchange(k).start()
        fb[c * tblocks + k] = jnp.where(c == 0, both[0], both[1])

    def across(k):
        got = []
        for j in range(cut):
            n = k * cut + j
            up_copy(n).wait_recv()
            total = mp[n] + up[n]
            got.append(total)
            total = jnp.concatenate([moved(total, j - g) for g in range(cut)], axis=0)
            f = project(2 * (1 - side), 2, total).reshape(2 * nc, cut, md // cut, LANES)
            f = packed([f[:, g].reshape(2 * nc * md // cut, LANES) for g in range(cut)], j)
            sx[n] = f.reshape(2 * nc, md // cut, LANES)
            for i in range(2 * nc):
                cross_copy(n, i).start()
        keep(k, project(z, 1, jnp.concatenate([packed(got, g) for g in range(cut)], axis=0)))

    head = pl.ds(0, LANES)
    loaded(pv.at[0, head], 0)
    chunk = 4 * LANES
    first = jnp.zeros((rows, LANES), f32)
    for start in range(0, taps, chunk):
        for r in range(start // LANES, (start + chunk) // LANES):
            cols = slice(r * LANES, (r + 1) * LANES)
            row = area[r : r + 1, :]
            w_ref[0:panels, cols] = jnp.where(panel_ref[:, cols] == ids, row, 0.0).astype(bf16)
            w_ref[panels:rows, cols] = jnp.where(floor_ref[:, cols] == fids, row, 0.0).astype(bf16)
        cols = slice(start, start + chunk)
        first = first + dot_nt(w_ref[:, cols], pv[0, head, cols])
    send_p[0] = first

    @pl.when(inner)
    def _():
        pl.semaphore_wait(barrier, 3 + ntm - 1)

    @pl.when(jnp.logical_not(inner))
    def _():
        pl.semaphore_wait(barrier, 2 + ntm - 1)

    pair_copy(0).start()
    rest = pl.ds(LANES, LANES)
    loaded(pv.at[0, rest], 1)
    mine[0] = dot_nt(w_ref[...], pv[0, rest])
    merge(0)

    @pl.when(inner)
    def _():
        pl.semaphore_signal(known, inc=1, device_id={"taps": far}, device_id_type=MESH)

    prepare()

    def aside(k):
        si[k] = project(mate, 1, mine[k, 0:panels]).reshape(nc, md, LANES)
        for j in range(nc):
            mate_copy(k, j).start()

    for k in range(1, tblocks):
        sums(k)
        pair_copy(k).start()
        if k == 1:

            @pl.when(inner)
            def _():
                aside(0)

    @pl.when(inner)
    def _():
        for k in range(1, tblocks):
            if k == tblocks - 1:
                pl.semaphore_wait(known, 1)
                pl.semaphore_signal(known, inc=1, device_id={"taps": mate}, device_id_type=MESH)
                across(0)
            merge(k)
            aside(k)
        across(1)

    @pl.when(jnp.logical_not(inner))
    def _():
        for k in range(1, tblocks):
            merge(k)

    @pl.when(jnp.logical_not(inner))
    def _():
        for k in range(tblocks):
            keep(k, project(z, 1, mine[k, 0:panels]))

    for k in range(tblocks):
        part = mine[k, panels:rows]
        for j in range(owners):
            fls[j, :, k * LANES : (k + 1) * LANES] = part[j * fd : (j + 1) * fd]

    hot_me = pick(me * md, md)
    d = jnp.sum(jnp.where(hot_me, decay_ref[...], 0.0), axis=1, keepdims=True)
    w = jnp.sum(jnp.where(hot_me, freq_ref[...], 0.0), axis=1, keepdims=True)
    ls = dot_nt(fshape_ref[...], hot_me.astype(f32).astype(bf16)).astype(bf16)
    e2 = 2.0 * d
    poly = jnp.full_like(e2, 1.0 / 40320.0)
    for coef in (1.0 / 5040, 1.0 / 720, 1.0 / 120, 1.0 / 24, 1.0 / 6, 0.5, 1.0):
        poly = coef - e2 * poly
    gain = jnp.sqrt(e2 * poly)
    nb = time_dev // LANES
    lane = lax.broadcasted_iota(jnp.int32, (md, LANES), 1)
    steps = lane.astype(f32)
    cos, sin = jnp.cos(w * steps), jnp.sin(w * steps)
    grow = gain * jnp.exp(d * steps)
    decay = jnp.exp(-d * steps)
    t_re, t_im = decay * cos, decay * sin
    for i, table in enumerate((t_re, t_im, grow * cos, -grow * sin)):
        tabs[i] = table
    upto = lax.broadcasted_iota(jnp.int32, (LANES, 2 * LANES), 0) <= lax.broadcasted_iota(
        jnp.int32, (LANES, 2 * LANES), 1
    )
    upto = upto.astype(f32).astype(bf16)

    def times(a_re, a_im, b_re, b_im):
        return a_re * b_re - a_im * b_im, a_re * b_im + a_im * b_re

    def wide(v):
        return jnp.broadcast_to(v, (md, LANES))

    last = LANES - 1
    for i, table in enumerate(
        times(t_re[:, 1:2], t_im[:, 1:2], t_re[:, last:], t_im[:, last:])
    ):
        tabs[4 + i] = wide(table)

    def turn(re, im):
        return times(tabs[4], tabs[5], re, im)

    @pl.when(inner)
    def _():
        for k in range(2, tblocks):
            across(k)

    @pl.when(jnp.logical_not(inner))
    def _():
        pl.semaphore_wait(known, 1)

    def load_copy(k):
        j = lax.rem(me + k, owners)
        return pltpu.make_async_remote_copy(
            src_ref=fls.at[j], dst_ref=flr.at[k - 1], send_sem=fl_s, recv_sem=fl_r,
            device_id={"taps": j // nc, "floors": lax.rem(j, nc)}, device_id_type=MESH,
        )

    def prefix(blks):
        parts = [fb[blk] * tabs[2 + i] for blk in blks for i in range(2)]
        v = jnp.concatenate(parts, axis=0)
        v = jnp.dot(
            jnp.concatenate(hi_lo(v), axis=1),
            jnp.concatenate([upto, upto], axis=0),
            preferred_element_type=f32,
        )
        for n, blk in enumerate(blks):
            for i, dst in enumerate((loc, loc_im)):
                part = v[(2 * n + i) * md : (2 * n + i + 1) * md]
                dst[blk] = part[:, :LANES]
                ends[blk, i] = part[:, LANES:]

    def response(blk, re, im):
        return tabs[0] * (loc[blk] + re) - tabs[1] * (loc_im[blk] + im)

    def respond(start, stop, re, im):
        ys = []
        for blk in range(start, stop):
            ys.append(response(blk, re, im))
            re, im = turn(ends[blk, 0] + re, ends[blk, 1] + im)
        y = jnp.concatenate(ys, axis=1)
        cols = slice(start * LANES, stop * LANES)
        part = dot_stacked(ls, y)
        for j in range(owners):
            fs[j, :, cols] = part[j * fd : (j + 1) * fd]
        y_ref[:, cols] = y
        return re, im

    def state_copy(to, src):
        return pltpu.make_async_remote_copy(
            src_ref=st_send, dst_ref=st_recv.at[src], send_sem=t_s.at[to - 1], recv_sem=t_r.at[src],
            device_id={"tm": to}, device_id_type=MESH,
        )

    def carry_copy(to, src, j):
        return pltpu.make_async_remote_copy(
            src_ref=cs.at[to - 1, j], dst_ref=cr.at[src, me], send_sem=c_s.at[to - 1], recv_sem=c_r.at[src],
            device_id={"tm": to, "taps": j // nc, "floors": j % nc}, device_id_type=MESH,
        )

    @pl.when(jnp.logical_not(inner))
    def _():
        pltpu.make_async_copy(fi, fi, i_r).wait()

    def motion_copy(k, start, stop):
        j = lax.rem(me + k, owners)
        cols = pl.ds(start * LANES, (stop - start) * LANES)
        return pltpu.make_async_remote_copy(
            src_ref=fs.at[j, :, cols], dst_ref=fr.at[k - 1, :, cols], send_sem=f_s, recv_sem=f_r,
            device_id={"taps": j // nc, "floors": lax.rem(j, nc)}, device_id_type=MESH,
        )

    for k in range(tblocks):
        exchange(k).wait_recv()

        @pl.when(jnp.logical_not(inner))
        def _():
            for h in range(nc):
                fb[h * tblocks + k] = fb[h * tblocks + k] + fi[k, h]

        pltpu.make_async_copy(fx.at[k], fx.at[k], x_r.at[k]).wait()
        if k == tblocks - 1:
            for i in range(1, owners):
                motion_copy(i, 0, k).start()
        for h in range(nc):
            parts = [fx[k, j, h] for j in range(cut)]
            come = jnp.concatenate([packed(parts, g) for g in range(cut)], axis=0)
            fb[h * tblocks + k] = fb[h * tblocks + k] + come
        prefix([h * tblocks + k for h in range(nc)])
        if k == tblocks - 2:
            for i in range(1, owners):
                load_copy(i).start()
            re, im = respond(0, k + 1, jnp.zeros((md, LANES), f32), jnp.zeros((md, LANES), f32))

    re, im = respond(tblocks - 1, nb, re, im)

    for k in range(1, owners):
        motion_copy(k, tblocks - 1, nb).start()
    s_re, s_im = re, im
    for to in range(1, ntm):

        @pl.when(x < to)
        def _():
            src = jnp.minimum(x, ntm - 2)
            re, im = s_re, s_im
            if ntm > 2:
                gap = ((to - 1 - x) * time_dev).astype(f32)
                pm = jnp.exp(-d * gap)
                re, im = times(pm * jnp.cos(w * gap), pm * jnp.sin(w * gap), re, im)
            ys = []
            for blk in range(nb):
                ys.append(tabs[0] * re - tabs[1] * im)
                re, im = turn(re, im)
            part = dot_stacked(ls, jnp.concatenate(ys, axis=1))
            for j in range(owners):
                cs[to - 1, j] = part[j * fd : (j + 1) * fd]
            for j in range(owners):
                carry_copy(to, src, j).start()
            st_send[...] = jnp.where(lane == 0, s_re, s_im)
            state_copy(to, src).start()

    in_re = jnp.zeros((md, LANES), f32)
    in_im = jnp.zeros((md, LANES), f32)
    for src in range(ntm - 1):

        @pl.when(x > src)
        def _():
            state_copy(lax.rem(x + 1, ntm), src).wait_recv()

        @pl.when(x <= src)
        def _():
            st_recv[src] = jnp.zeros_like(st_send)

        got_re, got_im = wide(st_recv[src][:, 0:1]), wide(st_recv[src][:, 1:2])
        if ntm == 2:
            in_re, in_im = got_re, got_im
            continue
        length = (jnp.maximum(x - 1 - src, 0) * time_dev).astype(f32)
        pm = jnp.exp(-d * length)
        got_re, got_im = times(pm * jnp.cos(w * length), pm * jnp.sin(w * length), got_re, got_im)
        in_re, in_im = in_re + got_re, in_im + got_im

    @pl.when(x > 0)
    def _():
        re, im = in_re, in_im
        for blk in range(nb):
            cols = slice(blk * LANES, (blk + 1) * LANES)
            y_ref[:, cols] = y_ref[:, cols] + tabs[0] * re - tabs[1] * im
            re, im = turn(re, im)

    def drain(ref, sem):
        pltpu.make_async_copy(ref, ref, sem).wait()

    drain(flr, fl_r)
    load_scale = (floors / (taps * owners)) ** 0.5
    halves = []
    for h in range(nc):
        total = jnp.where(c == h, fls[me], 0.0)
        for k in range(1, owners):
            src = lax.rem(me + owners - k, owners)
            total = total + jnp.where(lax.rem(src, nc) == h, flr[k - 1], 0.0)
        halves.append(total * load_scale)
    for h in range(nc):
        fl_ref[:, h * th : (h + 1) * th] = halves[h]

    drain(send_p, pp_s)

    @pl.when(inner)
    def _():
        drain(si, i_s)
        drain(sx, x_s)

    @pl.when(jnp.logical_not(inner))
    def _():
        drain(up, u_s)

    drain(sp, e_s)
    drain(flr, fl_s)
    for to in range(1, ntm):

        @pl.when(x < to)
        def _():
            state_copy(to, jnp.minimum(x, ntm - 2)).wait_send()

    drain(fr, f_r)
    total = fs[me]
    for k in range(1, owners):
        total = total + fr[k - 1]
    fm_ref[...] = total
    drain(fr, f_s)
    for src in range(ntm - 1):

        @pl.when(x > src)
        def _():
            drain(cr.at[src], c_r.at[src])
            carried = fm_ref[...]
            for j in range(owners):
                carried = carried + cr[src, j]
            fm_ref[...] = carried

    for to in range(1, ntm):

        @pl.when(x < to)
        def _():
            drain(cs.at[to - 1], c_s.at[to - 1])


def write_out(y, fm, fl, y_out, fm_out, fl_out, sem):
    copies = [
        pltpu.make_async_copy(src, dst, sem.at[i])
        for i, (src, dst) in enumerate(((y, y_out), (fm, fm_out), (fl, fl_out)))
    ]
    for cp in copies:
        cp.start()
    for cp in copies:
        cp.wait()


def on_device(
    pressures, tap_area, tap_panel, tap_floor, panel_shape, floor_shape, mode_order, mode_decay, mode_freq
):
    nz, nc, ntm = lax.axis_size("taps"), lax.axis_size("floors"), lax.axis_size("tm")
    owners = nz * nc
    time_dev, taps = pressures.shape
    panels, modes = panel_shape.shape
    floors = floor_shape.shape[0]
    rows = panels + floors
    splits = 2
    th = time_dev // nc
    md, fd = modes // owners, floors // owners
    nch = th // LANES * splits
    xrows = md + -(-fd // 8) * 8
    vmem = pl.BlockSpec(memory_space=pltpu.VMEM)
    dma = pltpu.SemaphoreType.DMA
    f32 = jnp.float32
    tb, nb = th // LANES, time_dev // LANES
    inputs = [
        pltpu.VMEM((taps // LANES, LANES), jnp.bfloat16),
        pltpu.VMEM((1, taps), jnp.int32),
        pltpu.VMEM((1, taps), jnp.int32),
        pltpu.VMEM(panel_shape.shape, jnp.bfloat16),
        pltpu.VMEM(floor_shape.shape, jnp.bfloat16),
        pltpu.VMEM((1, modes), jnp.int32),
        pltpu.VMEM((1, modes), f32),
        pltpu.VMEM((1, modes), f32),
        pltpu.VMEM((modes, LANES), f32),
        pltpu.VMEM((time_dev, taps), jnp.bfloat16),
        pltpu.VMEM((rows, taps), jnp.bfloat16),
    ]
    response = [
        pltpu.VMEM((16, md, LANES), f32),
        pltpu.VMEM((nb, md, LANES), f32),
        pltpu.VMEM((nb, md, LANES), f32),
        pltpu.VMEM((md, LANES), f32),
        pltpu.VMEM((max(ntm - 1, 1), md, LANES), f32),
    ]
    if nz == 4 and nc == 2 and tb > 2:
        block = pltpu.VMEM((tb, rows, LANES), f32)
        later = dma((max(ntm - 1, 1),))
        body = functools.partial(two_stage, (nz, nc, ntm, CUT))
        scratch = (
            inputs[:-2]
            + [pltpu.VMEM((tb, nc * LANES, taps), jnp.bfloat16), inputs[-1]]
            + [pltpu.VMEM((modes, panels), jnp.bfloat16), block, block, block]
            + [
                pltpu.VMEM((tb * CUT, panels // CUT, LANES), f32),
                pltpu.VMEM((tb * CUT, panels // CUT, LANES), f32),
                pltpu.VMEM((tb * CUT, 2 * nc, md // CUT, LANES), f32),
                pltpu.VMEM((tb, CUT, nc, md // CUT, LANES), f32),
                pltpu.VMEM((tb, nc, md, LANES), f32),
                pltpu.VMEM((tb, nc, md, LANES), f32),
                pltpu.VMEM((tb, md, LANES), f32),
                pltpu.VMEM((nb, md, LANES), f32),
            ]
            + response[:3]
            + [pltpu.VMEM((nb, 2, md, LANES), f32)]
            + response[3:]
            + [
                pltpu.VMEM((owners, fd, th), f32),
                pltpu.VMEM((owners - 1, fd, th), f32),
                pltpu.VMEM((owners, fd, time_dev), f32),
                pltpu.VMEM((owners - 1, fd, time_dev), f32),
                pltpu.VMEM((max(ntm - 1, 1), owners, fd, time_dev), f32),
                pltpu.VMEM((max(ntm - 1, 1), owners, fd, time_dev), f32),
                dma((8,)), dma((tb + 1,)), dma((tb,)), dma((tb * CUT,)), dma((tb,)),
                dma(()), dma((tb,)), dma(()), later, later, dma(()), later, later,
                pltpu.SemaphoreType.REGULAR,
            ]
        )
    else:
        chunk = pltpu.VMEM((nch, rows // splits, LANES), f32)
        body = functools.partial(kernel, (nz, nc, ntm, splits))
        scratch = (
            inputs
            + [chunk] * 7
            + [pltpu.VMEM((tb, xrows, LANES), f32), pltpu.VMEM((nb, xrows, LANES), f32)]
            + response
            + [
                pltpu.VMEM((owners, fd, time_dev), f32),
                pltpu.VMEM((owners, fd, time_dev), f32),
                dma((8,)),
                dma((2 * (th // min(256, th)),)),
                dma((nch,)), dma((nch,)), dma((nch,)), dma((nch,)), dma((nch,)), dma((nch,)),
                dma((tb,)), dma((tb,)),
                dma((ntm,)), dma((ntm,)),
                dma((owners,)), dma((owners,)),
            ]
        )
    out = pl.pallas_call(
        body,
        out_shape=(
            pltpu.VMEM((md, time_dev), f32),
            pltpu.VMEM((fd, time_dev), f32),
            pltpu.VMEM((fd, time_dev), f32),
        ),
        in_specs=[pl.BlockSpec(memory_space=pltpu.HBM)] * 9,
        out_specs=(vmem,) * 3,
        scratch_shapes=scratch,
        compiler_params=pltpu.CompilerParams(
            collective_id=0, has_side_effects=True, vmem_limit_bytes=VMEM_LIMIT
        ),
    )(
        *(
            pltpu.with_memory_space_constraint(a, pltpu.HBM)
            for a in (
                pressures,
                tap_area.reshape(taps // LANES, LANES),
                tap_panel.reshape(1, taps),
                tap_floor.reshape(1, taps),
                panel_shape,
                floor_shape,
                mode_order.reshape(1, modes),
                mode_decay.reshape(1, modes),
                mode_freq.reshape(1, modes),
            )
        )
    )
    return pl.pallas_call(
        write_out,
        out_shape=tuple(jax.ShapeDtypeStruct(o.shape, o.dtype) for o in out),
        in_specs=[vmem] * 3,
        out_specs=(pl.BlockSpec(memory_space=pltpu.HBM),) * 3,
        scratch_shapes=[dma((3,))],
        compiler_params=pltpu.CompilerParams(vmem_limit_bytes=VMEM_LIMIT),
    )(*out)


def solution(mesh):
    own = P(("taps", "floors"))
    out_spec = P(("taps", "floors"), ("dirs", "tm"))
    return jax.shard_map(
        on_device,
        mesh=mesh,
        in_specs=(P(("dirs", "tm"), ("taps", "floors")), own, own, own, P(), P(), P(), P(), P()),
        out_specs=(out_spec, out_spec, out_spec),
        check_vma=False,
    )
```
